32 devices in a mesh: dp: 4 (over x, core), ctx: 2 (over y), tensor: 4 (over z).
Axes of the slice: x: 2, y: 2, z: 4, core: 2. Of those that a mesh axis runs over, the one named last changes fastest.
Arguments:
- inputs: bfloat16 [2048, 2048], P(('dp', 'ctx'), 'tensor'), may hold values from -6 to 6
- cotangent: bfloat16 [2048, 2048], P(('dp', 'ctx')), may hold values from -6 to 6
- segments: int32 [4, 512], P('dp'), may hold values from 0 to 15, as said below
- positions: int32 [4, 512], P('dp', 'ctx'), may hold values from 0 to 511, as said below
- attention_gain: bfloat16 [2048], replicated, may hold values from 0.5 to 1.5
- query_weight: bfloat16 [2048, 2048], P(None, 'tensor'), may hold values from -0.125 to 0.125
- key_weight: bfloat16 [2048, 1024], P(None, 'tensor'), may hold values from -0.125 to 0.125
- value_weight: bfloat16 [2048, 1024], P(None, 'tensor'), may hold values from -0.125 to 0.125
- query_gain: bfloat16 [128], replicated, may hold values from 0.5 to 1.5
- key_gain: bfloat16 [128], replicated, may hold values from 0.5 to 1.5
- output_weight: bfloat16 [2048, 2048], P('tensor'), may hold values from -0.75 to 0.75
- feed_gain: bfloat16 [2048], replicated, may hold values from 0.3 to 5, as said below
- gate_weight: bfloat16 [2048, 6144], P(None, 'tensor'), may hold values from -0.125 to 0.125
- up_weight: bfloat16 [2048, 6144], P(None, 'tensor'), may hold values from -0.125 to 0.125
- down_weight: bfloat16 [6144, 2048], P('tensor'), may hold values from -0.078125 to 0.078125
Outputs:
- outputs: bfloat16 [2048, 2048], P(('dp', 'ctx'), 'tensor')
- grad_inputs: float32 [2048, 2048], P(('dp', 'ctx'), 'tensor')
- grad_attention_gain: float32 [2048], P('tensor')
- grad_query_weight: float32 [2048, 2048], P(None, 'tensor')
- grad_key_weight: float32 [2048, 1024], P(None, 'tensor')
- grad_value_weight: float32 [2048, 1024], P(None, 'tensor')
- grad_query_gain: float32 [128], replicated
- grad_key_gain: float32 [128], replicated
- grad_output_weight: float32 [2048, 2048], P('tensor')
- grad_feed_gain: float32 [2048], P('tensor')
- grad_gate_weight: float32 [2048, 6144], P(None, 'tensor')
- grad_up_weight: float32 [2048, 6144], P(None, 'tensor')
- grad_down_weight: float32 [6144, 2048], P('tensor')
The draws below stay inside these ranges and needn't reach their ends.
Inputs may be any that keep to these rules, and one draw needn't show every extreme that they name: `segments`: in each sequence the document numbers start at 0, never fall, and each document is one run of equal numbers; a sequence holds at most 16 documents. `positions`: a token's position counts from 0 at the first token of its document. `feed_gain`: positive gains.
All inputs are finite; a program needn't handle non-finite values.
Results may differ from the reference program's by a relative error of at most 0.024.
Values may be sent and summed in bfloat16 or wider, within the bound.
No kernel may reach another device: no remote copies, remote signals or barrier semaphores. Data moves between devices by JAX's collectives and lax.ppermute only.
A program may use at most 256 MiB of HBM per device.

```python
import jax
import jax.numpy as jnp
from jax import lax

D = 2048
HEADS = 16
KV_HEADS = 8
HD = 128
FF = 6144
SEQ_LEN = 512
SEQS = 4
TOKENS = 2048


def document_layout(key):
    count_key, order_key = jax.random.split(jax.random.fold_in(key, 11))
    documents = jax.random.randint(count_key, (SEQS, 1), 1, 17)
    row_number = jnp.arange(SEQS, dtype=jnp.int32)[:, None]
    documents = jnp.where(row_number == 0, 16, jnp.where(row_number == 1, 1, documents))
    orders = jax.vmap(lambda subkey: jax.random.permutation(subkey, SEQ_LEN - 1))(jax.random.split(order_key, SEQS))
    orders = jnp.concatenate([jnp.full((SEQS, 1), SEQ_LEN, jnp.int32), orders.astype(jnp.int32)], axis=1)
    index = jnp.arange(SEQ_LEN, dtype=jnp.int32)[None, :]
    starts = orders < documents - 1
    segment = jnp.cumsum(starts.astype(jnp.int32), axis=1).astype(jnp.int32)
    first = lax.cummax(jnp.where(starts, index, 0), axis=1)
    return (segment, (index - first).astype(jnp.int32))


def draw_segments(key, part):
    return document_layout(key)[0]


def draw_positions(key, part):
    return document_layout(key)[1]


def draw_feed_gain(key, part):
    ramp = jnp.arange(D, dtype=jnp.float32) / (D - 1)
    start_gain = 0.5
    end_gain = 4.0
    base = jnp.exp(jnp.log(start_gain) + ramp * jnp.log(end_gain / start_gain))
    jitter = jax.random.uniform(jax.random.fold_in(key, 23), (D,), jnp.float32, 0.85, 1.15)
    return (base * jitter).astype(jnp.bfloat16)


def levels(rng, shape, pieces, low, largest):
    def one(axis_at, blocks):
        steps = jax.random.uniform(jax.random.fold_in(jax.random.fold_in(rng, 6), axis_at), (blocks,), jnp.float32, low / len(pieces), largest / len(pieces))
        return jnp.repeat(jnp.exp(steps), shape[axis_at] // blocks).reshape((-1,) + (1,) * (len(shape) - axis_at - 1))

    factor_of = one(*pieces[0])
    for cut in pieces[1:]:
        factor_of = factor_of * one(*cut)
    return factor_of


def scatter_about(own_key, shape, spread, bound, shards=(), held_as=jnp.bfloat16):
    level = levels(own_key, shape, shards, -0.22, 0.18) if shards else 1.0
    values = jax.random.normal(own_key, shape, jnp.float32) * spread * level
    return jnp.minimum(jnp.maximum(values, -bound), bound).astype(held_as)


def setup_inputs(seed: int = 0) -> dict:
    seeds = jax.random.split(jax.random.key(seed), 16)
    inputs = scatter_about(seeds[0], (TOKENS, D), 1.0, 6.0, ((0, 8), (1, 4)))
    cotangent = scatter_about(seeds[1], (TOKENS, D), 1.0, 6.0, ((0, 8),))
    segments = draw_segments(jax.random.fold_in(seeds[15], 71), 0)
    positions = draw_positions(jax.random.fold_in(seeds[15], 71), 0)
    attention_gain = jnp.clip(1.0 + 0.1 * jax.random.normal(seeds[4], (D,), jnp.float32), 0.5, 1.5).astype(jnp.bfloat16)
    query_weight = scatter_about(seeds[5], (D, HEADS * HD), D ** -0.5, 0.125, ((1, 4),))
    key_weight = scatter_about(seeds[6], (D, KV_HEADS * HD), D ** -0.5, 0.125, ((1, 4),))
    value_weight = scatter_about(seeds[7], (D, KV_HEADS * HD), D ** -0.5, 0.125, ((1, 4),))
    query_gain = jnp.clip(1.0 + 0.1 * jax.random.normal(seeds[8], (HD,), jnp.float32), 0.5, 1.5).astype(jnp.bfloat16)
    key_gain = jnp.clip(1.0 + 0.1 * jax.random.normal(seeds[9], (HD,), jnp.float32), 0.5, 1.5).astype(jnp.bfloat16)
    output_weight = scatter_about(seeds[10], (HEADS * HD, D), (HEADS * HD // 32) ** -0.5, 0.75, ((0, 4),))
    feed_gain = draw_feed_gain(jax.random.fold_in(seeds[15], 71), 0)
    gate_weight = scatter_about(seeds[12], (D, FF), D ** -0.5, 0.125, ((1, 4),))
    up_weight = scatter_about(seeds[13], (D, FF), D ** -0.5, 0.125, ((1, 4),))
    down_weight = scatter_about(seeds[14], (FF, D), FF ** -0.5, 0.078125, ((0, 4),))
    return {"inputs": inputs, "cotangent": cotangent, "segments": segments, "positions": positions, "attention_gain": attention_gain, "query_weight": query_weight, "key_weight": key_weight, "value_weight": value_weight, "query_gain": query_gain, "key_gain": key_gain, "output_weight": output_weight, "feed_gain": feed_gain, "gate_weight": gate_weight, "up_weight": up_weight, "down_weight": down_weight}


EPS = 1e-06
THETA = 1000000.0
NEG = -1e+30

@jax.custom_vjp
def low(v):
    return lax.optimization_barrier(v.astype(jnp.bfloat16)).astype(jnp.float32)

@jax.custom_vjp
def low_back(v):
    return v

def low_keep(v):
    return (low(v), None)

def low_pass(kept, grad):
    return (grad,)

def back_keep(v):
    return (v, None)

def back_low(kept, grad):
    return (low(grad),)
low.defvjp(low_keep, low_pass)
low_back.defvjp(back_keep, back_low)

def rms_scale(value, gain):
    return value * lax.rsqrt(lax.optimization_barrier(jnp.mean(value * value, axis=-1, keepdims=True)) + EPS) * gain

def rope_tables(position_row):
    half = HD // 2
    freqs = jnp.exp(-(2.0 * jnp.arange(half, dtype=jnp.float32) / HD) * jnp.log(jnp.float32(THETA)))
    angles = position_row.astype(jnp.float32)[:, None] * freqs[None, :]
    return (jnp.cos(angles)[:, None, :], jnp.sin(angles)[:, None, :])

def rotate(value, cosine, sine):
    half = value.shape[-1] // 2
    first = value[..., :half]
    second = value[..., half:]
    return jnp.concatenate([first * cosine - second * sine, second * cosine + first * sine], axis=-1)

def matmul(left, right):
    return jnp.dot(left, right, precision=lax.Precision.HIGHEST)

def layer(inputs, segment_row, position_row, params):
    attention_gain, query_weight, key_weight, value_weight, query_gain, key_gain, output_weight, feed_gain, gate_weight, up_weight, down_weight = params
    length = inputs.shape[0]
    group = HEADS // KV_HEADS
    cosine, sine = rope_tables(position_row)
    normed = low(rms_scale(inputs, attention_gain))
    queries = low_back(matmul(normed, query_weight)).reshape(length, HEADS, HD)
    keys = low_back(matmul(normed, key_weight)).reshape(length, KV_HEADS, HD)
    values = low(low_back(matmul(normed, value_weight))).reshape(length, KV_HEADS, HD)
    queries = low(rotate(rms_scale(queries, query_gain), cosine, sine)).reshape(length, KV_HEADS, group, HD)
    keys = low(rotate(rms_scale(keys, key_gain), cosine, sine))
    block = min(512, length)
    factor = HD ** (-0.5)
    key_index = jnp.arange(length, dtype=jnp.int32)

    def attend(start):
        rows = lax.dynamic_slice_in_dim(queries, start, block, 0)
        row_index = start + jnp.arange(block, dtype=jnp.int32)
        row_segment = lax.dynamic_slice_in_dim(segment_row, start, block, 0)
        scores = jnp.einsum('qhgd,khd->hgqk', rows, keys, precision=lax.Precision.HIGHEST) * factor
        scores = low_back(scores)
        allowed = (row_segment[:, None] == segment_row[None, :]) & (key_index[None, :] <= row_index[:, None])
        scores = jnp.where(allowed[None, None], scores, NEG)
        weights = low(jax.nn.softmax(scores, axis=-1))
        return jnp.einsum('hgqk,khd->qhgd', weights, values, precision=lax.Precision.HIGHEST)
    starts = jnp.arange(0, length, block, dtype=jnp.int32)
    mixed = lax.map(jax.checkpoint(attend), starts).reshape(length, HEADS * HD)
    mixed = low(low_back(mixed))
    branch = low_back(matmul(mixed, output_weight))
    resid = low(inputs + branch)
    normed_two = low(rms_scale(resid, feed_gain))
    gate = low_back(matmul(normed_two, gate_weight))
    up_rows = low_back(matmul(normed_two, up_weight))
    hidden = low(jax.nn.silu(gate) * up_rows)
    return resid + low_back(matmul(hidden, down_weight))

def reference(inputs, cotangent, segments, positions, attention_gain, query_weight, key_weight, value_weight, query_gain, key_gain, output_weight, feed_gain, gate_weight, up_weight, down_weight):
    params = tuple((weight.astype(jnp.float32) for weight in (attention_gain, query_weight, key_weight, value_weight, query_gain, key_gain, output_weight, feed_gain, gate_weight, up_weight, down_weight)))
    seq_inputs = inputs.astype(jnp.float32).reshape(SEQS, SEQ_LEN, D)
    seq_cotangent = cotangent.astype(jnp.float32).reshape(SEQS, SEQ_LEN, D)

    def step(totals, item):
        block_in, block_cot, segment_row, position_row = item
        result, pull = jax.vjp(lambda value, weights: layer(value, segment_row, position_row, weights), block_in, params)
        grad_in, grad_params = pull(block_cot)
        return (jax.tree.map(jnp.add, totals, grad_params), (result, grad_in))
    zeros = jax.tree.map(jnp.zeros_like, params)
    grads, (results, grad_rows) = lax.scan(step, zeros, (seq_inputs, seq_cotangent, segments, positions))
    outputs = results.reshape(TOKENS, D).astype(jnp.bfloat16)
    grad_inputs = grad_rows.reshape(TOKENS, D)
    return (outputs, grad_inputs, grads[0], grads[1], grads[2], grads[3], grads[4], grads[5], grads[6], grads[7], grads[8], grads[9], grads[10])
```

```python
import jax
import jax.numpy as jnp
from jax import lax
from jax.sharding import PartitionSpec as P

HD = 128
EPS = 1e-06
THETA = 1000000.0
NEG = -1e30
BF = jnp.bfloat16
F32 = jnp.float32


def swap(value, axis, bit):
    size = lax.axis_size(axis)
    return lax.ppermute(value, axis, [(i, i ^ bit) for i in range(size)])


def bits_of(size):
    out = []
    bit = 1
    while bit < size:
        out.append(bit)
        bit *= 2
    return out


def gather_pieces(value, axis):
    pieces = {0: value}
    for bit in reversed(bits_of(lax.axis_size(axis))):
        for s in list(pieces):
            pieces[s | bit] = swap(pieces[s], axis, bit)
    return [pieces[s] for s in range(len(pieces))]


def scatter_pieces(pieces, axis):
    pieces = dict(enumerate(pieces))
    size = lax.axis_size(axis)
    for bit in bits_of(size):
        keep = [s for s in sorted(pieces, reverse=True) if not s & bit]
        for s in keep:
            total = pieces[s].astype(F32) + swap(pieces[s | bit].astype(BF), axis, bit).astype(F32)
            pieces[s] = total
            del pieces[s | bit]
    return pieces[0]


def in_order(pieces, index):
    count = len(pieces)
    blocks = list(pieces)
    for bit in bits_of(count):
        flag = (index & bit) != 0
        blocks = [jnp.where(flag, blocks[s ^ bit], blocks[s]) for s in range(count)]
    return jnp.concatenate(blocks, axis=-1)


def out_of_order(value, index, count):
    width = value.shape[-1] // count
    return [
        lax.dynamic_slice_in_dim(value, (index ^ s) * width, width, value.ndim - 1)
        for s in range(count)
    ]


def plane_far():
    far = [("dp", bit) for bit in bits_of(lax.axis_size("dp")) if bit > 1]
    return far + [("ctx", bit) for bit in bits_of(lax.axis_size("ctx"))]


def plane_gather(value):
    half = value.shape[0] // 2
    far = plane_far()
    out = []
    for part, order in ((value[:half], far), (value[half:], far[::-1])):
        rows = [part]
        for count, (axis, bit) in enumerate(order):
            more = [swap(r, axis, bit) for r in rows]
            rows = [jnp.concatenate(rows + more, axis=0)] if count == 0 else rows + more
        if lax.axis_size("dp") > 1:
            rows = rows + [swap(r, "dp", 1) for r in rows]
        out += rows
    return out


def plane_sum_halving(value, order):
    kept = []
    for axis, bit in order:
        flag = ((lax.axis_index(axis) // bit) % 2).astype(jnp.int32)
        half = value.shape[0] // 2
        keep = lax.dynamic_slice_in_dim(value, flag * half, half, 0)
        send = lax.dynamic_slice_in_dim(value, (1 - flag) * half, half, 0)
        value = (keep.astype(F32) + swap(send, axis, bit).astype(F32)).astype(BF)
        kept.append(flag)
    for (axis, bit), flag in zip(reversed(order), reversed(kept)):
        other = swap(value, axis, bit)
        value = jnp.where(
            flag == 0,
            jnp.concatenate([value, other], axis=0),
            jnp.concatenate([other, value], axis=0),
        )
    return value


def rope_tables(position_row):
    half = HD // 2
    freqs = jnp.exp(-(2.0 * jnp.arange(half, dtype=F32) / HD) * jnp.log(F32(THETA)))
    angles = position_row.astype(F32)[:, None] * freqs[None, :]
    return (jnp.cos(angles)[:, None, :], jnp.sin(angles)[:, None, :])


def rotate(value, cosine, sine):
    half = value.shape[-1] // 2
    first = value[..., :half]
    second = value[..., half:]
    return jnp.concatenate(
        [first * cosine - second * sine, second * cosine + first * sine], axis=-1
    )


def head_prepare(raw, gain, cosine, sine):
    count = raw.shape[0]
    heads = raw.reshape(count, -1, HD)
    normed = heads * lax.rsqrt(jnp.mean(heads * heads, axis=-1, keepdims=True) + EPS) * gain
    return rotate(normed, cosine, sine).reshape(count, -1)


def matmul(left, right):
    return jnp.dot(left, right, preferred_element_type=F32)


def matmul_nt(left, right):
    return lax.dot_general(left, right, (((1,), (1,)), ((), ())), preferred_element_type=F32)


def matmul_tn(left, right):
    return lax.dot_general(left, right, (((0,), (0,)), ((), ())), preferred_element_type=F32)


def per_device(
    inputs,
    cotangent,
    segments,
    positions,
    attention_gain,
    query_weight,
    key_weight,
    value_weight,
    query_gain,
    key_gain,
    output_weight,
    feed_gain,
    gate_weight,
    up_weight,
    down_weight,
):
    count = inputs.shape[0]
    shard = inputs.shape[1]
    width = cotangent.shape[1]
    tensor = lax.axis_size("tensor")
    me = lax.axis_index("tensor")
    column = me * shard
    place = lax.axis_index("ctx")
    core = lax.axis_index("dp") % 2
    kv_local = key_weight.shape[1] // HD
    group = query_weight.shape[1] // key_weight.shape[1]
    factor = HD ** (-0.5)
    gain_one = attention_gain.astype(F32)
    gain_two = feed_gain.astype(F32)
    gain_one_part = lax.dynamic_slice_in_dim(gain_one, column, shard)

    input_pieces = gather_pieces(inputs, "tensor")
    all_cotangent = plane_gather(cotangent)
    gathered = in_order(input_pieces, me).astype(F32)
    inverse_one = lax.rsqrt(jnp.mean(gathered * gathered, axis=-1, keepdims=True) + EPS)
    unit_one = gathered * inverse_one
    normed_one = (unit_one * gain_one).astype(BF)
    cosine, sine = rope_tables(positions[0])
    value_rows = matmul(normed_one, value_weight).astype(BF)
    key_raw = matmul(normed_one, key_weight)
    key_float, key_pull = jax.vjp(
        lambda raw, gain: head_prepare(raw, gain, cosine, sine), key_raw, key_gain.astype(F32)
    )
    key_rows = key_float.astype(BF)
    kv_rows = jnp.concatenate([key_rows, value_rows], axis=1)
    kv_pieces = gather_pieces(kv_rows, "ctx")
    query_raw = matmul(normed_one, query_weight)
    query_float, query_pull = jax.vjp(
        lambda raw, gain: head_prepare(raw, gain, cosine, sine), query_raw, query_gain.astype(F32)
    )
    query_rows = query_float.astype(BF)
    all_normed_one = plane_gather(normed_one)

    segment_row = segments[0]
    blocks = len(kv_pieces)
    kv_all = jnp.concatenate(kv_pieces, axis=0)
    kv_width = key_rows.shape[1]
    total_keys = kv_all.shape[0]
    key_heads = kv_all[:, :kv_width].reshape(total_keys, kv_local, HD)
    value_heads = kv_all[:, kv_width:].reshape(total_keys, kv_local, HD)
    block_iota = jnp.arange(count, dtype=jnp.int32)
    row_index = place * count + block_iota
    key_index = jnp.concatenate([(place ^ s) * count + block_iota for s in range(blocks)])
    row_segment = lax.dynamic_slice_in_dim(segment_row, place * count, count)
    key_segment = jnp.concatenate(
        [lax.dynamic_slice_in_dim(segment_row, (place ^ s) * count, count) for s in range(blocks)]
    )
    allowed = (row_segment[:, None] == key_segment[None, :]) & (
        key_index[None, :] <= row_index[:, None]
    )
    query_heads = query_rows.reshape(count, kv_local, group, HD)
    scores = (
        jnp.einsum("qhgd,khd->hgqk", query_heads, key_heads, preferred_element_type=F32) * factor
    )
    scores = jnp.where(allowed[None, None], scores, NEG)
    top = jnp.max(scores, axis=-1, keepdims=True)
    raised = jnp.exp(scores - top)
    total = jnp.sum(raised, axis=-1, keepdims=True)
    probs = raised / total
    weights = probs.astype(BF)
    mixed = jnp.einsum("hgqk,khd->qhgd", weights, value_heads, preferred_element_type=F32)
    mixed_rows = mixed.astype(BF).reshape(count, -1)
    branch_part = matmul(mixed_rows, output_weight).astype(BF)
    branch = scatter_pieces(out_of_order(branch_part, me, tensor), "tensor")
    resid_part = (inputs.astype(F32) + branch).astype(BF)
    resid_rows = in_order(gather_pieces(resid_part, "tensor"), me).astype(F32)

    inverse_two = lax.rsqrt(jnp.mean(resid_rows * resid_rows, axis=-1, keepdims=True) + EPS)
    unit_two = resid_rows * inverse_two
    normed_two = (unit_two * gain_two).astype(BF)
    all_normed_two = plane_gather(normed_two)

    def feed_forward(rows, grads, gate_w, up_w, down_w):
        gate = matmul(rows, gate_w)
        up = matmul(rows, up_w)
        sigmoid = jax.nn.sigmoid(gate)
        silu = gate * sigmoid
        hidden = (silu * up).astype(BF)
        grad_hidden = matmul_nt(grads, down_w)
        grad_gate = (grad_hidden * up * sigmoid * (1.0 + gate * (1.0 - sigmoid))).astype(BF)
        grad_up = (grad_hidden * silu).astype(BF)
        return hidden, grad_gate, grad_up

    hidden, grad_gate, grad_up = feed_forward(
        normed_two, cotangent, gate_weight, up_weight, down_weight
    )
    grad_normed_two = (matmul_nt(grad_gate, gate_weight) + matmul_nt(grad_up, up_weight)).astype(BF)
    grad_two_part = scatter_pieces(out_of_order(grad_normed_two, me, tensor), "tensor")
    grad_two = in_order(gather_pieces(grad_two_part.astype(BF), "tensor"), me).astype(F32)
    feed_part = matmul(hidden, down_weight).astype(BF)
    feed = scatter_pieces(out_of_order(feed_part, me, tensor), "tensor")
    outputs = (resid_part.astype(F32) + feed).astype(BF)

    row_total_two = jnp.sum(gain_two * grad_two * unit_two, axis=-1, keepdims=True)
    feed_sums = jnp.sum(grad_two * unit_two, axis=0)
    grad_resid = (
        cotangent.astype(F32)
        + inverse_two * (gain_two * grad_two)
        - unit_two * (inverse_two / width) * row_total_two
    )
    grad_resid_low = grad_resid.astype(BF)
    grad_resid_part = lax.dynamic_slice_in_dim(grad_resid, column, shard, 1)

    grad_mixed = matmul_nt(grad_resid_low, output_weight).astype(BF)
    grad_heads = grad_mixed.reshape(count, kv_local, group, HD)
    grad_probs = jnp.einsum("qhgd,khd->hgqk", grad_heads, value_heads, preferred_element_type=F32)
    delta = jnp.sum(probs * grad_probs, axis=-1, keepdims=True)
    grad_scores = (probs * (grad_probs - delta)).astype(BF)
    grad_keys = (
        jnp.einsum("hgqk,qhgd->khd", grad_scores, query_heads, preferred_element_type=F32) * factor
    ).reshape(total_keys, -1)
    grad_values = jnp.einsum(
        "hgqk,qhgd->khd", weights, grad_heads, preferred_element_type=F32
    ).reshape(total_keys, -1)
    grad_kv = jnp.concatenate([grad_keys, grad_values], axis=1)
    grad_kv = scatter_pieces(
        [grad_kv[s * count : (s + 1) * count] for s in range(blocks)], "ctx"
    )
    grad_query_rows = (
        jnp.einsum("hgqk,khd->qhgd", grad_scores, key_heads, preferred_element_type=F32) * factor
    ).reshape(count, -1)
    grad_query_raw, grad_query_gain = query_pull(grad_query_rows)
    grad_key_raw, grad_key_gain = key_pull(grad_kv[:, :kv_width])
    grad_query_low = grad_query_raw.astype(BF)
    grad_key_low = grad_key_raw.astype(BF)
    grad_value_low = grad_kv[:, kv_width:].astype(BF)

    grad_normed_one = (
        matmul_nt(grad_query_low, query_weight)
        + matmul_nt(grad_key_low, key_weight)
        + matmul_nt(grad_value_low, value_weight)
    )
    row_term_one = jnp.sum(gain_one * grad_normed_one * unit_one, axis=-1)
    attention_sums = jnp.sum(grad_normed_one * unit_one, axis=0)
    small = jnp.concatenate(
        [row_term_one, feed_sums * (1.0 / tensor), attention_sums, grad_query_gain, grad_key_gain]
    )
    for bit in bits_of(tensor):
        small = small + swap(small, "tensor", bit)
    row_total_one = small[:count, None]
    small = small[count:]
    for axis in ("dp", "ctx"):
        for bit in bits_of(lax.axis_size(axis)):
            small = small + swap(small, axis, bit)
    grad_one_part = scatter_pieces(
        out_of_order(grad_normed_one.astype(BF), me, tensor), "tensor"
    )
    unit_one_part = lax.dynamic_slice_in_dim(unit_one, column, shard, 1)
    grad_inputs = (
        grad_resid_part
        + inverse_one * (gain_one_part * grad_one_part)
        - unit_one_part * (inverse_one / width) * row_total_one
    )
    grad_feed_gain = lax.dynamic_slice_in_dim(small, column, shard)
    grad_attention_gain = lax.dynamic_slice_in_dim(small, width + column, shard)
    grad_query_gain = small[2 * width : 2 * width + HD]
    grad_key_gain = small[2 * width + HD :]

    order = [("dp", 1)] + plane_far() if lax.axis_size("dp") > 1 else plane_far()
    grad_output_w = plane_sum_halving(matmul_tn(mixed_rows, grad_resid_low).astype(BF), order)
    grad_output_w = grad_output_w.astype(F32)
    grad_low = jnp.concatenate([grad_query_low, grad_key_low, grad_value_low], axis=1)
    rows_one = jnp.concatenate(all_normed_one, axis=0)
    grads_one = jnp.concatenate(plane_gather(grad_low), axis=0)
    q_width = query_weight.shape[1]
    grad_query_w = matmul_tn(rows_one, grads_one[:, :q_width])
    grad_key_w = matmul_tn(rows_one, grads_one[:, q_width : q_width + kv_width])
    grad_value_w = matmul_tn(rows_one, grads_one[:, q_width + kv_width :])

    half = gate_weight.shape[1] // 2
    rows_two = jnp.concatenate(all_normed_two, axis=0)
    rows_cot = jnp.concatenate(all_cotangent, axis=0)
    gate_half = lax.dynamic_slice_in_dim(gate_weight, core * half, half, 1)
    up_half = lax.dynamic_slice_in_dim(up_weight, core * half, half, 1)
    down_half = lax.dynamic_slice_in_dim(down_weight, core * half, half, 0)
    all_hidden, all_grad_gate, all_grad_up = feed_forward(
        rows_two, rows_cot, gate_half, up_half, down_half
    )

    def both_halves(mine, axis):
        other = swap(mine.astype(BF), "dp", 1).astype(F32)
        return jnp.where(
            core == 0,
            jnp.concatenate([mine, other], axis=axis),
            jnp.concatenate([other, mine], axis=axis),
        )

    grad_down_w = both_halves(matmul_tn(all_hidden, rows_cot), 0)
    grad_gate_w = both_halves(matmul_tn(rows_two, all_grad_gate), 1)
    grad_up_w = both_halves(matmul_tn(rows_two, all_grad_up), 1)

    return (
        outputs,
        grad_inputs,
        grad_attention_gain,
        grad_query_w,
        grad_key_w,
        grad_value_w,
        grad_query_gain,
        grad_key_gain,
        grad_output_w,
        grad_feed_gain,
        grad_gate_w,
        grad_up_w,
        grad_down_w,
    )


def solution(mesh):
    in_specs = (
        P(("dp", "ctx"), "tensor"),
        P(("dp", "ctx"), None),
        P("dp", None),
        P("dp", "ctx"),
        P(),
        P(None, "tensor"),
        P(None, "tensor"),
        P(None, "tensor"),
        P(),
        P(),
        P("tensor", None),
        P(),
        P(None, "tensor"),
        P(None, "tensor"),
        P("tensor", None),
    )
    out_specs = (
        P(("dp", "ctx"), "tensor"),
        P(("dp", "ctx"), "tensor"),
        P("tensor"),
        P(None, "tensor"),
        P(None, "tensor"),
        P(None, "tensor"),
        P(),
        P(),
        P("tensor", None),
        P("tensor"),
        P(None, "tensor"),
        P(None, "tensor"),
        P("tensor", None),
    )
    return jax.shard_map(
        per_device, mesh=mesh, in_specs=in_specs, out_specs=out_specs, check_vma=False
    )
```

```python
import functools

import jax
import jax.numpy as jnp
from jax import lax
from jax.experimental import pallas as pl
from jax.experimental.pallas import tpu as pltpu
from jax.sharding import PartitionSpec as P

HD = 128
EPS = 1e-06
THETA = 1000000.0
NEG = -1e30
BF = jnp.bfloat16
F32 = jnp.float32
MIB = 1024 * 1024
VMEM_LIMIT = 63 * MIB + 900 * 1024
EXTRA = 16
SCALE = 1


def swap(value, axis, bit):
    size = lax.axis_size(axis)
    return lax.ppermute(value, axis, [(i, i ^ bit) for i in range(size)])


def bits_of(size):
    out = []
    bit = 1
    while bit < size:
        out.append(bit)
        bit *= 2
    return out


def gather_pieces(value, axis):
    pieces = {0: value}
    for bit in reversed(bits_of(lax.axis_size(axis))):
        for s in list(pieces):
            pieces[s | bit] = swap(pieces[s], axis, bit)
    return [pieces[s] for s in range(len(pieces))]


def send_pieces(pieces, axis):
    size = lax.axis_size(axis)
    return [
        lax.ppermute(pieces[s], axis, [(i, i ^ s) for i in range(size)])
        for s in sorted(range(1, size), key=lambda s: -s)
    ]


def send_all(value, axis):
    size = lax.axis_size(axis)
    pieces = {0: value}
    for s in range(size - 1, 0, -1):
        pieces[s] = lax.ppermute(value, axis, [(i, i ^ s) for i in range(size)])
    return [pieces[s] for s in range(size)]


def first_half(pieces, axis, *later):
    pieces = dict(enumerate(pieces))
    for s in [s for s in sorted(pieces, reverse=True) if not s & 1]:
        other = order_after(swap(pieces.pop(s | 1), axis, 1), *later)
        pieces[s] = (pieces[s].astype(F32) + other.astype(F32)).astype(BF if s else F32)
    return pieces


def second_half(pieces, axis, *earlier):
    for bit in bits_of(lax.axis_size(axis))[1:]:
        for s in [s for s in sorted(pieces, reverse=True) if not s & bit]:
            other = swap(order_after(pieces.pop(s | bit), *earlier), axis, bit)
            pieces[s] = (pieces[s].astype(F32) + other.astype(F32)).astype(BF if s else F32)
    return pieces[0]


def total_of(own, others):
    total = own.astype(F32)
    for other in others:
        total = total + other.astype(F32)
    return total


def far_masks():
    size = lax.axis_size("ctx")
    bits = [size * bit for bit in bits_of(lax.axis_size("dp")) if bit > 1] + bits_of(size)
    masks = [0]
    for bit in bits:
        masks = masks + [mask | bit for mask in masks]
    return masks


def send_plane(value, mask):
    if mask == 0:
        return value
    size = lax.axis_size("dp") * lax.axis_size("ctx")
    return lax.ppermute(value, ("dp", "ctx"), [(i, i ^ mask) for i in range(size)])


def plane_all(value):
    return lax.all_gather(value, ("dp", "ctx"), axis=0, tiled=True)


def sum_tensor(value):
    return lax.psum_scatter(value, "tensor", scatter_dimension=1, tiled=True)


def has_pair():
    return lax.axis_size("dp") > 1


def partners(parts, *earlier):
    if not has_pair():
        return []
    return [swap(order_after(part, *earlier), "dp", 1) for part in parts]


def order_after(value, *earlier):
    return lax.optimization_barrier((value, *earlier))[0] if earlier else value


def pieces_of(order, index, shard):
    return pl.multiple_of((index ^ order) * shard, shard)


def dot(left, right):
    return jnp.dot(left, right, preferred_element_type=F32)


def dot_nt(left, right):
    return lax.dot_general(left, right, (((1,), (1,)), ((), ())), preferred_element_type=F32)


def dot_tn(left, right):
    return lax.dot_general(left, right, (((0,), (0,)), ((), ())), preferred_element_type=F32)


def shape(*dims, dtype=BF):
    return jax.ShapeDtypeStruct(dims, dtype)


def size_of(arrays):
    return sum(a.size * a.dtype.itemsize for a in arrays)


def cost(flops, moved):
    return pl.CostEstimate(
        flops=int(flops) // SCALE, bytes_accessed=int(moved) // SCALE, transcendentals=0
    )


class Loads:
    def __init__(self, copies, buffers):
        self.copies = dict(enumerate(copies))
        self.buffers = buffers

    def __getitem__(self, index):
        if isinstance(index, slice):
            return [self[i] for i in range(*index.indices(len(self.buffers)))]
        if index in self.copies:
            self.copies.pop(index).wait()
        return self.buffers[index]

    def finish(self):
        for index in list(self.copies):
            self[index]


ANY = pl.BlockSpec(memory_space=pl.ANY)
SMEM = pl.BlockSpec(memory_space=pltpu.SMEM)


def kernel_call(body, ids, arrays, outs, flops, name, after=(), scratch=()):
    count, extra, results = len(arrays), len(after), len(outs)

    def run(ids, *refs):
        sources = refs[:count]
        out_refs = refs[count + extra : count + extra + results]
        buffers = refs[count + extra + results : 2 * count + extra + results]
        sems = refs[2 * count + extra + results]
        copies = [
            pltpu.make_async_copy(source, buffer, sems.at[i])
            for i, (source, buffer) in enumerate(zip(sources, buffers))
        ]
        for copy in copies:
            copy.start()
        loads = Loads(copies, buffers)
        body(ids, loads, *out_refs, *refs[2 * count + extra + results + 1 :])
        loads.finish()

    moved = size_of(arrays) + size_of(outs)
    return pl.pallas_call(
        run,
        out_shape=tuple(outs),
        in_specs=[SMEM] + [ANY] * (count + extra),
        out_specs=tuple(pl.BlockSpec(memory_space=pltpu.VMEM) for _ in outs),
        scratch_shapes=[pltpu.VMEM(a.shape, a.dtype) for a in arrays]
        + [pltpu.SemaphoreType.DMA((count,))]
        + [pltpu.VMEM(a.shape, a.dtype) for a in scratch],
        compiler_params=pltpu.CompilerParams(vmem_limit_bytes=VMEM_LIMIT),
        cost_estimate=cost(flops, moved),
        name=name,
    )(ids, *arrays, *after)


def turn(value):
    return pltpu.roll(value, HD // 2, 1)


def head_forward(raw, gain, cosine, sine):
    scale = lax.rsqrt(jnp.mean(raw * raw, axis=-1, keepdims=True) + EPS)
    normed = raw * scale * gain
    return normed * cosine + turn(normed) * sine


def head_backward(grad, raw, gain, cosine, sine):
    scale = lax.rsqrt(jnp.mean(raw * raw, axis=-1, keepdims=True) + EPS)
    unit = raw * scale
    grad_normed = grad * cosine + turn(grad * sine)
    grad_gain = jnp.sum(grad_normed * unit, axis=0, keepdims=True)
    inner = grad_normed * gain
    grad_raw = scale * (inner - unit * jnp.mean(inner * unit, axis=-1, keepdims=True))
    return grad_raw, grad_gain


def key_value_body(count, ids, loads, normed_ref, kv, raw_ref, inverse_ref):
    pieces = loads[:count]
    rows, shard = pieces[0].shape
    squares = 0.0
    for piece in pieces:
        x = piece[...].astype(F32)
        squares += jnp.sum(x * x, axis=-1, keepdims=True)
    inverse = lax.rsqrt(squares * (1.0 / (shard * count)) + EPS)
    inverse_ref[...] = inverse
    gain, key_gain, cosine, sine, wk, wv = loads[count : count + 6]
    kv_width = wk.shape[1]
    key_raw = jnp.zeros((rows, kv_width), F32)
    values = jnp.zeros((rows, kv_width), F32)
    for s in range(count):
        off = pieces_of(s, ids[0], shard)
        normed = (pieces[s][...].astype(F32) * inverse * gain[:, pl.ds(off, shard)]).astype(BF)
        normed_ref[:, pl.ds(off, shard)] = normed
        key_raw += dot(normed, wk[pl.ds(off, shard), :])
        values += dot(normed, wv[pl.ds(off, shard), :])
    raw_ref[...] = key_raw
    for h in range(kv_width // HD):
        cols = slice(h * HD, (h + 1) * HD)
        out = head_forward(key_raw[:, cols], key_gain[...], cosine[...], sine[...])
        kv[:, cols] = out.astype(BF)
    kv[:, kv_width:] = values.astype(BF)


def query_body(ids, loads, q_ref, raw_ref):
    normed, wq, query_gain, cosine, sine = loads[:5]
    raw = dot(normed[...], wq[...])
    raw_ref[...] = raw
    for h in range(wq.shape[1] // HD):
        cols = slice(h * HD, (h + 1) * HD)
        out = head_forward(raw[:, cols], query_gain[...], cosine[...], sine[...])
        q_ref[:, cols] = out.astype(BF)


def head_probs(ids, q, blocks, head, group, row_segment, key_segments):
    rows = q.shape[0]
    kv = head // group
    cols = slice(head * HD, (head + 1) * HD)
    row_index = ids[1] * rows + lax.broadcasted_iota(jnp.int32, (rows, rows), 0)
    parts = []
    for s, block in enumerate(blocks):
        scores = dot_nt(q[:, cols], block[:, kv * HD : (kv + 1) * HD]) * HD ** (-0.5)
        key_index = (ids[1] ^ s) * rows + lax.broadcasted_iota(jnp.int32, (rows, rows), 1)
        allowed = (row_segment[...] == key_segments[s][...]) & (key_index <= row_index)
        parts.append(jnp.where(allowed, scores, NEG))
    top = parts[0].max(axis=-1, keepdims=True)
    for part in parts[1:]:
        top = jnp.maximum(top, part.max(axis=-1, keepdims=True))
    parts = [jnp.exp(part - top) for part in parts]
    total = sum(jnp.sum(part, axis=-1, keepdims=True) for part in parts)
    share = 1.0 / total
    return [part * share for part in parts]


def attention_body(count, group, blocks, ids, loads, mixed_ref, *outs):
    q, row_segment = loads[:2]
    kvs = loads[2 : 2 + blocks]
    key_segments = loads[2 + blocks : 2 + 2 * blocks]
    kv_width = kvs[0].shape[1] // 2
    for h in range(q.shape[1] // HD):
        probs = head_probs(ids, q, kvs, h, group, row_segment, key_segments)
        start = kv_width + (h // group) * HD
        mixed = sum(
            dot(p.astype(BF), block[:, start : start + HD]) for p, block in zip(probs, kvs)
        )
        mixed_ref[:, h * HD : (h + 1) * HD] = mixed.astype(BF)
    wo = loads[2 + 2 * blocks]
    shard = wo.shape[1] // count
    for s in range(count):
        off = pieces_of(s, ids[0], shard)
        outs[s][...] = dot(mixed_ref[...], wo[:, pl.ds(off, shard)]).astype(BF)


def second_norm_body(count, ids, loads, normed_ref, resid_ref, inverse_ref):
    pieces = loads[:count]
    gain = loads[count]
    rows, shard = pieces[0].shape
    squares = 0.0
    for piece in pieces:
        x = piece[...].astype(F32)
        squares += jnp.sum(x * x, axis=-1, keepdims=True)
    inverse = lax.rsqrt(squares * (1.0 / (shard * count)) + EPS)
    inverse_ref[...] = inverse
    for s in range(count):
        off = pieces_of(s, ids[0], shard)
        cols = pl.ds(off, shard)
        x = pieces[s][...]
        resid_ref[:, cols] = x
        normed_ref[:, cols] = (x.astype(F32) * inverse * gain[:, cols]).astype(BF)


def gated_terms(gate, up, grad_hidden):
    sigmoid = jax.nn.sigmoid(gate)
    silu = gate * sigmoid
    grad_gate = grad_hidden * up * sigmoid * (1.0 + gate * (1.0 - sigmoid))
    return silu * up, grad_gate, grad_hidden * silu


def feed_forward_body(tile, extra, ids, normed_hbm, cot_hbm, wg_hbm, wu_hbm, wd_hbm, *refs):
    refs = refs[extra:]
    grad_out, feed_out, normed, cot, wg, wu, wd, total, feed, sems = refs
    units = wg.shape[1]
    tiles = units // tile
    first = [
        pltpu.make_async_copy(normed_hbm, normed, sems.at[3 * tiles]),
        pltpu.make_async_copy(cot_hbm, cot, sems.at[3 * tiles + 1]),
    ]

    def weights(t):
        cols = pl.ds(pl.multiple_of(t * tile, tile), tile)
        return [
            pltpu.make_async_copy(wg_hbm.at[:, cols], wg.at[:, cols], sems.at[t]),
            pltpu.make_async_copy(wu_hbm.at[:, cols], wu.at[:, cols], sems.at[tiles + t]),
            pltpu.make_async_copy(wd_hbm.at[cols, :], wd.at[cols, :], sems.at[2 * tiles + t]),
        ]

    for copy in first:
        copy.start()
    for t in range(tiles):
        for copy in weights(t):
            copy.start()
    total[...] = jnp.zeros_like(total)
    feed[...] = jnp.zeros_like(feed)
    for copy in first:
        copy.wait()

    def step(t, carry):
        cols = pl.ds(pl.multiple_of(t * tile, tile), tile)
        gate_copy, up_copy, down_copy = weights(t)
        gate_copy.wait()
        up_copy.wait()
        down_copy.wait()
        gate = dot(normed[...], wg[:, cols])
        up = dot(normed[...], wu[:, cols])
        grad_hidden = dot_nt(cot[...], wd[cols, :])
        hidden, grad_gate, grad_up = gated_terms(gate, up, grad_hidden)
        total[...] += dot_nt(grad_gate.astype(BF), wg[:, cols]) + dot_nt(
            grad_up.astype(BF), wu[:, cols]
        )
        feed[...] += dot(hidden.astype(BF), wd[cols, :])
        return carry

    lax.fori_loop(0, tiles, step, 0)
    grad_out[...] = total[...].astype(BF)
    feed_out[...] = feed[...].astype(BF)


def feed_forward(ids, normed, cot, wg, wu, wd, after=()):
    rows, width = cot.shape
    units = wg.shape[1]
    tile = max(t for t in (512, 384, 256, 128) if units % t == 0)
    arrays = [normed, cot, wg, wu, wd]
    outs = [shape(rows, width)] * 2
    moved = size_of(arrays) + size_of(outs)
    return pl.pallas_call(
        functools.partial(feed_forward_body, tile, len(after)),
        out_shape=outs,
        in_specs=[SMEM] + [ANY] * (5 + len(after)),
        out_specs=[pl.BlockSpec(memory_space=pltpu.VMEM) for _ in outs],
        scratch_shapes=[pltpu.VMEM(a.shape, a.dtype) for a in arrays]
        + [
            pltpu.VMEM((rows, width), F32),
            pltpu.VMEM((rows, width), F32),
            pltpu.SemaphoreType.DMA((3 * (units // tile) + 2,)),
        ],
        compiler_params=pltpu.CompilerParams(
            vmem_limit_bytes=VMEM_LIMIT
        ),
        cost_estimate=cost(12 * rows * width * units, moved),
        name="feed_forward",
    )(ids, *arrays, *after)


def middle_body(count, group, blocks, ids, loads, own_ref, low_ref, sums_ref, *outs):
    grads, resid, inverse_ref, gain, cot = loads[:5]
    rows, width = grads.shape
    shard = width // count
    inverse = inverse_ref[...]
    row_total = 0.0
    for s in range(count):
        cols = pl.ds(pieces_of(s, ids[0], shard), shard)
        product = grads[:, cols].astype(F32) * (resid[:, cols].astype(F32) * inverse)
        sums_ref[:, cols] = jnp.sum(product, axis=0, keepdims=True)
        row_total += jnp.sum(product * gain[:, cols], axis=-1, keepdims=True)
    scale = row_total * inverse * (1.0 / width)
    wo = loads[5]
    mixed = jnp.zeros((rows, wo.shape[0]), F32)
    for s in range(count):
        cols = pl.ds(pieces_of(s, ids[0], shard), shard)
        unit = resid[:, cols].astype(F32) * inverse
        grad = (
            cot[:, cols].astype(F32)
            + inverse * (gain[:, cols] * grads[:, cols].astype(F32))
            - unit * scale
        )
        if s == 0:
            own_ref[...] = grad
        low = grad.astype(BF)
        low_ref[:, cols] = low
        mixed += dot_nt(low, wo[:, cols])
    attention_backward(group, blocks, ids, loads[6:], mixed.astype(BF), *outs)


def attention_backward(group, blocks, ids, loads, grads, low_ref, gain_ref, own_ref, *others):
    q, row_segment = loads[:2]
    kvs = loads[2 : 2 + blocks]
    key_segments = loads[2 + blocks : 2 + 2 * blocks]
    raw, query_gain, cosine, sine = loads[2 + 2 * blocks : 6 + 2 * blocks]
    kv_width = kvs[0].shape[1] // 2
    factor = HD ** (-0.5)
    gain_total = jnp.zeros((1, HD), F32)
    outs = [own_ref] + list(others)
    for kv in range(kv_width // HD):
        key_cols = slice(kv * HD, (kv + 1) * HD)
        value_cols = slice(kv_width + kv * HD, kv_width + (kv + 1) * HD)
        key_sums = [0.0] * blocks
        value_sums = [0.0] * blocks
        for h in range(kv * group, (kv + 1) * group):
            cols = slice(h * HD, (h + 1) * HD)
            probs = head_probs(ids, q, kvs, h, group, row_segment, key_segments)
            grad = grads[:, cols]
            grad_probs = [dot_nt(grad, block[:, value_cols]) for block in kvs]
            delta = sum(jnp.sum(p * g, axis=-1, keepdims=True) for p, g in zip(probs, grad_probs))
            scores = [(p * (g - delta)).astype(BF) for p, g in zip(probs, grad_probs)]
            grad_query = sum(dot(g, block[:, key_cols]) for g, block in zip(scores, kvs)) * factor
            for s in range(blocks):
                key_sums[s] += dot_tn(scores[s], q[:, cols])
                value_sums[s] += dot_tn(probs[s].astype(BF), grad)
            grad_raw, grad_gain = head_backward(
                grad_query, raw[:, cols], query_gain[...], cosine[...], sine[...]
            )
            low_ref[:, cols] = grad_raw.astype(BF)
            gain_total += grad_gain
        for s in range(blocks):
            outs[s][:, key_cols] = (key_sums[s] * factor).astype(outs[s].dtype)
            outs[s][:, value_cols] = value_sums[s].astype(outs[s].dtype)
    gain_ref[...] = gain_total


def key_backward_body(blocks, ids, loads, low_ref, gain_ref):
    sums = loads[:blocks]
    raw, key_gain, cosine, sine, query_low = loads[blocks : blocks + 5]
    q_width = query_low.shape[1]
    kv_width = raw.shape[1]
    low_ref[:, :q_width] = query_low[...]
    total = sums[0][...]
    for other in sums[1:]:
        total = total + other[...].astype(F32)
    gain_total = jnp.zeros((1, HD), F32)
    for h in range(kv_width // HD):
        cols = slice(h * HD, (h + 1) * HD)
        grad_raw, grad_gain = head_backward(
            total[:, cols], raw[:, cols], key_gain[...], cosine[...], sine[...]
        )
        low_ref[:, q_width + h * HD : q_width + (h + 1) * HD] = grad_raw.astype(BF)
        gain_total += grad_gain
    low_ref[:, q_width + kv_width :] = total[:, kv_width:].astype(BF)
    gain_ref[...] = gain_total


def first_grad_body(count, ids, loads, *outs):
    pieces = loads[:count]
    inverse_ref, gain, query_sums, key_sums, grads, wq, wk, wv = loads[count : count + 8]
    rows, shard = pieces[0].shape
    q_width, kv_width = wq.shape[1], wk.shape[1]
    inverse = inverse_ref[...]
    row_total = jnp.zeros((rows, 1), F32)
    for s in range(count):
        cols = pl.ds(pieces_of(s, ids[0], shard), shard)
        grad = (
            dot_nt(grads[:, :q_width], wq[cols, :])
            + dot_nt(grads[:, q_width : q_width + kv_width], wk[cols, :])
            + dot_nt(grads[:, q_width + kv_width :], wv[cols, :])
        )
        product = grad * (pieces[s][...].astype(F32) * inverse)
        outs[s][:rows, :] = grad.astype(BF)
        outs[s][rows:, :] = jnp.zeros((EXTRA, shard), BF)
        outs[s][rows : rows + 1, :] = jnp.sum(product, axis=0, keepdims=True).astype(BF)
        row_total += jnp.sum(product * gain[:, cols], axis=-1, keepdims=True)
    turned = jnp.broadcast_to(row_total, (rows, HD)).T[:1]
    small = jnp.concatenate([turned, query_sums[...], key_sums[...]], axis=1).astype(BF)
    for s in range(count):
        for r in range(small.shape[1] // shard):
            row = rows + 1 + r
            outs[s][row : row + 1, :] = small[:, r * shard : (r + 1) * shard]


def feed_weight_body(parts, extra, last, block, ids, *refs):
    rows_hbm, cots_hbm = refs[:parts], refs[parts : 2 * parts]
    wg_hbm, wu_hbm, wd_hbm = refs[2 * parts : 2 * parts + 3]
    refs = refs[2 * parts + 3 + extra :]
    dwg, dwu, dwd = refs[:3]
    lows = refs[3:6] if last else ()
    refs = refs[6:] if last else refs[3:]
    rows, cots, hid, gates, ups, wg, wu, wd, gate_out, up_out, down_out = refs[:11]
    refs = refs[11:]
    if last:
        gate_held, up_held, down_held, gate_cut, up_cut, down_cut = refs[:6]
        refs = refs[6:]
    row_sems, cot_sems, weight_sems, held_sems, out_sems = refs
    width = rows.shape[1]
    size = rows_hbm[0].shape[0]
    group = min(2, parts)
    chunk = group * size
    steps = wg_hbm.shape[1] // block // 2
    tile = width // 2

    def mine(b):
        return pl.ds(pl.multiple_of((ids[2] * steps + b) * block, block), block)

    def weights(b, slot):
        return [
            pltpu.make_async_copy(wg_hbm.at[:, mine(b)], wg.at[slot], weight_sems.at[slot, 0]),
            pltpu.make_async_copy(wu_hbm.at[:, mine(b)], wu.at[slot], weight_sems.at[slot, 1]),
            pltpu.make_async_copy(wd_hbm.at[mine(b), :], wd.at[slot], weight_sems.at[slot, 2]),
        ]

    def tile_at(t):
        return pl.ds(pl.multiple_of(t * tile, tile), tile)

    def held(b, t):
        at = tile_at(t)
        pairs = [
            (dwg.at[at, mine(b)], gate_held.at[at, :]),
            (dwu.at[at, mine(b)], up_held.at[at, :]),
            (dwd.at[mine(b), at], down_held.at[:, at]),
        ]
        return [pltpu.make_async_copy(a, c, held_sems.at[t, i]) for i, (a, c) in enumerate(pairs)]

    def results(b, t):
        at = tile_at(t)
        low = pl.ds(pl.multiple_of(b * block, block), block)
        pairs = [
            (gate_out.at[at, :], dwg.at[at, mine(b)]),
            (up_out.at[at, :], dwu.at[at, mine(b)]),
            (down_out.at[:, at], dwd.at[mine(b), at]),
        ]
        if last:
            pairs += [
                (gate_cut.at[at, :], lows[0].at[at, low]),
                (up_cut.at[at, :], lows[1].at[at, low]),
                (down_cut.at[:, at], lows[2].at[low, at]),
            ]
        return [pltpu.make_async_copy(a, c, out_sems.at[t, i]) for i, (a, c) in enumerate(pairs)]

    for copy in weights(0, 0):
        copy.start()
    for i in range(parts):
        place = pl.ds(i * size, size)
        pltpu.make_async_copy(rows_hbm[i], rows.at[place, :], row_sems.at[i // group]).start()
        pltpu.make_async_copy(cots_hbm[i], cots.at[place, :], cot_sems.at[i // group]).start()

    def one_block(b, carry):
        slot = lax.rem(b, 2)
        for copy in weights(b, slot):
            copy.wait()
        if last:
            for t in range(2):
                for copy in held(b, t):
                    copy.start()

        @pl.when(b + 1 < steps)
        def _():
            for copy in weights(b + 1, 1 - slot):
                copy.start()

        def recompute(c, carry):
            place = pl.ds(pl.multiple_of(c * chunk, chunk), chunk)

            @pl.when(b == 0)
            def _():
                pltpu.make_async_copy(rows.at[place, :], rows.at[place, :], row_sems.at[c]).wait()
                pltpu.make_async_copy(cots.at[place, :], cots.at[place, :], cot_sems.at[c]).wait()

            own = rows[place, :]
            gate = dot(own, wg[slot])
            up = dot(own, wu[slot])
            grad_hidden = dot_nt(cots[place, :], wd[slot])
            hidden, grad_gate, grad_up = gated_terms(gate, up, grad_hidden)
            hid[place, :] = hidden.astype(BF)
            gates[place, :] = grad_gate.astype(BF)
            ups[place, :] = grad_up.astype(BF)
            return carry

        lax.fori_loop(0, parts // group, recompute, 0)

        def products(t, carry):
            @pl.when(b > 0)
            def _():
                for copy in results(b, t):
                    copy.wait()

            cols = tile_at(t)
            down = dot_tn(hid[...], cots[:, cols])
            gate = dot_tn(rows[:, cols], gates[...])
            up = dot_tn(rows[:, cols], ups[...])
            if last:
                for copy in held(b, t):
                    copy.wait()
                down = (down + down_held[:, cols]).astype(BF)
                gate = (gate + gate_held[cols, :]).astype(BF)
                up = (up + up_held[cols, :]).astype(BF)
                down_cut[:, cols] = down
                gate_cut[cols, :] = gate
                up_cut[cols, :] = up
            down_out[:, cols] = down.astype(F32)
            gate_out[cols, :] = gate.astype(F32)
            up_out[cols, :] = up.astype(F32)
            for copy in results(b, t):
                copy.start()
            return carry

        lax.fori_loop(0, 2, products, 0)
        return carry

    lax.fori_loop(0, steps, one_block, 0)
    for t in range(2):
        for copy in results(0, t):
            copy.wait()


def feed_weights(ids, rows, cots, wg, wu, wd, block, held, last, after=()):
    parts = len(rows)
    size, width = rows[0].shape
    tokens = size * parts
    units = wg.shape[1]
    held = list(held or ())
    outs = [
        shape(width, units, dtype=F32),
        shape(width, units, dtype=F32),
        shape(units, width, dtype=F32),
    ]
    tiles = [
        shape(width, block, dtype=F32),
        shape(width, block, dtype=F32),
        shape(block, width, dtype=F32),
    ]
    scratch = [
        shape(tokens, width),
        shape(tokens, width),
        shape(tokens, block),
        shape(tokens, block),
        shape(tokens, block),
        shape(2, width, block),
        shape(2, width, block),
        shape(2, block, width),
        *tiles,
    ]
    if last:
        outs += [shape(width, units // 2), shape(width, units // 2), shape(units // 2, width)]
        scratch += [*tiles, shape(width, block), shape(width, block), shape(block, width)]
    if not held and last:
        held = [jnp.zeros(o.shape, F32) for o in outs[:3]]
    extra = len(held) + len(after)
    return pl.pallas_call(
        functools.partial(feed_weight_body, parts, extra, last, block),
        out_shape=outs,
        in_specs=[SMEM] + [ANY] * (2 * parts + 3 + extra),
        out_specs=[ANY] * len(outs),
        scratch_shapes=[pltpu.VMEM(a.shape, a.dtype) for a in scratch]
        + [
            pltpu.SemaphoreType.DMA((parts,)),
            pltpu.SemaphoreType.DMA((parts,)),
            pltpu.SemaphoreType.DMA((2, 3)),
            pltpu.SemaphoreType.DMA((2, 3)),
            pltpu.SemaphoreType.DMA((2, 6)),
        ],
        input_output_aliases={4 + 2 * parts + i: i for i in range(len(held))},
        compiler_params=pltpu.CompilerParams(vmem_limit_bytes=VMEM_LIMIT),
        cost_estimate=cost(6 * tokens * width * units, 4 * tokens * width),
        name="feed_weights",
    )(ids, *rows, *cots, wg, wu, wd, *held, *after)


def assemble_body(extra, ids, gate_low, up_low, down_low, *refs):
    dwg, dwu, dwd = refs[-3:]
    dwg[...] = gate_low[...].astype(F32)
    dwu[...] = up_low[...].astype(F32)
    dwd[...] = down_low[...].astype(F32)


def assemble(ids, lows, block, held, after=()):
    width, units = held[0].shape
    steps = units // block // 2
    tile = width // 2
    cols_in = pl.BlockSpec((tile, block), lambda b, i, ids: (i, b))
    rows_in = pl.BlockSpec((block, tile), lambda b, i, ids: (b, i))
    cols_out = pl.BlockSpec((tile, block), lambda b, i, ids: (i, (1 - ids[2]) * steps + b))
    rows_out = pl.BlockSpec((block, tile), lambda b, i, ids: ((1 - ids[2]) * steps + b, i))
    return pl.pallas_call(
        functools.partial(assemble_body, len(after)),
        out_shape=[shape(*a.shape, dtype=F32) for a in held],
        grid_spec=pltpu.PrefetchScalarGridSpec(
            num_scalar_prefetch=1,
            grid=(steps, 2),
            in_specs=[cols_in, cols_in, rows_in] + [ANY] * (3 + len(after)),
            out_specs=[cols_out, cols_out, rows_out],
        ),
        input_output_aliases={4: 0, 5: 1, 6: 2},
        compiler_params=pltpu.CompilerParams(vmem_limit_bytes=VMEM_LIMIT),
        cost_estimate=cost(0, 9 * width * units),
        name="assemble",
    )(ids, *lows, *held, *after)


def projection_body(parts, tile, extra, ids, *refs):
    rows_hbm, grads_hbm = refs[:parts], refs[parts : 2 * parts]
    refs = refs[2 * parts + extra :]
    outs_hbm = refs[:3]
    rows, grads, *outs, row_sems, grad_sem, out_sems = refs[3:]
    width = rows.shape[1]
    tiles = width // tile
    at = 0
    for i in range(parts):
        place = pl.ds(at, grads_hbm[i].shape[0])
        pltpu.make_async_copy(grads_hbm[i], grads.at[place, :], grad_sem).start()
        at += grads_hbm[i].shape[0]
    for t in range(tiles):
        cols = pl.ds(t * tile, tile)
        at = 0
        for i in range(parts):
            place = pl.ds(at, rows_hbm[i].shape[0])
            pltpu.make_async_copy(
                rows_hbm[i].at[:, cols], rows.at[place, cols], row_sems.at[t]
            ).start()
            at += rows_hbm[i].shape[0]
    pltpu.make_async_copy(grads, grads, grad_sem).wait()
    q_width, kv_width = outs[0].shape[1], outs[1].shape[1]

    def copies(t):
        cols = pl.ds(pl.multiple_of(t * tile, tile), tile)
        return [
            pltpu.make_async_copy(a.at[cols, :], b.at[cols, :], out_sems.at[t, i])
            for i, (a, b) in enumerate(zip(outs, outs_hbm))
        ]

    def products(t, carry):
        cols = pl.ds(pl.multiple_of(t * tile, tile), tile)
        pltpu.make_async_copy(rows.at[:, cols], rows.at[:, cols], row_sems.at[t]).wait()
        total = dot_tn(rows[:, cols], grads[...])
        outs[0][cols, :] = total[:, :q_width]
        outs[1][cols, :] = total[:, q_width : q_width + kv_width]
        outs[2][cols, :] = total[:, q_width + kv_width :]
        for copy in copies(t):
            copy.start()
        return carry

    lax.fori_loop(0, tiles, products, 0)

    def finish(t, carry):
        for copy in copies(t):
            copy.wait()
        return carry

    lax.fori_loop(0, tiles, finish, 0)


def projection_weights(ids, rows, grads, q_width, kv_width, after):
    parts = len(rows)
    width = rows[0].shape[1]
    tokens = sum(a.shape[0] for a in rows)
    tile = 512
    outs = [shape(width, w, dtype=F32) for w in (q_width, kv_width, kv_width)]
    scratch = [shape(tokens, width), shape(tokens, q_width + 2 * kv_width)] + outs
    return pl.pallas_call(
        functools.partial(projection_body, parts, tile, len(after)),
        out_shape=outs,
        in_specs=[SMEM] + [ANY] * (2 * parts + len(after)),
        out_specs=[ANY] * 3,
        scratch_shapes=[pltpu.VMEM(a.shape, a.dtype) for a in scratch]
        + [
            pltpu.SemaphoreType.DMA((width // tile,)),
            pltpu.SemaphoreType.DMA(()),
            pltpu.SemaphoreType.DMA((width // tile, 3)),
        ],
        compiler_params=pltpu.CompilerParams(
            vmem_limit_bytes=VMEM_LIMIT
        ),
        cost_estimate=cost(2 * tokens * width * (q_width + 2 * kv_width), 2 * tokens * width),
        name="projection_weights",
    )(ids, *rows, *grads, *after)


def matmul_tn(left, right):
    return lax.dot_general(left, right, (((0,), (0,)), ((), ())), preferred_element_type=F32)


def rope_tables(position_row):
    half = HD // 2
    freqs = jnp.exp(-(2.0 * jnp.arange(half, dtype=F32) / HD) * jnp.log(F32(THETA)))
    angles = position_row.astype(F32)[:, None] * freqs[None, :]
    cosine, sine = jnp.cos(angles), jnp.sin(angles)
    return jnp.concatenate([cosine, cosine], axis=1), jnp.concatenate([-sine, sine], axis=1)


def per_device(
    inputs,
    cotangent,
    segments,
    positions,
    attention_gain,
    query_weight,
    key_weight,
    value_weight,
    query_gain,
    key_gain,
    output_weight,
    feed_gain,
    gate_weight,
    up_weight,
    down_weight,
):
    count, shard = inputs.shape
    width = cotangent.shape[1]
    tensor = lax.axis_size("tensor")
    me = lax.axis_index("tensor")
    column = me * shard
    place = lax.axis_index("ctx")
    core = lax.axis_index("dp") % 2
    ids = jnp.stack([me, place, core, lax.axis_index("dp")]).astype(jnp.int32)
    q_width, kv_width = query_weight.shape[1], key_weight.shape[1]
    group = q_width // kv_width
    blocks = lax.axis_size("ctx")
    gain_one = attention_gain.astype(F32)[None]
    gain_two = feed_gain.astype(F32)[None]
    gain_q = query_gain.astype(F32)[None]
    gain_k = key_gain.astype(F32)[None]
    gain_one_part = lax.dynamic_slice_in_dim(gain_one, column, shard, 1)
    hidden_units = gate_weight.shape[1]
    block = 256 if (hidden_units // 2) % 256 == 0 else 128

    masks = far_masks()
    first_masks = len(masks) // 2 or 1
    x_pieces = gather_pieces(inputs, "tensor")
    cot_parts = [send_plane(cotangent, mask) for mask in masks[:first_masks + 1]]
    cosine, sine = rope_tables(positions[0])
    normed_one, kv_rows, key_raw, inverse_one = kernel_call(
        functools.partial(key_value_body, tensor),
        ids,
        [*x_pieces, gain_one, gain_k, cosine, sine, key_weight, value_weight],
        [
            shape(count, width),
            shape(count, 2 * kv_width),
            shape(count, kv_width, dtype=F32),
            shape(count, 1, dtype=F32),
        ],
        4 * count * width * kv_width,
        "key_value",
        after=cot_parts[1:],
    )
    kv_pieces = gather_pieces(kv_rows, "ctx")
    all_normed_one = plane_all(order_after(normed_one, *kv_pieces[1:]))
    query_rows, query_raw = kernel_call(
        query_body,
        ids,
        [normed_one, query_weight, gain_q, cosine, sine],
        [shape(count, q_width), shape(count, q_width, dtype=F32)],
        2 * count * width * q_width,
        "query",
    )

    segment_row = segments[0]
    row_segment = lax.dynamic_slice_in_dim(segment_row, place * count, count)[:, None]
    key_segments = [
        lax.dynamic_slice_in_dim(segment_row, (place ^ s) * count, count)[None]
        for s in range(blocks)
    ]
    mixed_rows, *branch_pieces = kernel_call(
        functools.partial(attention_body, tensor, group, blocks),
        ids,
        [query_rows, row_segment, *kv_pieces, *key_segments, output_weight],
        [shape(count, q_width)] + [shape(count, shard)] * tensor,
        4 * count * count * blocks * q_width + 2 * count * width * q_width,
        "attention",
    )
    branch = second_half(first_half(branch_pieces, "tensor"), "tensor")
    resid_part = (inputs.astype(F32) + branch).astype(BF)
    resid_pieces = gather_pieces(resid_part, "tensor")
    cot_partners = partners(cot_parts[: first_masks + 1])

    normed_two, resid, inverse_two = kernel_call(
        functools.partial(second_norm_body, tensor),
        ids,
        [*resid_pieces, gain_two],
        [shape(count, width), shape(count, width), shape(count, 1, dtype=F32)],
        8 * count * width,
        "second_norm",
        after=cot_partners,
    )
    two_parts = [send_plane(normed_two, mask) for mask in masks[: first_masks + 1]]
    grad_two_part, feed_part = feed_forward(
        ids, normed_two, cotangent, gate_weight, up_weight, down_weight
    )
    feed_done = feed_part
    grad_two_part = sum_tensor(grad_two_part)
    late = order_after(normed_two, feed_done)
    two_parts += [send_plane(late, mask) for mask in masks[first_masks + 1 :]]
    late = order_after(cotangent, feed_done)
    cot_parts += [send_plane(late, mask) for mask in masks[first_masks + 1 :]]
    groups = [slice(0, first_masks), slice(first_masks, None)] if len(masks) > 1 else [slice(0, None)]
    last = len(groups) - 1
    two_partners = partners(two_parts[:1]) + partners(two_parts[1 : first_masks + 1], feed_done)

    def weights_of(g, held, after):
        return feed_weights(
            ids,
            two_parts[groups[g]] + two_partners[groups[g]],
            cot_parts[groups[g]] + cot_partners[groups[g]],
            gate_weight,
            up_weight,
            down_weight,
            block,
            held,
            g == last,
            after,
        )

    held, done = None, [feed_done, *two_partners, all_normed_one]
    for g in range(last):
        held = weights_of(g, held, done)
        done = held[:1]
    two_partners += partners(two_parts[first_masks + 1 :], *done)
    cot_partners += partners(cot_parts[first_masks + 1 :], *done)
    grad_two = lax.all_gather(grad_two_part, "tensor", axis=1, tiled=True)
    *held, gate_low, up_low, down_low = weights_of(last, held, [grad_two_part])
    lows = [gate_low, up_low, down_low]
    feed = sum_tensor(order_after(feed_part, gate_low))
    lows = [swap(low, "dp", 1) for low in lows] if has_pair() else lows

    (
        grad_resid_part,
        grad_resid_low,
        feed_sums,
        grad_query_low,
        grad_query_gain,
        grad_kv,
        *grad_kv_sent,
    ) = kernel_call(
        functools.partial(middle_body, tensor, group, blocks),
        ids,
        [
            grad_two,
            resid,
            inverse_two,
            gain_two,
            cotangent,
            output_weight,
            query_rows,
            row_segment,
            *kv_pieces,
            *key_segments,
            query_raw,
            gain_q,
            cosine,
            sine,
        ],
        [
            shape(count, shard, dtype=F32),
            shape(count, width),
            shape(1, width, dtype=F32),
            shape(count, q_width),
            shape(1, HD, dtype=F32),
            shape(count, 2 * kv_width, dtype=F32),
        ]
        + [shape(count, 2 * kv_width)] * (blocks - 1),
        2 * count * width * q_width,
        "middle",
        after=[gate_low],
    )
    kv_sums = [grad_kv] + [
        lax.ppermute(sent, "ctx", [(i, i ^ (s + 1)) for i in range(blocks)])
        for s, sent in enumerate(grad_kv_sent)
    ]
    output_part = matmul_tn(mixed_rows, grad_resid_low).astype(BF)
    if has_pair():
        half = q_width // 2
        keep = lax.dynamic_slice_in_dim(output_part, core * half, half, 0)
        send = lax.dynamic_slice_in_dim(output_part, (1 - core) * half, half, 0)
        output_part = (keep.astype(F32) + swap(send, "dp", 1).astype(F32)).astype(BF)
    half = output_part.shape[0] // 2
    output_parts = [output_part[:half], output_part[half:]]
    bits = [mask for mask in masks if mask and mask & (mask - 1) == 0]

    def summed(parts, bit_of, earlier=(), later=()):
        received = [
            send_plane(order_after(part, *earlier), bit) for part, bit in zip(parts, bit_of)
        ]
        return [
            (part.astype(F32) + order_after(other, *later).astype(F32)).astype(BF)
            for part, other in zip(parts, received)
        ]

    grad_low, grad_key_gain = kernel_call(
        functools.partial(key_backward_body, len(kv_sums)),
        ids,
        [*kv_sums, key_raw, gain_k, cosine, sine, grad_query_low],
        [shape(count, q_width + 2 * kv_width), shape(1, HD, dtype=F32)],
        40 * count * kv_width,
        "key_backward",
        after=[output_part],
    )
    all_grad_low = plane_all(grad_low)
    first_parts = output_parts

    grad_one_pieces = kernel_call(
        functools.partial(first_grad_body, tensor),
        ids,
        [
            *x_pieces,
            inverse_one,
            gain_one,
            grad_query_gain,
            grad_key_gain,
            grad_low,
            query_weight,
            key_weight,
            value_weight,
        ],
        [shape(count + EXTRA, shard)] * tensor,
        2 * count * width * (q_width + 2 * kv_width),
        "first_grad",
    )
    outputs = (resid_part.astype(F32) + order_after(feed, grad_one_pieces[0]).astype(F32)).astype(BF)
    grad_gate_w, grad_up_w, grad_down_w = assemble(ids, lows, block, held, [outputs])

    grad_one = first_half(grad_one_pieces, "tensor", grad_gate_w)
    grad_query_w, grad_key_w, grad_value_w = projection_weights(
        ids, [all_normed_one], [all_grad_low], q_width, kv_width, [grad_gate_w, *grad_one.values()]
    )

    grad_one = second_half(grad_one, "tensor")
    grad_one_part = grad_one[:count]
    small = grad_one[count + 1 : count + 1 + (count + 2 * HD) // shard].reshape(-1)
    row_total_one = small[:count, None]
    feed_part_sums = lax.dynamic_slice_in_dim(feed_sums[0], column, shard)
    small = jnp.concatenate([grad_one[count], feed_part_sums, small[count:]])
    if has_pair():
        small = small + swap(small, "dp", 1)
    unit_one_part = inputs.astype(F32) * inverse_one
    grad_inputs = (
        grad_resid_part
        + inverse_one * (gain_one_part * grad_one_part)
        - unit_one_part * (inverse_one / width) * row_total_one
    )

    output_parts = summed(first_parts, (bits[0], bits[-1]), (), [grad_gate_w])
    for i in range(1, len(bits)):
        output_parts = summed(output_parts, (bits[i], bits[-1 - i]), [grad_gate_w], [grad_query_w])
    small = order_after(small, grad_query_w)
    for bit in bits:
        small = small + send_plane(small, bit)
    grad_attention_gain = small[:shard]
    grad_feed_gain = small[shard : 2 * shard]
    grad_query_gain = small[2 * shard : 2 * shard + HD]
    grad_key_gain = small[2 * shard + HD :]
    if has_pair():
        others = [swap(part, "dp", 1) for part in output_parts]
        grad_output_w = jnp.where(
            core == 0,
            jnp.concatenate(output_parts + others, axis=0),
            jnp.concatenate(others + output_parts, axis=0),
        )
    else:
        grad_output_w = jnp.concatenate(output_parts, axis=0)
    grad_output_w = grad_output_w.astype(F32)

    return (
        outputs,
        grad_inputs,
        grad_attention_gain,
        grad_query_w,
        grad_key_w,
        grad_value_w,
        grad_query_gain,
        grad_key_gain,
        grad_output_w,
        grad_feed_gain,
        grad_gate_w,
        grad_up_w,
        grad_down_w,
    )


def solution(mesh):
    in_specs = (
        P(("dp", "ctx"), "tensor"),
        P(("dp", "ctx"), None),
        P("dp", None),
        P("dp", "ctx"),
        P(),
        P(None, "tensor"),
        P(None, "tensor"),
        P(None, "tensor"),
        P(),
        P(),
        P("tensor", None),
        P(),
        P(None, "tensor"),
        P(None, "tensor"),
        P("tensor", None),
    )
    out_specs = (
        P(("dp", "ctx"), "tensor"),
        P(("dp", "ctx"), "tensor"),
        P("tensor"),
        P(None, "tensor"),
        P(None, "tensor"),
        P(None, "tensor"),
        P(),
        P(),
        P("tensor", None),
        P("tensor"),
        P(None, "tensor"),
        P(None, "tensor"),
        P("tensor", None),
    )
    return jax.shard_map(
        per_device, mesh=mesh, in_specs=in_specs, out_specs=out_specs, check_vma=False
    )
```

```python
import functools

import jax
import jax.numpy as jnp
from jax import lax
from jax.experimental import pallas as pl
from jax.experimental.pallas import tpu as pltpu
from jax.sharding import PartitionSpec as P

HD = 128
EPS = 1e-06
THETA = 1000000.0
NEG = -1e30
BF = jnp.bfloat16
F32 = jnp.float32
MIB = 1024 * 1024
VMEM_LIMIT = 63 * MIB + 900 * 1024
EXTRA = 16
SCALE = 1


def swap(value, axis, bit):
    size = lax.axis_size(axis)
    return lax.ppermute(value, axis, [(i, i ^ bit) for i in range(size)])


def bits_of(size):
    out = []
    bit = 1
    while bit < size:
        out.append(bit)
        bit *= 2
    return out


def gather_pieces(value, axis):
    pieces = {0: value}
    for bit in reversed(bits_of(lax.axis_size(axis))):
        for s in list(pieces):
            pieces[s | bit] = swap(pieces[s], axis, bit)
    return [pieces[s] for s in range(len(pieces))]


def send_pieces(pieces, axis):
    size = lax.axis_size(axis)
    return [
        lax.ppermute(pieces[s], axis, [(i, i ^ s) for i in range(size)])
        for s in sorted(range(1, size), key=lambda s: -s)
    ]


def send_all(value, axis):
    size = lax.axis_size(axis)
    pieces = {0: value}
    for s in range(size - 1, 0, -1):
        pieces[s] = lax.ppermute(value, axis, [(i, i ^ s) for i in range(size)])
    return [pieces[s] for s in range(size)]


def first_half(pieces, axis, *later):
    pieces = dict(enumerate(pieces))
    for s in [s for s in sorted(pieces, reverse=True) if not s & 1]:
        other = order_after(swap(pieces.pop(s | 1), axis, 1), *later)
        pieces[s] = (pieces[s].astype(F32) + other.astype(F32)).astype(BF if s else F32)
    return pieces


def second_half(pieces, axis, later=()):
    pieces = dict(pieces)
    for bit in bits_of(lax.axis_size(axis))[1:]:
        for s in [s for s in sorted(pieces, reverse=True) if not s & bit]:
            other = order_after(swap(pieces.pop(s | bit), axis, bit), *later)
            pieces[s] = (pieces[s].astype(F32) + other.astype(F32)).astype(BF if s else F32)
    return pieces[0]


def total_of(own, others):
    total = own.astype(F32)
    for other in others:
        total = total + other.astype(F32)
    return total


def far_masks():
    size = lax.axis_size("ctx")
    bits = [size * bit for bit in bits_of(lax.axis_size("dp")) if bit > 1] + bits_of(size)
    masks = [0]
    for bit in bits:
        masks = masks + [mask | bit for mask in masks]
    return masks


def send_plane(value, mask):
    if mask == 0:
        return value
    size = lax.axis_size("dp") * lax.axis_size("ctx")
    return lax.ppermute(value, ("dp", "ctx"), [(i, i ^ mask) for i in range(size)])


def pass_on(parts, masks, highest, *earlier):
    parts = list(parts)
    for mask in masks[len(parts) :]:
        bit = 1 << (mask.bit_length() - 1) if highest else mask & -mask
        parts.append(send_plane(order_after(parts[masks.index(mask ^ bit)], *earlier), bit))
    return parts


def plane_all(value):
    return lax.all_gather(value, ("dp", "ctx"), axis=0, tiled=True)


def sum_tensor(value):
    return lax.psum_scatter(value, "tensor", scatter_dimension=1, tiled=True)


def has_pair():
    return lax.axis_size("dp") > 1


def partners(parts, *earlier):
    if not has_pair():
        return []
    return [swap(order_after(part, *earlier), "dp", 1) for part in parts]


def order_after(value, *earlier):
    return lax.optimization_barrier((value, *earlier))[0] if earlier else value


def pieces_of(order, index, shard):
    return pl.multiple_of((index ^ order) * shard, shard)


def dot(left, right):
    return jnp.dot(left, right, preferred_element_type=F32)


def dot_nt(left, right):
    return lax.dot_general(left, right, (((1,), (1,)), ((), ())), preferred_element_type=F32)


def dot_tn(left, right):
    return lax.dot_general(left, right, (((0,), (0,)), ((), ())), preferred_element_type=F32)


def shape(*dims, dtype=BF):
    return jax.ShapeDtypeStruct(dims, dtype)


def size_of(arrays):
    return sum(a.size * a.dtype.itemsize for a in arrays)


def cost(flops, moved):
    return pl.CostEstimate(
        flops=int(flops) // SCALE, bytes_accessed=int(moved) // SCALE, transcendentals=0
    )


class Loads:
    def __init__(self, copies, buffers):
        self.copies = dict(enumerate(copies))
        self.buffers = buffers

    def __getitem__(self, index):
        if isinstance(index, slice):
            return [self[i] for i in range(*index.indices(len(self.buffers)))]
        if index in self.copies:
            self.copies.pop(index).wait()
        return self.buffers[index]

    def finish(self):
        for index in list(self.copies):
            self[index]


ANY = pl.BlockSpec(memory_space=pl.ANY)
SMEM = pl.BlockSpec(memory_space=pltpu.SMEM)


def kernel_call(body, ids, arrays, outs, flops, name, after=(), scratch=()):
    count, extra, results = len(arrays), len(after), len(outs)

    def run(ids, *refs):
        sources = refs[:count]
        out_refs = refs[count + extra : count + extra + results]
        buffers = refs[count + extra + results : 2 * count + extra + results]
        sems = refs[2 * count + extra + results]
        copies = [
            pltpu.make_async_copy(source, buffer, sems.at[i])
            for i, (source, buffer) in enumerate(zip(sources, buffers))
        ]
        for copy in copies:
            copy.start()
        loads = Loads(copies, buffers)
        body(ids, loads, *out_refs, *refs[2 * count + extra + results + 1 :])
        loads.finish()

    moved = size_of(arrays) + size_of(outs)
    return pl.pallas_call(
        run,
        out_shape=tuple(outs),
        in_specs=[SMEM] + [ANY] * (count + extra),
        out_specs=tuple(pl.BlockSpec(memory_space=pltpu.VMEM) for _ in outs),
        scratch_shapes=[pltpu.VMEM(a.shape, a.dtype) for a in arrays]
        + [pltpu.SemaphoreType.DMA((count,))]
        + [pltpu.VMEM(a.shape, a.dtype) for a in scratch],
        compiler_params=pltpu.CompilerParams(vmem_limit_bytes=VMEM_LIMIT),
        cost_estimate=cost(flops, moved),
        name=name,
    )(ids, *arrays, *after)


def turn(value):
    return pltpu.roll(value, HD // 2, 1)


def head_forward(raw, gain, cosine, sine):
    scale = lax.rsqrt(jnp.mean(raw * raw, axis=-1, keepdims=True) + EPS)
    normed = raw * scale * gain
    return normed * cosine + turn(normed) * sine


def head_backward(grad, raw, gain, cosine, sine):
    scale = lax.rsqrt(jnp.mean(raw * raw, axis=-1, keepdims=True) + EPS)
    unit = raw * scale
    grad_normed = grad * cosine + turn(grad * sine)
    grad_gain = jnp.sum(grad_normed * unit, axis=0, keepdims=True)
    inner = grad_normed * gain
    grad_raw = scale * (inner - unit * jnp.mean(inner * unit, axis=-1, keepdims=True))
    return grad_raw, grad_gain


def key_value_body(count, ids, loads, normed_ref, kv, raw_ref, inverse_ref):
    pieces = loads[:count]
    rows, shard = pieces[0].shape
    squares = 0.0
    for piece in pieces:
        x = piece[...].astype(F32)
        squares += jnp.sum(x * x, axis=-1, keepdims=True)
    inverse = lax.rsqrt(squares * (1.0 / (shard * count)) + EPS)
    inverse_ref[...] = inverse
    gain, key_gain, cosine, sine, wk, wv = loads[count : count + 6]
    kv_width = wk.shape[1]
    key_raw = jnp.zeros((rows, kv_width), F32)
    values = jnp.zeros((rows, kv_width), F32)
    for s in range(count):
        off = pieces_of(s, ids[0], shard)
        normed = (pieces[s][...].astype(F32) * inverse * gain[:, pl.ds(off, shard)]).astype(BF)
        normed_ref[:, pl.ds(off, shard)] = normed
        key_raw += dot(normed, wk[pl.ds(off, shard), :])
        values += dot(normed, wv[pl.ds(off, shard), :])
    raw_ref[...] = key_raw
    for h in range(kv_width // HD):
        cols = slice(h * HD, (h + 1) * HD)
        out = head_forward(key_raw[:, cols], key_gain[...], cosine[...], sine[...])
        kv[:, cols] = out.astype(BF)
    kv[:, kv_width:] = values.astype(BF)


def query_body(ids, loads, q_ref, raw_ref):
    normed, wq, query_gain, cosine, sine = loads[:5]
    raw = dot(normed[...], wq[...])
    raw_ref[...] = raw
    for h in range(wq.shape[1] // HD):
        cols = slice(h * HD, (h + 1) * HD)
        out = head_forward(raw[:, cols], query_gain[...], cosine[...], sine[...])
        q_ref[:, cols] = out.astype(BF)


def head_probs(ids, q, blocks, head, group, row_segment, key_segments):
    rows = q.shape[0]
    kv = head // group
    cols = slice(head * HD, (head + 1) * HD)
    row_index = ids[1] * rows + lax.broadcasted_iota(jnp.int32, (rows, rows), 0)
    parts = []
    for s, block in enumerate(blocks):
        scores = dot_nt(q[:, cols], block[:, kv * HD : (kv + 1) * HD]) * HD ** (-0.5)
        key_index = (ids[1] ^ s) * rows + lax.broadcasted_iota(jnp.int32, (rows, rows), 1)
        allowed = (row_segment[...] == key_segments[s][...]) & (key_index <= row_index)
        parts.append(jnp.where(allowed, scores, NEG))
    top = parts[0].max(axis=-1, keepdims=True)
    for part in parts[1:]:
        top = jnp.maximum(top, part.max(axis=-1, keepdims=True))
    parts = [jnp.exp(part - top) for part in parts]
    total = sum(jnp.sum(part, axis=-1, keepdims=True) for part in parts)
    share = 1.0 / total
    return [part * share for part in parts]


def attention_body(count, group, blocks, ids, loads, mixed_ref, *outs):
    q, row_segment = loads[:2]
    kvs = loads[2 : 2 + blocks]
    key_segments = loads[2 + blocks : 2 + 2 * blocks]
    kv_width = kvs[0].shape[1] // 2
    for h in range(q.shape[1] // HD):
        probs = head_probs(ids, q, kvs, h, group, row_segment, key_segments)
        start = kv_width + (h // group) * HD
        mixed = sum(
            dot(p.astype(BF), block[:, start : start + HD]) for p, block in zip(probs, kvs)
        )
        mixed_ref[:, h * HD : (h + 1) * HD] = mixed.astype(BF)
    wo = loads[2 + 2 * blocks]
    shard = wo.shape[1] // count
    for s in range(count):
        off = pieces_of(s, ids[0], shard)
        outs[s][...] = dot(mixed_ref[...], wo[:, pl.ds(off, shard)]).astype(BF)


def second_norm_body(count, ids, loads, normed_ref, resid_ref, inverse_ref):
    pieces = loads[:count]
    gain = loads[count]
    rows, shard = pieces[0].shape
    squares = 0.0
    for piece in pieces:
        x = piece[...].astype(F32)
        squares += jnp.sum(x * x, axis=-1, keepdims=True)
    inverse = lax.rsqrt(squares * (1.0 / (shard * count)) + EPS)
    inverse_ref[...] = inverse
    for s in range(count):
        off = pieces_of(s, ids[0], shard)
        cols = pl.ds(off, shard)
        x = pieces[s][...]
        resid_ref[:, cols] = x
        normed_ref[:, cols] = (x.astype(F32) * inverse * gain[:, cols]).astype(BF)


def gated_terms(gate, up, grad_hidden):
    sigmoid = jax.nn.sigmoid(gate)
    silu = gate * sigmoid
    grad_gate = grad_hidden * up * sigmoid * (1.0 + gate * (1.0 - sigmoid))
    return silu * up, grad_gate, grad_hidden * silu


def feed_forward_body(tile, extra, ids, normed_hbm, cot_hbm, wg_hbm, wu_hbm, wd_hbm, *refs):
    refs = refs[extra:]
    grad_out, feed_out, normed, cot, wg, wu, wd, total, feed, sems = refs
    units = wg.shape[1]
    tiles = units // tile
    first = [
        pltpu.make_async_copy(normed_hbm, normed, sems.at[3 * tiles]),
        pltpu.make_async_copy(cot_hbm, cot, sems.at[3 * tiles + 1]),
    ]

    def weights(t):
        cols = pl.ds(pl.multiple_of(t * tile, tile), tile)
        return [
            pltpu.make_async_copy(wg_hbm.at[:, cols], wg.at[:, cols], sems.at[t]),
            pltpu.make_async_copy(wu_hbm.at[:, cols], wu.at[:, cols], sems.at[tiles + t]),
            pltpu.make_async_copy(wd_hbm.at[cols, :], wd.at[cols, :], sems.at[2 * tiles + t]),
        ]

    for copy in first:
        copy.start()
    for t in range(tiles):
        for copy in weights(t):
            copy.start()
    total[...] = jnp.zeros_like(total)
    feed[...] = jnp.zeros_like(feed)
    for copy in first:
        copy.wait()

    def step(t, carry):
        cols = pl.ds(pl.multiple_of(t * tile, tile), tile)
        gate_copy, up_copy, down_copy = weights(t)
        gate_copy.wait()
        gate = dot(normed[...], wg[:, cols])
        up_copy.wait()
        up = dot(normed[...], wu[:, cols])
        down_copy.wait()
        grad_hidden = dot_nt(cot[...], wd[cols, :])
        hidden, grad_gate, grad_up = gated_terms(gate, up, grad_hidden)
        total[...] += dot_nt(grad_gate.astype(BF), wg[:, cols]) + dot_nt(
            grad_up.astype(BF), wu[:, cols]
        )
        feed[...] += dot(hidden.astype(BF), wd[cols, :])
        return carry

    lax.fori_loop(0, tiles, step, 0)
    grad_out[...] = total[...].astype(BF)
    feed_out[...] = feed[...].astype(BF)


def feed_forward(ids, normed, cot, wg, wu, wd, after=()):
    rows, width = cot.shape
    units = wg.shape[1]
    tile = max(t for t in (512, 384, 256, 128) if units % t == 0)
    arrays = [normed, cot, wg, wu, wd]
    outs = [shape(rows, width)] * 2
    moved = size_of(arrays) + size_of(outs)
    return pl.pallas_call(
        functools.partial(feed_forward_body, tile, len(after)),
        out_shape=outs,
        in_specs=[SMEM] + [ANY] * (5 + len(after)),
        out_specs=[pl.BlockSpec(memory_space=pltpu.VMEM) for _ in outs],
        scratch_shapes=[pltpu.VMEM(a.shape, a.dtype) for a in arrays]
        + [
            pltpu.VMEM((rows, width), F32),
            pltpu.VMEM((rows, width), F32),
            pltpu.SemaphoreType.DMA((3 * (units // tile) + 2,)),
        ],
        compiler_params=pltpu.CompilerParams(
            vmem_limit_bytes=VMEM_LIMIT
        ),
        cost_estimate=cost(12 * rows * width * units, moved),
        name="feed_forward",
    )(ids, *arrays, *after)


def middle_body(count, group, blocks, ids, loads, own_ref, low_ref, sums_ref, *outs):
    grads, resid, inverse_ref, gain, cot = loads[:5]
    rows, width = grads.shape
    shard = width // count
    inverse = inverse_ref[...]
    row_total = 0.0
    for s in range(count):
        cols = pl.ds(pieces_of(s, ids[0], shard), shard)
        product = grads[:, cols].astype(F32) * (resid[:, cols].astype(F32) * inverse)
        sums_ref[:, cols] = jnp.sum(product, axis=0, keepdims=True)
        row_total += jnp.sum(product * gain[:, cols], axis=-1, keepdims=True)
    scale = row_total * inverse * (1.0 / width)
    wo = loads[5]
    mixed = jnp.zeros((rows, wo.shape[0]), F32)
    for s in range(count):
        cols = pl.ds(pieces_of(s, ids[0], shard), shard)
        unit = resid[:, cols].astype(F32) * inverse
        grad = (
            cot[:, cols].astype(F32)
            + inverse * (gain[:, cols] * grads[:, cols].astype(F32))
            - unit * scale
        )
        if s == 0:
            own_ref[...] = grad
        low = grad.astype(BF)
        low_ref[:, cols] = low
        mixed += dot_nt(low, wo[:, cols])
    attention_backward(group, blocks, ids, loads[6:], mixed.astype(BF), *outs)


def attention_backward(group, blocks, ids, loads, grads, low_ref, gain_ref, own_ref, *others):
    q, row_segment = loads[:2]
    kvs = loads[2 : 2 + blocks]
    key_segments = loads[2 + blocks : 2 + 2 * blocks]
    raw, query_gain, cosine, sine = loads[2 + 2 * blocks : 6 + 2 * blocks]
    kv_width = kvs[0].shape[1] // 2
    factor = HD ** (-0.5)
    gain_total = jnp.zeros((1, HD), F32)
    outs = [own_ref] + list(others)
    for kv in range(kv_width // HD):
        key_cols = slice(kv * HD, (kv + 1) * HD)
        value_cols = slice(kv_width + kv * HD, kv_width + (kv + 1) * HD)
        key_sums = [0.0] * blocks
        value_sums = [0.0] * blocks
        for h in range(kv * group, (kv + 1) * group):
            cols = slice(h * HD, (h + 1) * HD)
            probs = head_probs(ids, q, kvs, h, group, row_segment, key_segments)
            grad = grads[:, cols]
            grad_probs = [dot_nt(grad, block[:, value_cols]) for block in kvs]
            delta = sum(jnp.sum(p * g, axis=-1, keepdims=True) for p, g in zip(probs, grad_probs))
            scores = [(p * (g - delta)).astype(BF) for p, g in zip(probs, grad_probs)]
            grad_query = sum(dot(g, block[:, key_cols]) for g, block in zip(scores, kvs)) * factor
            for s in range(blocks):
                key_sums[s] += dot_tn(scores[s], q[:, cols])
                value_sums[s] += dot_tn(probs[s].astype(BF), grad)
            grad_raw, grad_gain = head_backward(
                grad_query, raw[:, cols], query_gain[...], cosine[...], sine[...]
            )
            low_ref[:, cols] = grad_raw.astype(BF)
            gain_total += grad_gain
        for s in range(blocks):
            outs[s][:, key_cols] = (key_sums[s] * factor).astype(outs[s].dtype)
            outs[s][:, value_cols] = value_sums[s].astype(outs[s].dtype)
    gain_ref[...] = gain_total


def key_backward_body(blocks, ids, loads, low_ref, gain_ref):
    sums = loads[:blocks]
    raw, key_gain, cosine, sine, query_low = loads[blocks : blocks + 5]
    q_width = query_low.shape[1]
    kv_width = raw.shape[1]
    low_ref[:, :q_width] = query_low[...]
    total = sums[0][...]
    for other in sums[1:]:
        total = total + other[...].astype(F32)
    gain_total = jnp.zeros((1, HD), F32)
    for h in range(kv_width // HD):
        cols = slice(h * HD, (h + 1) * HD)
        grad_raw, grad_gain = head_backward(
            total[:, cols], raw[:, cols], key_gain[...], cosine[...], sine[...]
        )
        low_ref[:, q_width + h * HD : q_width + (h + 1) * HD] = grad_raw.astype(BF)
        gain_total += grad_gain
    low_ref[:, q_width + kv_width :] = total[:, kv_width:].astype(BF)
    gain_ref[...] = gain_total


def first_grad_body(count, ids, loads, *outs):
    pieces = loads[:count]
    inverse_ref, gain, query_sums, key_sums, grads, wq, wk, wv = loads[count : count + 8]
    rows, shard = pieces[0].shape
    q_width, kv_width = wq.shape[1], wk.shape[1]
    inverse = inverse_ref[...]
    row_total = jnp.zeros((rows, 1), F32)
    for s in range(count):
        cols = pl.ds(pieces_of(s, ids[0], shard), shard)
        grad = (
            dot_nt(grads[:, :q_width], wq[cols, :])
            + dot_nt(grads[:, q_width : q_width + kv_width], wk[cols, :])
            + dot_nt(grads[:, q_width + kv_width :], wv[cols, :])
        )
        product = grad * (pieces[s][...].astype(F32) * inverse)
        outs[s][:rows, :] = grad.astype(BF)
        outs[s][rows:, :] = jnp.zeros((EXTRA, shard), BF)
        outs[s][rows : rows + 1, :] = jnp.sum(product, axis=0, keepdims=True).astype(BF)
        row_total += jnp.sum(product * gain[:, cols], axis=-1, keepdims=True)
    turned = jnp.broadcast_to(row_total, (rows, HD)).T[:1]
    small = jnp.concatenate([turned, query_sums[...], key_sums[...]], axis=1).astype(BF)
    for s in range(count):
        for r in range(small.shape[1] // shard):
            row = rows + 1 + r
            outs[s][row : row + 1, :] = small[:, r * shard : (r + 1) * shard]


def feed_weight_body(parts, extra, last, block, ids, *refs):
    rows_hbm, cots_hbm = refs[:parts], refs[parts : 2 * parts]
    wg_hbm, wu_hbm, wd_hbm = refs[2 * parts : 2 * parts + 3]
    refs = refs[2 * parts + 3 + extra :]
    dwg, dwu, dwd = refs[:3]
    lows = refs[3:6] if last else ()
    refs = refs[6:] if last else refs[3:]
    rows, cots, hid, gates, ups, wg, wu, wd, gate_out, up_out, down_out = refs[:11]
    refs = refs[11:]
    if last:
        gate_held, up_held, down_held, gate_cut, up_cut, down_cut = refs[:6]
        refs = refs[6:]
    row_sems, cot_sems, weight_sems, held_sems, out_sems = refs
    width = rows.shape[1]
    size = rows_hbm[0].shape[0]
    group = 2 if parts % 2 == 0 else 1
    chunk = group * size
    steps = wg_hbm.shape[1] // block // 2
    tile = width // 2

    def mine(b):
        return pl.ds(pl.multiple_of((ids[2] * steps + b) * block, block), block)

    def weights(b, slot):
        return [
            pltpu.make_async_copy(wg_hbm.at[:, mine(b)], wg.at[slot], weight_sems.at[slot, 0]),
            pltpu.make_async_copy(wu_hbm.at[:, mine(b)], wu.at[slot], weight_sems.at[slot, 1]),
            pltpu.make_async_copy(wd_hbm.at[mine(b), :], wd.at[slot], weight_sems.at[slot, 2]),
        ]

    def tile_at(t):
        return pl.ds(pl.multiple_of(t * tile, tile), tile)

    def held(b, t):
        at = tile_at(t)
        pairs = [
            (dwg.at[at, mine(b)], gate_held.at[at, :]),
            (dwu.at[at, mine(b)], up_held.at[at, :]),
            (dwd.at[mine(b), at], down_held.at[:, at]),
        ]
        return [pltpu.make_async_copy(a, c, held_sems.at[t, i]) for i, (a, c) in enumerate(pairs)]

    def results(b, t):
        at = tile_at(t)
        low = pl.ds(pl.multiple_of(b * block, block), block)
        pairs = [
            (gate_out.at[at, :], dwg.at[at, mine(b)]),
            (up_out.at[at, :], dwu.at[at, mine(b)]),
            (down_out.at[:, at], dwd.at[mine(b), at]),
        ]
        if last:
            pairs += [
                (gate_cut.at[at, :], lows[0].at[at, low]),
                (up_cut.at[at, :], lows[1].at[at, low]),
                (down_cut.at[:, at], lows[2].at[low, at]),
            ]
        return [pltpu.make_async_copy(a, c, out_sems.at[t, i]) for i, (a, c) in enumerate(pairs)]

    for copy in weights(0, 0):
        copy.start()
    for i in range(parts):
        place = pl.ds(i * size, size)
        pltpu.make_async_copy(rows_hbm[i], rows.at[place, :], row_sems.at[i // group]).start()
        pltpu.make_async_copy(cots_hbm[i], cots.at[place, :], cot_sems.at[i // group]).start()

    def one_block(b, carry):
        slot = lax.rem(b, 2)
        for copy in weights(b, slot):
            copy.wait()
        if last:
            for t in range(2):
                for copy in held(b, t):
                    copy.start()

        @pl.when(b + 1 < steps)
        def _():
            for copy in weights(b + 1, 1 - slot):
                copy.start()

        def recompute(c, carry):
            place = pl.ds(pl.multiple_of(c * chunk, chunk), chunk)

            @pl.when(b == 0)
            def _():
                pltpu.make_async_copy(rows.at[place, :], rows.at[place, :], row_sems.at[c]).wait()
                pltpu.make_async_copy(cots.at[place, :], cots.at[place, :], cot_sems.at[c]).wait()

            own = rows[place, :]
            gate = dot(own, wg[slot])
            up = dot(own, wu[slot])
            grad_hidden = dot_nt(cots[place, :], wd[slot])
            hidden, grad_gate, grad_up = gated_terms(gate, up, grad_hidden)
            hid[place, :] = hidden.astype(BF)
            gates[place, :] = grad_gate.astype(BF)
            ups[place, :] = grad_up.astype(BF)
            return carry

        lax.fori_loop(0, parts // group, recompute, 0)

        def products(t, carry):
            @pl.when(b > 0)
            def _():
                for copy in results(b, t):
                    copy.wait()

            cols = tile_at(t)
            down = dot_tn(hid[...], cots[:, cols])
            gate = dot_tn(rows[:, cols], gates[...])
            up = dot_tn(rows[:, cols], ups[...])
            if last:
                for copy in held(b, t):
                    copy.wait()
                down = (down + down_held[:, cols]).astype(BF)
                gate = (gate + gate_held[cols, :]).astype(BF)
                up = (up + up_held[cols, :]).astype(BF)
                down_cut[:, cols] = down
                gate_cut[cols, :] = gate
                up_cut[cols, :] = up
            down_out[:, cols] = down.astype(F32)
            gate_out[cols, :] = gate.astype(F32)
            up_out[cols, :] = up.astype(F32)
            for copy in results(b, t):
                copy.start()
            return carry

        lax.fori_loop(0, 2, products, 0)
        return carry

    lax.fori_loop(0, steps, one_block, 0)
    for t in range(2):
        for copy in results(0, t):
            copy.wait()


def feed_weights(ids, rows, cots, wg, wu, wd, block, held, last, after=()):
    parts = len(rows)
    size, width = rows[0].shape
    tokens = size * parts
    units = wg.shape[1]
    held = list(held or ())
    outs = [
        shape(width, units, dtype=F32),
        shape(width, units, dtype=F32),
        shape(units, width, dtype=F32),
    ]
    tiles = [
        shape(width, block, dtype=F32),
        shape(width, block, dtype=F32),
        shape(block, width, dtype=F32),
    ]
    scratch = [
        shape(tokens, width),
        shape(tokens, width),
        shape(tokens, block),
        shape(tokens, block),
        shape(tokens, block),
        shape(2, width, block),
        shape(2, width, block),
        shape(2, block, width),
        *tiles,
    ]
    if last:
        outs += [shape(width, units // 2), shape(width, units // 2), shape(units // 2, width)]
        scratch += [*tiles, shape(width, block), shape(width, block), shape(block, width)]
    if not held and last:
        held = [jnp.zeros(o.shape, F32) for o in outs[:3]]
    extra = len(held) + len(after)
    return pl.pallas_call(
        functools.partial(feed_weight_body, parts, extra, last, block),
        out_shape=outs,
        in_specs=[SMEM] + [ANY] * (2 * parts + 3 + extra),
        out_specs=[ANY] * len(outs),
        scratch_shapes=[pltpu.VMEM(a.shape, a.dtype) for a in scratch]
        + [
            pltpu.SemaphoreType.DMA((parts,)),
            pltpu.SemaphoreType.DMA((parts,)),
            pltpu.SemaphoreType.DMA((2, 3)),
            pltpu.SemaphoreType.DMA((2, 3)),
            pltpu.SemaphoreType.DMA((2, 6)),
        ],
        input_output_aliases={4 + 2 * parts + i: i for i in range(len(held))},
        compiler_params=pltpu.CompilerParams(vmem_limit_bytes=VMEM_LIMIT),
        cost_estimate=cost(6 * tokens * width * units, 4 * tokens * width),
        name="feed_weights",
    )(ids, *rows, *cots, wg, wu, wd, *held, *after)


def assemble_body(extra, ids, gate_low, up_low, down_low, *refs):
    dwg, dwu, dwd = refs[-3:]
    dwg[...] = gate_low[...].astype(F32)
    dwu[...] = up_low[...].astype(F32)
    dwd[...] = down_low[...].astype(F32)


def assemble(ids, lows, block, held, after=()):
    width, units = held[0].shape
    steps = units // block // 2
    tile = width // 2
    cols_in = pl.BlockSpec((tile, block), lambda b, i, ids: (i, b))
    rows_in = pl.BlockSpec((block, tile), lambda b, i, ids: (b, i))
    cols_out = pl.BlockSpec((tile, block), lambda b, i, ids: (i, (1 - ids[2]) * steps + b))
    rows_out = pl.BlockSpec((block, tile), lambda b, i, ids: ((1 - ids[2]) * steps + b, i))
    return pl.pallas_call(
        functools.partial(assemble_body, len(after)),
        out_shape=[shape(*a.shape, dtype=F32) for a in held],
        grid_spec=pltpu.PrefetchScalarGridSpec(
            num_scalar_prefetch=1,
            grid=(steps, 2),
            in_specs=[cols_in, cols_in, rows_in] + [ANY] * (3 + len(after)),
            out_specs=[cols_out, cols_out, rows_out],
        ),
        input_output_aliases={4: 0, 5: 1, 6: 2},
        compiler_params=pltpu.CompilerParams(vmem_limit_bytes=VMEM_LIMIT),
        cost_estimate=cost(0, 9 * width * units),
        name="assemble",
    )(ids, *lows, *held, *after)


def projection_body(parts, tile, extra, ids, *refs):
    rows_hbm, grads_hbm = refs[:parts], refs[parts : 2 * parts]
    refs = refs[2 * parts + extra :]
    outs_hbm = refs[:3]
    rows, grads, *outs, row_sems, grad_sem, out_sems = refs[3:]
    width = rows.shape[1]
    tiles = width // tile
    at = 0
    for i in range(parts):
        place = pl.ds(at, grads_hbm[i].shape[0])
        pltpu.make_async_copy(grads_hbm[i], grads.at[place, :], grad_sem).start()
        at += grads_hbm[i].shape[0]
    for t in range(tiles):
        cols = pl.ds(t * tile, tile)
        at = 0
        for i in range(parts):
            place = pl.ds(at, rows_hbm[i].shape[0])
            pltpu.make_async_copy(
                rows_hbm[i].at[:, cols], rows.at[place, cols], row_sems.at[t]
            ).start()
            at += rows_hbm[i].shape[0]
    pltpu.make_async_copy(grads, grads, grad_sem).wait()
    q_width, kv_width = outs[0].shape[1], outs[1].shape[1]

    def copies(t):
        cols = pl.ds(pl.multiple_of(t * tile, tile), tile)
        return [
            pltpu.make_async_copy(a.at[cols, :], b.at[cols, :], out_sems.at[t, i])
            for i, (a, b) in enumerate(zip(outs, outs_hbm))
        ]

    def products(t, carry):
        cols = pl.ds(pl.multiple_of(t * tile, tile), tile)
        pltpu.make_async_copy(rows.at[:, cols], rows.at[:, cols], row_sems.at[t]).wait()
        total = dot_tn(rows[:, cols], grads[...])
        outs[0][cols, :] = total[:, :q_width]
        outs[1][cols, :] = total[:, q_width : q_width + kv_width]
        outs[2][cols, :] = total[:, q_width + kv_width :]
        for copy in copies(t):
            copy.start()
        return carry

    lax.fori_loop(0, tiles, products, 0)

    def finish(t, carry):
        for copy in copies(t):
            copy.wait()
        return carry

    lax.fori_loop(0, tiles, finish, 0)


def projection_weights(ids, rows, grads, q_width, kv_width, after):
    parts = len(rows)
    width = rows[0].shape[1]
    tokens = sum(a.shape[0] for a in rows)
    tile = 512
    outs = [shape(width, w, dtype=F32) for w in (q_width, kv_width, kv_width)]
    scratch = [shape(tokens, width), shape(tokens, q_width + 2 * kv_width)] + outs
    return pl.pallas_call(
        functools.partial(projection_body, parts, tile, len(after)),
        out_shape=outs,
        in_specs=[SMEM] + [ANY] * (2 * parts + len(after)),
        out_specs=[ANY] * 3,
        scratch_shapes=[pltpu.VMEM(a.shape, a.dtype) for a in scratch]
        + [
            pltpu.SemaphoreType.DMA((width // tile,)),
            pltpu.SemaphoreType.DMA(()),
            pltpu.SemaphoreType.DMA((width // tile, 3)),
        ],
        compiler_params=pltpu.CompilerParams(
            vmem_limit_bytes=VMEM_LIMIT
        ),
        cost_estimate=cost(2 * tokens * width * (q_width + 2 * kv_width), 2 * tokens * width),
        name="projection_weights",
    )(ids, *rows, *grads, *after)


def matmul_tn(left, right):
    return lax.dot_general(left, right, (((0,), (0,)), ((), ())), preferred_element_type=F32)


def rope_tables(position_row):
    half = HD // 2
    freqs = jnp.exp(-(2.0 * jnp.arange(half, dtype=F32) / HD) * jnp.log(F32(THETA)))
    angles = position_row.astype(F32)[:, None] * freqs[None, :]
    cosine, sine = jnp.cos(angles), jnp.sin(angles)
    return jnp.concatenate([cosine, cosine], axis=1), jnp.concatenate([-sine, sine], axis=1)


def per_device(
    inputs,
    cotangent,
    segments,
    positions,
    attention_gain,
    query_weight,
    key_weight,
    value_weight,
    query_gain,
    key_gain,
    output_weight,
    feed_gain,
    gate_weight,
    up_weight,
    down_weight,
):
    count, shard = inputs.shape
    width = cotangent.shape[1]
    tensor = lax.axis_size("tensor")
    me = lax.axis_index("tensor")
    column = me * shard
    place = lax.axis_index("ctx")
    core = lax.axis_index("dp") % 2
    ids = jnp.stack([me, place, core, lax.axis_index("dp")]).astype(jnp.int32)
    q_width, kv_width = query_weight.shape[1], key_weight.shape[1]
    group = q_width // kv_width
    blocks = lax.axis_size("ctx")
    gain_one = attention_gain.astype(F32)[None]
    gain_two = feed_gain.astype(F32)[None]
    gain_q = query_gain.astype(F32)[None]
    gain_k = key_gain.astype(F32)[None]
    gain_one_part = lax.dynamic_slice_in_dim(gain_one, column, shard, 1)
    hidden_units = gate_weight.shape[1]
    block = 256 if (hidden_units // 2) % 256 == 0 else 128

    masks = far_masks()
    first_masks = len(masks) // 2 or 1
    x_pieces = gather_pieces(inputs, "tensor")
    cot_parts = [send_plane(cotangent, mask) for mask in masks[:first_masks + 1]]
    cosine, sine = rope_tables(positions[0])
    segment_row = segments[0]
    row_segment = lax.dynamic_slice_in_dim(segment_row, place * count, count)[:, None]
    key_segments = [
        lax.dynamic_slice_in_dim(segment_row, (place ^ s) * count, count)[None]
        for s in range(blocks)
    ]
    normed_one, kv_rows, key_raw, inverse_one = kernel_call(
        functools.partial(key_value_body, tensor),
        ids,
        [*x_pieces, gain_one, gain_k, cosine, sine, key_weight, value_weight],
        [
            shape(count, width),
            shape(count, 2 * kv_width),
            shape(count, kv_width, dtype=F32),
            shape(count, 1, dtype=F32),
        ],
        4 * count * width * kv_width,
        "key_value",
        after=[*cot_parts[1:], row_segment, *key_segments],
    )
    kv_pieces = gather_pieces(kv_rows, "ctx")
    all_normed_one = plane_all(normed_one)
    query_rows, query_raw = kernel_call(
        query_body,
        ids,
        [normed_one, query_weight, gain_q, cosine, sine],
        [shape(count, q_width), shape(count, q_width, dtype=F32)],
        2 * count * width * q_width,
        "query",
    )

    mixed_rows, *branch_pieces = kernel_call(
        functools.partial(attention_body, tensor, group, blocks),
        ids,
        [query_rows, row_segment, *kv_pieces, *key_segments, output_weight],
        [shape(count, q_width)] + [shape(count, shard)] * tensor,
        4 * count * count * blocks * q_width + 2 * count * width * q_width,
        "attention",
    )
    branch = second_half(first_half(branch_pieces, "tensor"), "tensor")
    resid_part = (inputs.astype(F32) + branch).astype(BF)
    resid_pieces = gather_pieces(resid_part, "tensor")
    cot_partners = partners(cot_parts[: first_masks + 1])

    normed_two, resid, inverse_two = kernel_call(
        functools.partial(second_norm_body, tensor),
        ids,
        [*resid_pieces, gain_two],
        [shape(count, width), shape(count, width), shape(count, 1, dtype=F32)],
        8 * count * width,
        "second_norm",
        after=cot_partners,
    )
    two_parts = [send_plane(normed_two, mask) for mask in masks[: first_masks + 1]]
    grad_two_part, feed_part = feed_forward(
        ids, normed_two, cotangent, gate_weight, up_weight, down_weight
    )
    feed_done = feed_part
    grad_two_part = sum_tensor(grad_two_part)
    two_parts = pass_on(two_parts, masks, True, feed_done)
    cot_parts = pass_on(cot_parts, masks, False, feed_done)
    groups = [slice(0, first_masks), slice(first_masks, None)] if len(masks) > 1 else [slice(0, None)]
    last = len(groups) - 1
    two_partners = partners(two_parts[:1]) + partners(two_parts[1 : first_masks + 1], feed_done)

    def weights_of(g, held, after):
        return feed_weights(
            ids,
            two_parts[groups[g]] + two_partners[groups[g]],
            cot_parts[groups[g]] + cot_partners[groups[g]],
            gate_weight,
            up_weight,
            down_weight,
            block,
            held,
            g == last,
            after,
        )

    held, done = None, [feed_done, *two_partners, all_normed_one]
    for g in range(last):
        held = weights_of(g, held, done)
        done = held[:1]
    two_partners += partners(two_parts[first_masks + 1 :], *done)
    cot_partners += partners(cot_parts[first_masks + 1 :], *done)
    grad_two = lax.all_gather(grad_two_part, "tensor", axis=1, tiled=True)
    *held, gate_low, up_low, down_low = weights_of(last, held, [grad_two_part])
    lows = [gate_low, up_low, down_low]
    feed = sum_tensor(order_after(feed_part, gate_low))
    lows = [swap(low, "dp", 1) for low in lows] if has_pair() else lows

    (
        grad_resid_part,
        grad_resid_low,
        feed_sums,
        grad_query_low,
        grad_query_gain,
        grad_kv,
        *grad_kv_sent,
    ) = kernel_call(
        functools.partial(middle_body, tensor, group, blocks),
        ids,
        [
            grad_two,
            resid,
            inverse_two,
            gain_two,
            cotangent,
            output_weight,
            query_rows,
            row_segment,
            *kv_pieces,
            *key_segments,
            query_raw,
            gain_q,
            cosine,
            sine,
        ],
        [
            shape(count, shard, dtype=F32),
            shape(count, width),
            shape(1, width, dtype=F32),
            shape(count, q_width),
            shape(1, HD, dtype=F32),
            shape(count, 2 * kv_width, dtype=F32),
        ]
        + [shape(count, 2 * kv_width)] * (blocks - 1),
        2 * count * width * q_width,
        "middle",
        after=[gate_low],
    )
    kv_sums = [grad_kv] + [
        lax.ppermute(sent, "ctx", [(i, i ^ (s + 1)) for i in range(blocks)])
        for s, sent in enumerate(grad_kv_sent)
    ]
    output_part = matmul_tn(mixed_rows, grad_resid_low).astype(BF)
    if has_pair():
        half = q_width // 2
        keep = lax.dynamic_slice_in_dim(output_part, core * half, half, 0)
        send = lax.dynamic_slice_in_dim(output_part, (1 - core) * half, half, 0)
        output_part = (keep.astype(F32) + swap(send, "dp", 1).astype(F32)).astype(BF)
    half = output_part.shape[0] // 2
    output_parts = [output_part[:half], output_part[half:]]
    bits = [mask for mask in masks if mask and mask & (mask - 1) == 0]

    def summed(parts, bit_of, earlier=(), later=()):
        received = [
            send_plane(order_after(part, *earlier), bit) for part, bit in zip(parts, bit_of)
        ]
        return [
            (part.astype(F32) + order_after(other, *later).astype(F32)).astype(BF)
            for part, other in zip(parts, received)
        ]

    grad_low, grad_key_gain = kernel_call(
        functools.partial(key_backward_body, len(kv_sums)),
        ids,
        [*kv_sums, key_raw, gain_k, cosine, sine, grad_query_low],
        [shape(count, q_width + 2 * kv_width), shape(1, HD, dtype=F32)],
        40 * count * kv_width,
        "key_backward",
        after=output_parts,
    )
    all_grad_low = plane_all(grad_low)
    first_parts = output_parts

    grad_one_pieces = kernel_call(
        functools.partial(first_grad_body, tensor),
        ids,
        [
            *x_pieces,
            inverse_one,
            gain_one,
            grad_query_gain,
            grad_key_gain,
            grad_low,
            query_weight,
            key_weight,
            value_weight,
        ],
        [shape(count + EXTRA, shard)] * tensor,
        2 * count * width * (q_width + 2 * kv_width),
        "first_grad",
    )
    grad_gate_w, grad_up_w, grad_down_w = assemble(ids, lows, block, held, grad_one_pieces[:1])
    outputs = (resid_part.astype(F32) + order_after(feed, grad_gate_w).astype(F32)).astype(BF)

    grad_one = first_half(grad_one_pieces, "tensor", grad_gate_w)
    grad_query_w, grad_key_w, grad_value_w = projection_weights(
        ids, [all_normed_one], [all_grad_low], q_width, kv_width, [grad_gate_w, *grad_one.values()]
    )

    grad_one = second_half(grad_one, "tensor", [grad_query_w])
    grad_one_part = grad_one[:count]
    small = grad_one[count + 1 : count + 1 + (count + 2 * HD) // shard].reshape(-1)
    row_total_one = small[:count, None]
    feed_part_sums = lax.dynamic_slice_in_dim(feed_sums[0], column, shard)
    small = jnp.concatenate([grad_one[count], feed_part_sums, small[count:]])
    unit_one_part = inputs.astype(F32) * inverse_one
    grad_inputs = (
        grad_resid_part
        + inverse_one * (gain_one_part * grad_one_part)
        - unit_one_part * (inverse_one / width) * row_total_one
    )

    output_parts = summed(first_parts, (bits[0], bits[-1]), (), [grad_gate_w])
    for i in range(1, len(bits)):
        output_parts = summed(output_parts, (bits[i], bits[-1 - i]), [grad_gate_w], [grad_query_w])
    if has_pair():
        small = small + swap(small, "dp", 1)
    for bit in bits:
        small = small + send_plane(small, bit)
    grad_attention_gain = small[:shard]
    grad_feed_gain = small[shard : 2 * shard]
    grad_query_gain = small[2 * shard : 2 * shard + HD]
    grad_key_gain = small[2 * shard + HD :]
    if has_pair():
        others = [swap(part, "dp", 1) for part in output_parts]
        grad_output_w = jnp.where(
            core == 0,
            jnp.concatenate(output_parts + others, axis=0),
            jnp.concatenate(others + output_parts, axis=0),
        )
    else:
        grad_output_w = jnp.concatenate(output_parts, axis=0)
    grad_output_w = grad_output_w.astype(F32)

    return (
        outputs,
        grad_inputs,
        grad_attention_gain,
        grad_query_w,
        grad_key_w,
        grad_value_w,
        grad_query_gain,
        grad_key_gain,
        grad_output_w,
        grad_feed_gain,
        grad_gate_w,
        grad_up_w,
        grad_down_w,
    )


def solution(mesh):
    in_specs = (
        P(("dp", "ctx"), "tensor"),
        P(("dp", "ctx"), None),
        P("dp", None),
        P("dp", "ctx"),
        P(),
        P(None, "tensor"),
        P(None, "tensor"),
        P(None, "tensor"),
        P(),
        P(),
        P("tensor", None),
        P(),
        P(None, "tensor"),
        P(None, "tensor"),
        P("tensor", None),
    )
    out_specs = (
        P(("dp", "ctx"), "tensor"),
        P(("dp", "ctx"), "tensor"),
        P("tensor"),
        P(None, "tensor"),
        P(None, "tensor"),
        P(None, "tensor"),
        P(),
        P(),
        P("tensor", None),
        P("tensor"),
        P(None, "tensor"),
        P(None, "tensor"),
        P("tensor", None),
    )
    return jax.shard_map(
        per_device, mesh=mesh, in_specs=in_specs, out_specs=out_specs, check_vma=False
    )
```

```python
import functools

import jax
import jax.numpy as jnp
from jax import lax
from jax.experimental import pallas as pl
from jax.experimental.pallas import tpu as pltpu
from jax.sharding import PartitionSpec as P

HD = 128
EPS = 1e-06
THETA = 1000000.0
NEG = -1e30
BF = jnp.bfloat16
F32 = jnp.float32
MIB = 1024 * 1024
VMEM_LIMIT = 63 * MIB + 900 * 1024
EXTRA = 16
SCALE = 2


def swap(value, axis, bit):
    size = lax.axis_size(axis)
    return lax.ppermute(value, axis, [(i, i ^ bit) for i in range(size)])


def bits_of(size):
    out = []
    bit = 1
    while bit < size:
        out.append(bit)
        bit *= 2
    return out


def gather_pieces(value, axis):
    pieces = {0: value}
    for bit in reversed(bits_of(lax.axis_size(axis))):
        for s in list(pieces):
            pieces[s | bit] = swap(pieces[s], axis, bit)
    return [pieces[s] for s in range(len(pieces))]


def send_pieces(pieces, axis):
    size = lax.axis_size(axis)
    return [
        lax.ppermute(pieces[s], axis, [(i, i ^ s) for i in range(size)])
        for s in sorted(range(1, size), key=lambda s: -s)
    ]


def send_all(value, axis):
    size = lax.axis_size(axis)
    pieces = {0: value}
    for s in range(size - 1, 0, -1):
        pieces[s] = lax.ppermute(value, axis, [(i, i ^ s) for i in range(size)])
    return [pieces[s] for s in range(size)]


def first_half(pieces, axis, *later):
    pieces = dict(enumerate(pieces))
    for s in [s for s in sorted(pieces, reverse=True) if not s & 1]:
        other = order_after(swap(pieces.pop(s | 1), axis, 1), *later)
        pieces[s] = (pieces[s].astype(F32) + other.astype(F32)).astype(BF if s else F32)
    return pieces


def second_half(pieces, axis, later=()):
    pieces = dict(pieces)
    for bit in bits_of(lax.axis_size(axis))[1:]:
        for s in [s for s in sorted(pieces, reverse=True) if not s & bit]:
            other = order_after(swap(pieces.pop(s | bit), axis, bit), *later)
            pieces[s] = (pieces[s].astype(F32) + other.astype(F32)).astype(BF if s else F32)
    return pieces[0]


def total_of(own, others):
    total = own.astype(F32)
    for other in others:
        total = total + other.astype(F32)
    return total


def far_masks():
    size = lax.axis_size("ctx")
    bits = [size * bit for bit in bits_of(lax.axis_size("dp")) if bit > 1] + bits_of(size)
    masks = [0]
    for bit in bits:
        masks = masks + [mask | bit for mask in masks]
    return masks


def send_plane(value, mask):
    if mask == 0:
        return value
    size = lax.axis_size("dp") * lax.axis_size("ctx")
    return lax.ppermute(value, ("dp", "ctx"), [(i, i ^ mask) for i in range(size)])


def pass_on(parts, masks, highest, *earlier):
    parts = list(parts)
    for mask in masks[len(parts) :]:
        bit = 1 << (mask.bit_length() - 1) if highest else mask & -mask
        parts.append(send_plane(order_after(parts[masks.index(mask ^ bit)], *earlier), bit))
    return parts


def plane_all(value):
    return lax.all_gather(value, ("dp", "ctx"), axis=0, tiled=True)


def sum_tensor(value):
    return lax.psum_scatter(value, "tensor", scatter_dimension=1, tiled=True)


def has_pair():
    return lax.axis_size("dp") > 1


def partners(parts, *earlier):
    if not has_pair():
        return []
    return [swap(order_after(part, *earlier), "dp", 1) for part in parts]


def order_after(value, *earlier):
    return lax.optimization_barrier((value, *earlier))[0] if earlier else value


def pieces_of(order, index, shard):
    return pl.multiple_of((index ^ order) * shard, shard)


def dot(left, right):
    return jnp.dot(left, right, preferred_element_type=F32)


def dot_nt(left, right):
    return lax.dot_general(left, right, (((1,), (1,)), ((), ())), preferred_element_type=F32)


def dot_tn(left, right):
    return lax.dot_general(left, right, (((0,), (0,)), ((), ())), preferred_element_type=F32)


def shape(*dims, dtype=BF):
    return jax.ShapeDtypeStruct(dims, dtype)


def size_of(arrays):
    return sum(a.size * a.dtype.itemsize for a in arrays)


def cost(flops, moved):
    return pl.CostEstimate(
        flops=int(flops) // SCALE, bytes_accessed=int(moved) // SCALE, transcendentals=0
    )


class Loads:
    def __init__(self, copies, buffers):
        self.copies = dict(enumerate(copies))
        self.buffers = buffers

    def __getitem__(self, index):
        if isinstance(index, slice):
            return [self[i] for i in range(*index.indices(len(self.buffers)))]
        if index in self.copies:
            self.copies.pop(index).wait()
        return self.buffers[index]

    def finish(self):
        for index in list(self.copies):
            self[index]


ANY = pl.BlockSpec(memory_space=pl.ANY)
SMEM = pl.BlockSpec(memory_space=pltpu.SMEM)


def kernel_call(body, ids, arrays, outs, flops, name, after=(), scratch=()):
    count, extra, results = len(arrays), len(after), len(outs)

    def run(ids, *refs):
        sources = refs[:count]
        out_refs = refs[count + extra : count + extra + results]
        buffers = refs[count + extra + results : 2 * count + extra + results]
        sems = refs[2 * count + extra + results]
        copies = [
            pltpu.make_async_copy(source, buffer, sems.at[i])
            for i, (source, buffer) in enumerate(zip(sources, buffers))
        ]
        for copy in copies:
            copy.start()
        loads = Loads(copies, buffers)
        body(ids, loads, *out_refs, *refs[2 * count + extra + results + 1 :])
        loads.finish()

    moved = size_of(arrays) + size_of(outs)
    return pl.pallas_call(
        run,
        out_shape=tuple(outs),
        in_specs=[SMEM] + [ANY] * (count + extra),
        out_specs=tuple(pl.BlockSpec(memory_space=pltpu.VMEM) for _ in outs),
        scratch_shapes=[pltpu.VMEM(a.shape, a.dtype) for a in arrays]
        + [pltpu.SemaphoreType.DMA((count,))]
        + [pltpu.VMEM(a.shape, a.dtype) for a in scratch],
        compiler_params=pltpu.CompilerParams(vmem_limit_bytes=VMEM_LIMIT),
        cost_estimate=cost(flops, moved),
        name=name,
    )(ids, *arrays, *after)


def turn(value):
    return pltpu.roll(value, HD // 2, 1)


def head_forward(raw, gain, cosine, sine):
    scale = lax.rsqrt(jnp.mean(raw * raw, axis=-1, keepdims=True) + EPS)
    normed = raw * scale * gain
    return normed * cosine + turn(normed) * sine


def head_backward(grad, raw, gain, cosine, sine):
    scale = lax.rsqrt(jnp.mean(raw * raw, axis=-1, keepdims=True) + EPS)
    unit = raw * scale
    grad_normed = grad * cosine + turn(grad * sine)
    grad_gain = jnp.sum(grad_normed * unit, axis=0, keepdims=True)
    inner = grad_normed * gain
    grad_raw = scale * (inner - unit * jnp.mean(inner * unit, axis=-1, keepdims=True))
    return grad_raw, grad_gain


def key_value_body(count, ids, loads, normed_ref, kv, raw_ref, inverse_ref):
    pieces = loads[:count]
    rows, shard = pieces[0].shape
    squares = 0.0
    for piece in pieces:
        x = piece[...].astype(F32)
        squares += jnp.sum(x * x, axis=-1, keepdims=True)
    inverse = lax.rsqrt(squares * (1.0 / (shard * count)) + EPS)
    inverse_ref[...] = inverse
    gain, key_gain, cosine, sine, wk, wv = loads[count : count + 6]
    kv_width = wk.shape[1]
    key_raw = jnp.zeros((rows, kv_width), F32)
    values = jnp.zeros((rows, kv_width), F32)
    for s in range(count):
        off = pieces_of(s, ids[0], shard)
        normed = (pieces[s][...].astype(F32) * inverse * gain[:, pl.ds(off, shard)]).astype(BF)
        normed_ref[:, pl.ds(off, shard)] = normed
        key_raw += dot(normed, wk[pl.ds(off, shard), :])
        values += dot(normed, wv[pl.ds(off, shard), :])
    raw_ref[...] = key_raw
    for h in range(kv_width // HD):
        cols = slice(h * HD, (h + 1) * HD)
        out = head_forward(key_raw[:, cols], key_gain[...], cosine[...], sine[...])
        kv[:, cols] = out.astype(BF)
    kv[:, kv_width:] = values.astype(BF)


def query_body(ids, loads, q_ref, raw_ref):
    normed, wq, query_gain, cosine, sine = loads[:5]
    raw = dot(normed[...], wq[...])
    raw_ref[...] = raw
    for h in range(wq.shape[1] // HD):
        cols = slice(h * HD, (h + 1) * HD)
        out = head_forward(raw[:, cols], query_gain[...], cosine[...], sine[...])
        q_ref[:, cols] = out.astype(BF)


def head_probs(ids, q, blocks, head, group, row_segment, key_segments):
    rows = q.shape[0]
    kv = head // group
    cols = slice(head * HD, (head + 1) * HD)
    row_index = ids[1] * rows + lax.broadcasted_iota(jnp.int32, (rows, rows), 0)
    parts = []
    for s, block in enumerate(blocks):
        scores = dot_nt(q[:, cols], block[:, kv * HD : (kv + 1) * HD]) * HD ** (-0.5)
        key_index = (ids[1] ^ s) * rows + lax.broadcasted_iota(jnp.int32, (rows, rows), 1)
        allowed = (row_segment[...] == key_segments[s][...]) & (key_index <= row_index)
        parts.append(jnp.where(allowed, scores, NEG))
    top = parts[0].max(axis=-1, keepdims=True)
    for part in parts[1:]:
        top = jnp.maximum(top, part.max(axis=-1, keepdims=True))
    parts = [jnp.exp(part - top) for part in parts]
    total = sum(jnp.sum(part, axis=-1, keepdims=True) for part in parts)
    share = 1.0 / total
    return [part * share for part in parts]


def attention_body(count, group, blocks, ids, loads, mixed_ref, *outs):
    q, row_segment = loads[:2]
    kvs = loads[2 : 2 + blocks]
    key_segments = loads[2 + blocks : 2 + 2 * blocks]
    kv_width = kvs[0].shape[1] // 2
    for h in range(q.shape[1] // HD):
        probs = head_probs(ids, q, kvs, h, group, row_segment, key_segments)
        start = kv_width + (h // group) * HD
        mixed = sum(
            dot(p.astype(BF), block[:, start : start + HD]) for p, block in zip(probs, kvs)
        )
        mixed_ref[:, h * HD : (h + 1) * HD] = mixed.astype(BF)
    wo = loads[2 + 2 * blocks]
    shard = wo.shape[1] // count
    for s in range(count):
        off = pieces_of(s, ids[0], shard)
        outs[s][...] = dot(mixed_ref[...], wo[:, pl.ds(off, shard)]).astype(BF)


def second_norm_body(count, ids, loads, normed_ref, resid_ref, inverse_ref):
    pieces = loads[:count]
    gain = loads[count]
    rows, shard = pieces[0].shape
    squares = 0.0
    for piece in pieces:
        x = piece[...].astype(F32)
        squares += jnp.sum(x * x, axis=-1, keepdims=True)
    inverse = lax.rsqrt(squares * (1.0 / (shard * count)) + EPS)
    inverse_ref[...] = inverse
    for s in range(count):
        off = pieces_of(s, ids[0], shard)
        cols = pl.ds(off, shard)
        x = pieces[s][...]
        resid_ref[:, cols] = x
        normed_ref[:, cols] = (x.astype(F32) * inverse * gain[:, cols]).astype(BF)


def gated_terms(gate, up, grad_hidden):
    sigmoid = jax.nn.sigmoid(gate)
    silu = gate * sigmoid
    grad_gate = grad_hidden * up * sigmoid * (1.0 + gate * (1.0 - sigmoid))
    return silu * up, grad_gate, grad_hidden * silu


def feed_forward_body(tile, extra, ids, normed_hbm, cot_hbm, wg_hbm, wu_hbm, wd_hbm, *refs):
    refs = refs[extra:]
    grad_out, feed_out, normed, cot, wg, wu, wd, total, feed, sems = refs
    units = wg.shape[1]
    tiles = units // tile
    first = [
        pltpu.make_async_copy(normed_hbm, normed, sems.at[3 * tiles]),
        pltpu.make_async_copy(cot_hbm, cot, sems.at[3 * tiles + 1]),
    ]

    def weights(t):
        cols = pl.ds(pl.multiple_of(t * tile, tile), tile)
        return [
            pltpu.make_async_copy(wg_hbm.at[:, cols], wg.at[:, cols], sems.at[t]),
            pltpu.make_async_copy(wu_hbm.at[:, cols], wu.at[:, cols], sems.at[tiles + t]),
            pltpu.make_async_copy(wd_hbm.at[cols, :], wd.at[cols, :], sems.at[2 * tiles + t]),
        ]

    for copy in first:
        copy.start()
    for t in range(tiles):
        for copy in weights(t):
            copy.start()
    total[...] = jnp.zeros_like(total)
    feed[...] = jnp.zeros_like(feed)
    for copy in first:
        copy.wait()

    def step(t, carry):
        cols = pl.ds(pl.multiple_of(t * tile, tile), tile)
        gate_copy, up_copy, down_copy = weights(t)
        gate_copy.wait()
        gate = dot(normed[...], wg[:, cols])
        up_copy.wait()
        up = dot(normed[...], wu[:, cols])
        down_copy.wait()
        grad_hidden = dot_nt(cot[...], wd[cols, :])
        hidden, grad_gate, grad_up = gated_terms(gate, up, grad_hidden)
        total[...] += dot_nt(grad_gate.astype(BF), wg[:, cols]) + dot_nt(
            grad_up.astype(BF), wu[:, cols]
        )
        feed[...] += dot(hidden.astype(BF), wd[cols, :])
        return carry

    lax.fori_loop(0, tiles, step, 0)
    grad_out[...] = total[...].astype(BF)
    feed_out[...] = feed[...].astype(BF)


def feed_forward(ids, normed, cot, wg, wu, wd, after=()):
    rows, width = cot.shape
    units = wg.shape[1]
    tile = max(t for t in (512, 384, 256, 128) if units % t == 0)
    arrays = [normed, cot, wg, wu, wd]
    outs = [shape(rows, width)] * 2
    moved = size_of(arrays) + size_of(outs)
    return pl.pallas_call(
        functools.partial(feed_forward_body, tile, len(after)),
        out_shape=outs,
        in_specs=[SMEM] + [ANY] * (5 + len(after)),
        out_specs=[pl.BlockSpec(memory_space=pltpu.VMEM) for _ in outs],
        scratch_shapes=[pltpu.VMEM(a.shape, a.dtype) for a in arrays]
        + [
            pltpu.VMEM((rows, width), F32),
            pltpu.VMEM((rows, width), F32),
            pltpu.SemaphoreType.DMA((3 * (units // tile) + 2,)),
        ],
        compiler_params=pltpu.CompilerParams(
            vmem_limit_bytes=VMEM_LIMIT
        ),
        cost_estimate=cost(12 * rows * width * units, moved),
        name="feed_forward",
    )(ids, *arrays, *after)


def middle_body(count, group, blocks, ids, loads, own_ref, low_ref, sums_ref, *outs):
    grads, resid, inverse_ref, gain, cot = loads[:5]
    rows, width = grads.shape
    shard = width // count
    inverse = inverse_ref[...]
    row_total = 0.0
    for s in range(count):
        cols = pl.ds(pieces_of(s, ids[0], shard), shard)
        product = grads[:, cols].astype(F32) * (resid[:, cols].astype(F32) * inverse)
        sums_ref[:, cols] = jnp.sum(product, axis=0, keepdims=True)
        row_total += jnp.sum(product * gain[:, cols], axis=-1, keepdims=True)
    scale = row_total * inverse * (1.0 / width)
    wo = loads[5]
    mixed = jnp.zeros((rows, wo.shape[0]), F32)
    for s in range(count):
        cols = pl.ds(pieces_of(s, ids[0], shard), shard)
        unit = resid[:, cols].astype(F32) * inverse
        grad = (
            cot[:, cols].astype(F32)
            + inverse * (gain[:, cols] * grads[:, cols].astype(F32))
            - unit * scale
        )
        if s == 0:
            own_ref[...] = grad
        low = grad.astype(BF)
        low_ref[:, cols] = low
        mixed += dot_nt(low, wo[:, cols])
    attention_backward(group, blocks, ids, loads[6:], mixed.astype(BF), *outs)


def attention_backward(group, blocks, ids, loads, grads, low_ref, gain_ref, own_ref, *others):
    q, row_segment = loads[:2]
    kvs = loads[2 : 2 + blocks]
    key_segments = loads[2 + blocks : 2 + 2 * blocks]
    raw, query_gain, cosine, sine = loads[2 + 2 * blocks : 6 + 2 * blocks]
    kv_width = kvs[0].shape[1] // 2
    factor = HD ** (-0.5)
    gain_total = jnp.zeros((1, HD), F32)
    outs = [own_ref] + list(others)
    for kv in range(kv_width // HD):
        key_cols = slice(kv * HD, (kv + 1) * HD)
        value_cols = slice(kv_width + kv * HD, kv_width + (kv + 1) * HD)
        key_sums = [0.0] * blocks
        value_sums = [0.0] * blocks
        for h in range(kv * group, (kv + 1) * group):
            cols = slice(h * HD, (h + 1) * HD)
            probs = head_probs(ids, q, kvs, h, group, row_segment, key_segments)
            grad = grads[:, cols]
            grad_probs = [dot_nt(grad, block[:, value_cols]) for block in kvs]
            delta = sum(jnp.sum(p * g, axis=-1, keepdims=True) for p, g in zip(probs, grad_probs))
            scores = [(p * (g - delta)).astype(BF) for p, g in zip(probs, grad_probs)]
            grad_query = sum(dot(g, block[:, key_cols]) for g, block in zip(scores, kvs)) * factor
            for s in range(blocks):
                key_sums[s] += dot_tn(scores[s], q[:, cols])
                value_sums[s] += dot_tn(probs[s].astype(BF), grad)
            grad_raw, grad_gain = head_backward(
                grad_query, raw[:, cols], query_gain[...], cosine[...], sine[...]
            )
            low_ref[:, cols] = grad_raw.astype(BF)
            gain_total += grad_gain
        for s in range(blocks):
            outs[s][:, key_cols] = (key_sums[s] * factor).astype(outs[s].dtype)
            outs[s][:, value_cols] = value_sums[s].astype(outs[s].dtype)
    gain_ref[...] = gain_total


def key_backward_body(blocks, ids, loads, low_ref, gain_ref):
    sums = loads[:blocks]
    raw, key_gain, cosine, sine, query_low = loads[blocks : blocks + 5]
    q_width = query_low.shape[1]
    kv_width = raw.shape[1]
    low_ref[:, :q_width] = query_low[...]
    total = sums[0][...]
    for other in sums[1:]:
        total = total + other[...].astype(F32)
    gain_total = jnp.zeros((1, HD), F32)
    for h in range(kv_width // HD):
        cols = slice(h * HD, (h + 1) * HD)
        grad_raw, grad_gain = head_backward(
            total[:, cols], raw[:, cols], key_gain[...], cosine[...], sine[...]
        )
        low_ref[:, q_width + h * HD : q_width + (h + 1) * HD] = grad_raw.astype(BF)
        gain_total += grad_gain
    low_ref[:, q_width + kv_width :] = total[:, kv_width:].astype(BF)
    gain_ref[...] = gain_total


def first_grad_body(count, ids, loads, *outs):
    pieces = loads[:count]
    inverse_ref, gain, query_sums, key_sums, grads, wq, wk, wv = loads[count : count + 8]
    rows, shard = pieces[0].shape
    q_width, kv_width = wq.shape[1], wk.shape[1]
    inverse = inverse_ref[...]
    row_total = jnp.zeros((rows, 1), F32)
    for s in range(count):
        cols = pl.ds(pieces_of(s, ids[0], shard), shard)
        grad = (
            dot_nt(grads[:, :q_width], wq[cols, :])
            + dot_nt(grads[:, q_width : q_width + kv_width], wk[cols, :])
            + dot_nt(grads[:, q_width + kv_width :], wv[cols, :])
        )
        product = grad * (pieces[s][...].astype(F32) * inverse)
        outs[s][:rows, :] = grad.astype(BF)
        outs[s][rows:, :] = jnp.zeros((EXTRA, shard), BF)
        outs[s][rows : rows + 1, :] = jnp.sum(product, axis=0, keepdims=True).astype(BF)
        row_total += jnp.sum(product * gain[:, cols], axis=-1, keepdims=True)
    turned = jnp.broadcast_to(row_total, (rows, HD)).T[:1]
    small = jnp.concatenate([turned, query_sums[...], key_sums[...]], axis=1).astype(BF)
    for s in range(count):
        for r in range(small.shape[1] // shard):
            row = rows + 1 + r
            outs[s][row : row + 1, :] = small[:, r * shard : (r + 1) * shard]


def feed_weight_body(parts, extra, last, block, ids, *refs):
    rows_hbm, cots_hbm = refs[:parts], refs[parts : 2 * parts]
    wg_hbm, wu_hbm, wd_hbm = refs[2 * parts : 2 * parts + 3]
    refs = refs[2 * parts + 3 + extra :]
    dwg, dwu, dwd = refs[:3]
    lows = refs[3:6] if last else ()
    refs = refs[6:] if last else refs[3:]
    rows, cots, hid, gates, ups, wg, wu, wd, gate_out, up_out, down_out = refs[:11]
    refs = refs[11:]
    if last:
        gate_held, up_held, down_held, gate_cut, up_cut, down_cut = refs[:6]
        refs = refs[6:]
    row_sems, cot_sems, weight_sems, held_sems, out_sems = refs
    width = rows.shape[1]
    size = rows_hbm[0].shape[0]
    group = 2 if parts % 2 == 0 else 1
    chunk = group * size
    steps = wg_hbm.shape[1] // block // 2
    tile = width // 2

    def mine(b):
        return pl.ds(pl.multiple_of((ids[2] * steps + b) * block, block), block)

    def weights(b, slot):
        return [
            pltpu.make_async_copy(wg_hbm.at[:, mine(b)], wg.at[slot], weight_sems.at[slot, 0]),
            pltpu.make_async_copy(wu_hbm.at[:, mine(b)], wu.at[slot], weight_sems.at[slot, 1]),
            pltpu.make_async_copy(wd_hbm.at[mine(b), :], wd.at[slot], weight_sems.at[slot, 2]),
        ]

    def tile_at(t):
        return pl.ds(pl.multiple_of(t * tile, tile), tile)

    def held(b, t):
        at = tile_at(t)
        pairs = [
            (dwg.at[at, mine(b)], gate_held.at[at, :]),
            (dwu.at[at, mine(b)], up_held.at[at, :]),
            (dwd.at[mine(b), at], down_held.at[:, at]),
        ]
        return [pltpu.make_async_copy(a, c, held_sems.at[t, i]) for i, (a, c) in enumerate(pairs)]

    def results(b, t):
        at = tile_at(t)
        low = pl.ds(pl.multiple_of(b * block, block), block)
        pairs = [
            (gate_out.at[at, :], dwg.at[at, mine(b)]),
            (up_out.at[at, :], dwu.at[at, mine(b)]),
            (down_out.at[:, at], dwd.at[mine(b), at]),
        ]
        if last:
            pairs += [
                (gate_cut.at[at, :], lows[0].at[at, low]),
                (up_cut.at[at, :], lows[1].at[at, low]),
                (down_cut.at[:, at], lows[2].at[low, at]),
            ]
        return [pltpu.make_async_copy(a, c, out_sems.at[t, i]) for i, (a, c) in enumerate(pairs)]

    for copy in weights(0, 0):
        copy.start()
    for i in range(parts):
        place = pl.ds(i * size, size)
        pltpu.make_async_copy(rows_hbm[i], rows.at[place, :], row_sems.at[i // group]).start()
        pltpu.make_async_copy(cots_hbm[i], cots.at[place, :], cot_sems.at[i // group]).start()

    def one_block(b, carry):
        slot = lax.rem(b, 2)
        for copy in weights(b, slot):
            copy.wait()
        if last:
            for t in range(2):
                for copy in held(b, t):
                    copy.start()

        @pl.when(b + 1 < steps)
        def _():
            for copy in weights(b + 1, 1 - slot):
                copy.start()

        def recompute(c, carry):
            place = pl.ds(pl.multiple_of(c * chunk, chunk), chunk)

            @pl.when(b == 0)
            def _():
                pltpu.make_async_copy(rows.at[place, :], rows.at[place, :], row_sems.at[c]).wait()
                pltpu.make_async_copy(cots.at[place, :], cots.at[place, :], cot_sems.at[c]).wait()

            own = rows[place, :]
            gate = dot(own, wg[slot])
            up = dot(own, wu[slot])
            grad_hidden = dot_nt(cots[place, :], wd[slot])
            hidden, grad_gate, grad_up = gated_terms(gate, up, grad_hidden)
            hid[place, :] = hidden.astype(BF)
            gates[place, :] = grad_gate.astype(BF)
            ups[place, :] = grad_up.astype(BF)
            return carry

        lax.fori_loop(0, parts // group, recompute, 0)

        def products(t, carry):
            @pl.when(b > 0)
            def _():
                for copy in results(b, t):
                    copy.wait()

            cols = tile_at(t)
            down = dot_tn(hid[...], cots[:, cols])
            gate = dot_tn(rows[:, cols], gates[...])
            up = dot_tn(rows[:, cols], ups[...])
            if last:
                for copy in held(b, t):
                    copy.wait()
                down = (down + down_held[:, cols]).astype(BF)
                gate = (gate + gate_held[cols, :]).astype(BF)
                up = (up + up_held[cols, :]).astype(BF)
                down_cut[:, cols] = down
                gate_cut[cols, :] = gate
                up_cut[cols, :] = up
            down_out[:, cols] = down.astype(F32)
            gate_out[cols, :] = gate.astype(F32)
            up_out[cols, :] = up.astype(F32)
            for copy in results(b, t):
                copy.start()
            return carry

        lax.fori_loop(0, 2, products, 0)
        return carry

    lax.fori_loop(0, steps, one_block, 0)
    for t in range(2):
        for copy in results(0, t):
            copy.wait()


def feed_weights(ids, rows, cots, wg, wu, wd, block, held, last, after=()):
    parts = len(rows)
    size, width = rows[0].shape
    tokens = size * parts
    units = wg.shape[1]
    held = list(held or ())
    outs = [
        shape(width, units, dtype=F32),
        shape(width, units, dtype=F32),
        shape(units, width, dtype=F32),
    ]
    tiles = [
        shape(width, block, dtype=F32),
        shape(width, block, dtype=F32),
        shape(block, width, dtype=F32),
    ]
    scratch = [
        shape(tokens, width),
        shape(tokens, width),
        shape(tokens, block),
        shape(tokens, block),
        shape(tokens, block),
        shape(2, width, block),
        shape(2, width, block),
        shape(2, block, width),
        *tiles,
    ]
    if last:
        outs += [shape(width, units // 2), shape(width, units // 2), shape(units // 2, width)]
        scratch += [*tiles, shape(width, block), shape(width, block), shape(block, width)]
    if not held and last:
        held = [jnp.zeros(o.shape, F32) for o in outs[:3]]
    extra = len(held) + len(after)
    return pl.pallas_call(
        functools.partial(feed_weight_body, parts, extra, last, block),
        out_shape=outs,
        in_specs=[SMEM] + [ANY] * (2 * parts + 3 + extra),
        out_specs=[ANY] * len(outs),
        scratch_shapes=[pltpu.VMEM(a.shape, a.dtype) for a in scratch]
        + [
            pltpu.SemaphoreType.DMA((parts,)),
            pltpu.SemaphoreType.DMA((parts,)),
            pltpu.SemaphoreType.DMA((2, 3)),
            pltpu.SemaphoreType.DMA((2, 3)),
            pltpu.SemaphoreType.DMA((2, 6)),
        ],
        input_output_aliases={4 + 2 * parts + i: i for i in range(len(held))},
        compiler_params=pltpu.CompilerParams(vmem_limit_bytes=VMEM_LIMIT),
        cost_estimate=cost(6 * tokens * width * units, 4 * tokens * width),
        name="feed_weights",
    )(ids, *rows, *cots, wg, wu, wd, *held, *after)


def assemble_body(extra, ids, gate_low, up_low, down_low, *refs):
    dwg, dwu, dwd = refs[-3:]
    dwg[...] = gate_low[...].astype(F32)
    dwu[...] = up_low[...].astype(F32)
    dwd[...] = down_low[...].astype(F32)


def assemble(ids, lows, block, held, after=()):
    width, units = held[0].shape
    steps = units // block // 2
    tile = width // 2
    cols_in = pl.BlockSpec((tile, block), lambda b, i, ids: (i, b))
    rows_in = pl.BlockSpec((block, tile), lambda b, i, ids: (b, i))
    cols_out = pl.BlockSpec((tile, block), lambda b, i, ids: (i, (1 - ids[2]) * steps + b))
    rows_out = pl.BlockSpec((block, tile), lambda b, i, ids: ((1 - ids[2]) * steps + b, i))
    return pl.pallas_call(
        functools.partial(assemble_body, len(after)),
        out_shape=[shape(*a.shape, dtype=F32) for a in held],
        grid_spec=pltpu.PrefetchScalarGridSpec(
            num_scalar_prefetch=1,
            grid=(steps, 2),
            in_specs=[cols_in, cols_in, rows_in] + [ANY] * (3 + len(after)),
            out_specs=[cols_out, cols_out, rows_out],
        ),
        input_output_aliases={4: 0, 5: 1, 6: 2},
        compiler_params=pltpu.CompilerParams(vmem_limit_bytes=VMEM_LIMIT),
        cost_estimate=cost(0, 9 * width * units),
        name="assemble",
    )(ids, *lows, *held, *after)


def projection_body(parts, tile, extra, ids, *refs):
    rows_hbm, grads_hbm = refs[:parts], refs[parts : 2 * parts]
    refs = refs[2 * parts + extra :]
    outs_hbm = refs[:3]
    rows, grads, *outs, row_sems, grad_sem, out_sems = refs[3:]
    width = rows.shape[1]
    tiles = width // tile
    at = 0
    for i in range(parts):
        place = pl.ds(at, grads_hbm[i].shape[0])
        pltpu.make_async_copy(grads_hbm[i], grads.at[place, :], grad_sem).start()
        at += grads_hbm[i].shape[0]
    for t in range(tiles):
        cols = pl.ds(t * tile, tile)
        at = 0
        for i in range(parts):
            place = pl.ds(at, rows_hbm[i].shape[0])
            pltpu.make_async_copy(
                rows_hbm[i].at[:, cols], rows.at[place, cols], row_sems.at[t]
            ).start()
            at += rows_hbm[i].shape[0]
    pltpu.make_async_copy(grads, grads, grad_sem).wait()
    q_width, kv_width = outs[0].shape[1], outs[1].shape[1]

    def copies(t):
        cols = pl.ds(pl.multiple_of(t * tile, tile), tile)
        return [
            pltpu.make_async_copy(a.at[cols, :], b.at[cols, :], out_sems.at[t, i])
            for i, (a, b) in enumerate(zip(outs, outs_hbm))
        ]

    def products(t, carry):
        cols = pl.ds(pl.multiple_of(t * tile, tile), tile)
        pltpu.make_async_copy(rows.at[:, cols], rows.at[:, cols], row_sems.at[t]).wait()
        total = dot_tn(rows[:, cols], grads[...])
        outs[0][cols, :] = total[:, :q_width]
        outs[1][cols, :] = total[:, q_width : q_width + kv_width]
        outs[2][cols, :] = total[:, q_width + kv_width :]
        for copy in copies(t):
            copy.start()
        return carry

    lax.fori_loop(0, tiles, products, 0)

    def finish(t, carry):
        for copy in copies(t):
            copy.wait()
        return carry

    lax.fori_loop(0, tiles, finish, 0)


def projection_weights(ids, rows, grads, q_width, kv_width, after):
    parts = len(rows)
    width = rows[0].shape[1]
    tokens = sum(a.shape[0] for a in rows)
    tile = 512
    outs = [shape(width, w, dtype=F32) for w in (q_width, kv_width, kv_width)]
    scratch = [shape(tokens, width), shape(tokens, q_width + 2 * kv_width)] + outs
    return pl.pallas_call(
        functools.partial(projection_body, parts, tile, len(after)),
        out_shape=outs,
        in_specs=[SMEM] + [ANY] * (2 * parts + len(after)),
        out_specs=[ANY] * 3,
        scratch_shapes=[pltpu.VMEM(a.shape, a.dtype) for a in scratch]
        + [
            pltpu.SemaphoreType.DMA((width // tile,)),
            pltpu.SemaphoreType.DMA(()),
            pltpu.SemaphoreType.DMA((width // tile, 3)),
        ],
        compiler_params=pltpu.CompilerParams(
            vmem_limit_bytes=VMEM_LIMIT
        ),
        cost_estimate=cost(2 * tokens * width * (q_width + 2 * kv_width), 2 * tokens * width),
        name="projection_weights",
    )(ids, *rows, *grads, *after)


def matmul_tn(left, right):
    return lax.dot_general(left, right, (((0,), (0,)), ((), ())), preferred_element_type=F32)


def rope_tables(position_row):
    half = HD // 2
    freqs = jnp.exp(-(2.0 * jnp.arange(half, dtype=F32) / HD) * jnp.log(F32(THETA)))
    angles = position_row.astype(F32)[:, None] * freqs[None, :]
    cosine, sine = jnp.cos(angles), jnp.sin(angles)
    return jnp.concatenate([cosine, cosine], axis=1), jnp.concatenate([-sine, sine], axis=1)


def per_device(
    inputs,
    cotangent,
    segments,
    positions,
    attention_gain,
    query_weight,
    key_weight,
    value_weight,
    query_gain,
    key_gain,
    output_weight,
    feed_gain,
    gate_weight,
    up_weight,
    down_weight,
):
    count, shard = inputs.shape
    width = cotangent.shape[1]
    tensor = lax.axis_size("tensor")
    me = lax.axis_index("tensor")
    column = me * shard
    place = lax.axis_index("ctx")
    core = lax.axis_index("dp") % 2
    ids = jnp.stack([me, place, core, lax.axis_index("dp")]).astype(jnp.int32)
    q_width, kv_width = query_weight.shape[1], key_weight.shape[1]
    group = q_width // kv_width
    blocks = lax.axis_size("ctx")
    gain_one = attention_gain.astype(F32)[None]
    gain_two = feed_gain.astype(F32)[None]
    gain_q = query_gain.astype(F32)[None]
    gain_k = key_gain.astype(F32)[None]
    gain_one_part = lax.dynamic_slice_in_dim(gain_one, column, shard, 1)
    hidden_units = gate_weight.shape[1]
    block = 256 if (hidden_units // 2) % 256 == 0 else 128

    masks = far_masks()
    first_masks = len(masks) // 2 or 1
    x_pieces = gather_pieces(inputs, "tensor")
    cot_parts = [send_plane(cotangent, mask) for mask in masks[:first_masks + 1]]
    cosine, sine = rope_tables(positions[0])
    segment_row = segments[0]
    row_segment = lax.dynamic_slice_in_dim(segment_row, place * count, count)[:, None]
    key_segments = [
        lax.dynamic_slice_in_dim(segment_row, (place ^ s) * count, count)[None]
        for s in range(blocks)
    ]
    normed_one, kv_rows, key_raw, inverse_one = kernel_call(
        functools.partial(key_value_body, tensor),
        ids,
        [*x_pieces, gain_one, gain_k, cosine, sine, key_weight, value_weight],
        [
            shape(count, width),
            shape(count, 2 * kv_width),
            shape(count, kv_width, dtype=F32),
            shape(count, 1, dtype=F32),
        ],
        4 * count * width * kv_width,
        "key_value",
        after=[*cot_parts[1:], row_segment, *key_segments],
    )
    kv_pieces = gather_pieces(kv_rows, "ctx")
    all_normed_one = plane_all(normed_one)
    query_rows, query_raw = kernel_call(
        query_body,
        ids,
        [normed_one, query_weight, gain_q, cosine, sine],
        [shape(count, q_width), shape(count, q_width, dtype=F32)],
        2 * count * width * q_width,
        "query",
    )

    mixed_rows, *branch_pieces = kernel_call(
        functools.partial(attention_body, tensor, group, blocks),
        ids,
        [query_rows, row_segment, *kv_pieces, *key_segments, output_weight],
        [shape(count, q_width)] + [shape(count, shard)] * tensor,
        4 * count * count * blocks * q_width + 2 * count * width * q_width,
        "attention",
    )
    branch = second_half(first_half(branch_pieces, "tensor"), "tensor")
    resid_part = (inputs.astype(F32) + branch).astype(BF)
    resid_pieces = gather_pieces(resid_part, "tensor")
    cot_partners = partners(cot_parts[: first_masks + 1])

    normed_two, resid, inverse_two = kernel_call(
        functools.partial(second_norm_body, tensor),
        ids,
        [*resid_pieces, gain_two],
        [shape(count, width), shape(count, width), shape(count, 1, dtype=F32)],
        8 * count * width,
        "second_norm",
        after=cot_partners,
    )
    two_parts = [send_plane(normed_two, mask) for mask in masks[: first_masks + 1]]
    grad_two_part, feed_part = feed_forward(
        ids, normed_two, cotangent, gate_weight, up_weight, down_weight
    )
    feed_done = feed_part
    grad_two_part = sum_tensor(grad_two_part)
    two_parts = pass_on(two_parts, masks, True, feed_done)
    cot_parts = pass_on(cot_parts, masks, False, feed_done)
    groups = [slice(0, first_masks), slice(first_masks, None)] if len(masks) > 1 else [slice(0, None)]
    last = len(groups) - 1
    two_partners = partners(two_parts[:1]) + partners(two_parts[1 : first_masks + 1], feed_done)

    def weights_of(g, held, after):
        return feed_weights(
            ids,
            two_parts[groups[g]] + two_partners[groups[g]],
            cot_parts[groups[g]] + cot_partners[groups[g]],
            gate_weight,
            up_weight,
            down_weight,
            block,
            held,
            g == last,
            after,
        )

    held, done = None, [feed_done, *two_partners, all_normed_one]
    for g in range(last):
        held = weights_of(g, held, done)
        done = held[:1]
    two_partners += partners(two_parts[first_masks + 1 :], *done)
    cot_partners += partners(cot_parts[first_masks + 1 :], *done)
    grad_two = lax.all_gather(grad_two_part, "tensor", axis=1, tiled=True)
    *held, gate_low, up_low, down_low = weights_of(last, held, [grad_two_part])
    lows = [gate_low, up_low, down_low]
    feed = sum_tensor(order_after(feed_part, gate_low))
    lows = [swap(low, "dp", 1) for low in lows] if has_pair() else lows

    (
        grad_resid_part,
        grad_resid_low,
        feed_sums,
        grad_query_low,
        grad_query_gain,
        grad_kv,
        *grad_kv_sent,
    ) = kernel_call(
        functools.partial(middle_body, tensor, group, blocks),
        ids,
        [
            grad_two,
            resid,
            inverse_two,
            gain_two,
            cotangent,
            output_weight,
            query_rows,
            row_segment,
            *kv_pieces,
            *key_segments,
            query_raw,
            gain_q,
            cosine,
            sine,
        ],
        [
            shape(count, shard, dtype=F32),
            shape(count, width),
            shape(1, width, dtype=F32),
            shape(count, q_width),
            shape(1, HD, dtype=F32),
            shape(count, 2 * kv_width, dtype=F32),
        ]
        + [shape(count, 2 * kv_width)] * (blocks - 1),
        2 * count * width * q_width,
        "middle",
        after=[gate_low],
    )
    kv_sums = [grad_kv] + [
        lax.ppermute(sent, "ctx", [(i, i ^ (s + 1)) for i in range(blocks)])
        for s, sent in enumerate(grad_kv_sent)
    ]
    output_part = matmul_tn(mixed_rows, grad_resid_low).astype(BF)
    if has_pair():
        half = q_width // 2
        keep = lax.dynamic_slice_in_dim(output_part, core * half, half, 0)
        send = lax.dynamic_slice_in_dim(output_part, (1 - core) * half, half, 0)
        output_part = (keep.astype(F32) + swap(send, "dp", 1).astype(F32)).astype(BF)
    half = output_part.shape[0] // 2
    output_parts = [output_part[:half], output_part[half:]]
    bits = [mask for mask in masks if mask and mask & (mask - 1) == 0]

    def summed(parts, bit_of, earlier=(), later=()):
        received = [
            send_plane(order_after(part, *earlier), bit) for part, bit in zip(parts, bit_of)
        ]
        return [
            (part.astype(F32) + order_after(other, *later).astype(F32)).astype(BF)
            for part, other in zip(parts, received)
        ]

    grad_low, grad_key_gain = kernel_call(
        functools.partial(key_backward_body, len(kv_sums)),
        ids,
        [*kv_sums, key_raw, gain_k, cosine, sine, grad_query_low],
        [shape(count, q_width + 2 * kv_width), shape(1, HD, dtype=F32)],
        40 * count * kv_width,
        "key_backward",
        after=output_parts,
    )
    all_grad_low = plane_all(grad_low)
    first_parts = output_parts

    grad_one_pieces = kernel_call(
        functools.partial(first_grad_body, tensor),
        ids,
        [
            *x_pieces,
            inverse_one,
            gain_one,
            grad_query_gain,
            grad_key_gain,
            grad_low,
            query_weight,
            key_weight,
            value_weight,
        ],
        [shape(count + EXTRA, shard)] * tensor,
        2 * count * width * (q_width + 2 * kv_width),
        "first_grad",
    )
    grad_gate_w, grad_up_w, grad_down_w = assemble(ids, lows, block, held, grad_one_pieces[:1])
    outputs = (resid_part.astype(F32) + order_after(feed, grad_gate_w).astype(F32)).astype(BF)

    grad_one = first_half(grad_one_pieces, "tensor", grad_gate_w)
    grad_query_w, grad_key_w, grad_value_w = projection_weights(
        ids, [all_normed_one], [all_grad_low], q_width, kv_width, [grad_gate_w, *grad_one.values()]
    )

    grad_one = second_half(grad_one, "tensor", [grad_query_w])
    grad_one_part = grad_one[:count]
    small = grad_one[count + 1 : count + 1 + (count + 2 * HD) // shard].reshape(-1)
    row_total_one = small[:count, None]
    feed_part_sums = lax.dynamic_slice_in_dim(feed_sums[0], column, shard)
    small = jnp.concatenate([grad_one[count], feed_part_sums, small[count:]])
    unit_one_part = inputs.astype(F32) * inverse_one
    grad_inputs = (
        grad_resid_part
        + inverse_one * (gain_one_part * grad_one_part)
        - unit_one_part * (inverse_one / width) * row_total_one
    )

    output_parts = summed(first_parts, (bits[0], bits[-1]), (), [grad_gate_w])
    for i in range(1, len(bits)):
        output_parts = summed(output_parts, (bits[i], bits[-1 - i]), [grad_gate_w], [grad_query_w])
    if has_pair():
        small = small + swap(small, "dp", 1)
    for bit in bits:
        small = small + send_plane(small, bit)
    grad_attention_gain = small[:shard]
    grad_feed_gain = small[shard : 2 * shard]
    grad_query_gain = small[2 * shard : 2 * shard + HD]
    grad_key_gain = small[2 * shard + HD :]
    if has_pair():
        others = [swap(part, "dp", 1) for part in output_parts]
        grad_output_w = jnp.where(
            core == 0,
            jnp.concatenate(output_parts + others, axis=0),
            jnp.concatenate(others + output_parts, axis=0),
        )
    else:
        grad_output_w = jnp.concatenate(output_parts, axis=0)
    grad_output_w = grad_output_w.astype(F32)

    return (
        outputs,
        grad_inputs,
        grad_attention_gain,
        grad_query_w,
        grad_key_w,
        grad_value_w,
        grad_query_gain,
        grad_key_gain,
        grad_output_w,
        grad_feed_gain,
        grad_gate_w,
        grad_up_w,
        grad_down_w,
    )


def solution(mesh):
    in_specs = (
        P(("dp", "ctx"), "tensor"),
        P(("dp", "ctx"), None),
        P("dp", None),
        P("dp", "ctx"),
        P(),
        P(None, "tensor"),
        P(None, "tensor"),
        P(None, "tensor"),
        P(),
        P(),
        P("tensor", None),
        P(),
        P(None, "tensor"),
        P(None, "tensor"),
        P("tensor", None),
    )
    out_specs = (
        P(("dp", "ctx"), "tensor"),
        P(("dp", "ctx"), "tensor"),
        P("tensor"),
        P(None, "tensor"),
        P(None, "tensor"),
        P(None, "tensor"),
        P(),
        P(),
        P("tensor", None),
        P("tensor"),
        P(None, "tensor"),
        P(None, "tensor"),
        P("tensor", None),
    )
    return jax.shard_map(
        per_device, mesh=mesh, in_specs=in_specs, out_specs=out_specs, check_vma=False
    )
```

```python
import functools

import jax
import jax.numpy as jnp
from jax import lax
from jax.experimental import pallas as pl
from jax.experimental.pallas import tpu as pltpu
from jax.sharding import PartitionSpec as P

HD = 128
EPS = 1e-06
THETA = 1000000.0
NEG = -1e30
BF = jnp.bfloat16
F32 = jnp.float32
MIB = 1024 * 1024
VMEM_LIMIT = 63 * MIB + 900 * 1024
EXTRA = 16
SCALE = 1


def swap(value, axis, bit):
    size = lax.axis_size(axis)
    return lax.ppermute(value, axis, [(i, i ^ bit) for i in range(size)])


def bits_of(size):
    out = []
    bit = 1
    while bit < size:
        out.append(bit)
        bit *= 2
    return out


def gather_pieces(value, axis):
    pieces = {0: value}
    for bit in reversed(bits_of(lax.axis_size(axis))):
        for s in list(pieces):
            pieces[s | bit] = swap(pieces[s], axis, bit)
    return [pieces[s] for s in range(len(pieces))]


def send_pieces(pieces, axis):
    size = lax.axis_size(axis)
    return [
        lax.ppermute(pieces[s], axis, [(i, i ^ s) for i in range(size)])
        for s in sorted(range(1, size), key=lambda s: -s)
    ]


def send_all(value, axis):
    size = lax.axis_size(axis)
    pieces = {0: value}
    for s in range(size - 1, 0, -1):
        pieces[s] = lax.ppermute(value, axis, [(i, i ^ s) for i in range(size)])
    return [pieces[s] for s in range(size)]


def first_half(pieces, axis, *later):
    pieces = dict(enumerate(pieces))
    for s in [s for s in sorted(pieces, reverse=True) if not s & 1]:
        other = order_after(swap(pieces.pop(s | 1), axis, 1), *later)
        pieces[s] = (pieces[s].astype(F32) + other.astype(F32)).astype(BF if s else F32)
    return pieces


def second_half(pieces, axis, later=()):
    pieces = dict(pieces)
    for bit in bits_of(lax.axis_size(axis))[1:]:
        for s in [s for s in sorted(pieces, reverse=True) if not s & bit]:
            other = order_after(swap(pieces.pop(s | bit), axis, bit), *later)
            pieces[s] = (pieces[s].astype(F32) + other.astype(F32)).astype(BF if s else F32)
    return pieces[0]


def total_of(own, others):
    total = own.astype(F32)
    for other in others:
        total = total + other.astype(F32)
    return total


def far_masks():
    size = lax.axis_size("ctx")
    bits = [size * bit for bit in bits_of(lax.axis_size("dp")) if bit > 1] + bits_of(size)
    masks = [0]
    for bit in bits:
        masks = masks + [mask | bit for mask in masks]
    return masks


def send_plane(value, mask):
    if mask == 0:
        return value
    size = lax.axis_size("dp") * lax.axis_size("ctx")
    return lax.ppermute(value, ("dp", "ctx"), [(i, i ^ mask) for i in range(size)])


def pass_on(parts, masks, highest, *earlier):
    parts = list(parts)
    for mask in masks[len(parts) :]:
        bit = 1 << (mask.bit_length() - 1) if highest else mask & -mask
        parts.append(send_plane(order_after(parts[masks.index(mask ^ bit)], *earlier), bit))
    return parts


def plane_all(value):
    return lax.all_gather(value, ("dp", "ctx"), axis=0, tiled=True)


def sum_tensor(value):
    return lax.psum_scatter(value, "tensor", scatter_dimension=1, tiled=True)


def has_pair():
    return lax.axis_size("dp") > 1


def partners(parts, *earlier):
    if not has_pair():
        return []
    return [swap(order_after(part, *earlier), "dp", 1) for part in parts]


def order_after(value, *earlier):
    return lax.optimization_barrier((value, *earlier))[0] if earlier else value


def pieces_of(order, index, shard):
    return pl.multiple_of((index ^ order) * shard, shard)


def dot(left, right):
    return jnp.dot(left, right, preferred_element_type=F32)


def dot_nt(left, right):
    return lax.dot_general(left, right, (((1,), (1,)), ((), ())), preferred_element_type=F32)


def dot_tn(left, right):
    return lax.dot_general(left, right, (((0,), (0,)), ((), ())), preferred_element_type=F32)


def shape(*dims, dtype=BF):
    return jax.ShapeDtypeStruct(dims, dtype)


def size_of(arrays):
    return sum(a.size * a.dtype.itemsize for a in arrays)


def cost(flops, moved):
    return pl.CostEstimate(
        flops=int(flops) * 2, bytes_accessed=int(moved) * 2, transcendentals=0
    )


class Loads:
    def __init__(self, copies, buffers):
        self.copies = dict(enumerate(copies))
        self.buffers = buffers

    def __getitem__(self, index):
        if isinstance(index, slice):
            return [self[i] for i in range(*index.indices(len(self.buffers)))]
        if index in self.copies:
            self.copies.pop(index).wait()
        return self.buffers[index]

    def finish(self):
        for index in list(self.copies):
            self[index]


ANY = pl.BlockSpec(memory_space=pl.ANY)
SMEM = pl.BlockSpec(memory_space=pltpu.SMEM)


def kernel_call(body, ids, arrays, outs, flops, name, after=(), scratch=()):
    count, extra, results = len(arrays), len(after), len(outs)

    def run(ids, *refs):
        sources = refs[:count]
        out_refs = refs[count + extra : count + extra + results]
        buffers = refs[count + extra + results : 2 * count + extra + results]
        sems = refs[2 * count + extra + results]
        copies = [
            pltpu.make_async_copy(source, buffer, sems.at[i])
            for i, (source, buffer) in enumerate(zip(sources, buffers))
        ]
        for copy in copies:
            copy.start()
        loads = Loads(copies, buffers)
        body(ids, loads, *out_refs, *refs[2 * count + extra + results + 1 :])
        loads.finish()

    moved = size_of(arrays) + size_of(outs)
    return pl.pallas_call(
        run,
        out_shape=tuple(outs),
        in_specs=[SMEM] + [ANY] * (count + extra),
        out_specs=tuple(pl.BlockSpec(memory_space=pltpu.VMEM) for _ in outs),
        scratch_shapes=[pltpu.VMEM(a.shape, a.dtype) for a in arrays]
        + [pltpu.SemaphoreType.DMA((count,))]
        + [pltpu.VMEM(a.shape, a.dtype) for a in scratch],
        compiler_params=pltpu.CompilerParams(vmem_limit_bytes=VMEM_LIMIT),
        cost_estimate=cost(flops, moved),
        name=name,
    )(ids, *arrays, *after)


def turn(value):
    return pltpu.roll(value, HD // 2, 1)


def head_forward(raw, gain, cosine, sine):
    scale = lax.rsqrt(jnp.mean(raw * raw, axis=-1, keepdims=True) + EPS)
    normed = raw * scale * gain
    return normed * cosine + turn(normed) * sine


def head_backward(grad, raw, gain, cosine, sine):
    scale = lax.rsqrt(jnp.mean(raw * raw, axis=-1, keepdims=True) + EPS)
    unit = raw * scale
    grad_normed = grad * cosine + turn(grad * sine)
    grad_gain = jnp.sum(grad_normed * unit, axis=0, keepdims=True)
    inner = grad_normed * gain
    grad_raw = scale * (inner - unit * jnp.mean(inner * unit, axis=-1, keepdims=True))
    return grad_raw, grad_gain


def key_value_body(count, ids, loads, normed_ref, kv, raw_ref, inverse_ref):
    pieces = loads[:count]
    rows, shard = pieces[0].shape
    squares = 0.0
    for piece in pieces:
        x = piece[...].astype(F32)
        squares += jnp.sum(x * x, axis=-1, keepdims=True)
    inverse = lax.rsqrt(squares * (1.0 / (shard * count)) + EPS)
    inverse_ref[...] = inverse
    gain, key_gain, cosine, sine, wk, wv = loads[count : count + 6]
    kv_width = wk.shape[1]
    key_raw = jnp.zeros((rows, kv_width), F32)
    values = jnp.zeros((rows, kv_width), F32)
    for s in range(count):
        off = pieces_of(s, ids[0], shard)
        normed = (pieces[s][...].astype(F32) * inverse * gain[:, pl.ds(off, shard)]).astype(BF)
        normed_ref[:, pl.ds(off, shard)] = normed
        key_raw += dot(normed, wk[pl.ds(off, shard), :])
        values += dot(normed, wv[pl.ds(off, shard), :])
    raw_ref[...] = key_raw
    for h in range(kv_width // HD):
        cols = slice(h * HD, (h + 1) * HD)
        out = head_forward(key_raw[:, cols], key_gain[...], cosine[...], sine[...])
        kv[:, cols] = out.astype(BF)
    kv[:, kv_width:] = values.astype(BF)


def query_body(ids, loads, q_ref, raw_ref):
    normed, wq, query_gain, cosine, sine = loads[:5]
    raw = dot(normed[...], wq[...])
    raw_ref[...] = raw
    for h in range(wq.shape[1] // HD):
        cols = slice(h * HD, (h + 1) * HD)
        out = head_forward(raw[:, cols], query_gain[...], cosine[...], sine[...])
        q_ref[:, cols] = out.astype(BF)


def head_probs(ids, q, blocks, head, group, row_segment, key_segments):
    rows = q.shape[0]
    kv = head // group
    cols = slice(head * HD, (head + 1) * HD)
    row_index = ids[1] * rows + lax.broadcasted_iota(jnp.int32, (rows, rows), 0)
    parts = []
    for s, block in enumerate(blocks):
        scores = dot_nt(q[:, cols], block[:, kv * HD : (kv + 1) * HD]) * HD ** (-0.5)
        key_index = (ids[1] ^ s) * rows + lax.broadcasted_iota(jnp.int32, (rows, rows), 1)
        allowed = (row_segment[...] == key_segments[s][...]) & (key_index <= row_index)
        parts.append(jnp.where(allowed, scores, NEG))
    top = parts[0].max(axis=-1, keepdims=True)
    for part in parts[1:]:
        top = jnp.maximum(top, part.max(axis=-1, keepdims=True))
    parts = [jnp.exp(part - top) for part in parts]
    total = sum(jnp.sum(part, axis=-1, keepdims=True) for part in parts)
    share = 1.0 / total
    return [part * share for part in parts]


def attention_body(count, group, blocks, ids, loads, mixed_ref, *outs):
    q, row_segment = loads[:2]
    kvs = loads[2 : 2 + blocks]
    key_segments = loads[2 + blocks : 2 + 2 * blocks]
    kv_width = kvs[0].shape[1] // 2
    for h in range(q.shape[1] // HD):
        probs = head_probs(ids, q, kvs, h, group, row_segment, key_segments)
        start = kv_width + (h // group) * HD
        mixed = sum(
            dot(p.astype(BF), block[:, start : start + HD]) for p, block in zip(probs, kvs)
        )
        mixed_ref[:, h * HD : (h + 1) * HD] = mixed.astype(BF)
    wo = loads[2 + 2 * blocks]
    shard = wo.shape[1] // count
    for s in range(count):
        off = pieces_of(s, ids[0], shard)
        outs[s][...] = dot(mixed_ref[...], wo[:, pl.ds(off, shard)]).astype(BF)


def second_norm_body(count, ids, loads, normed_ref, resid_ref, inverse_ref):
    pieces = loads[:count]
    gain = loads[count]
    rows, shard = pieces[0].shape
    squares = 0.0
    for piece in pieces:
        x = piece[...].astype(F32)
        squares += jnp.sum(x * x, axis=-1, keepdims=True)
    inverse = lax.rsqrt(squares * (1.0 / (shard * count)) + EPS)
    inverse_ref[...] = inverse
    for s in range(count):
        off = pieces_of(s, ids[0], shard)
        cols = pl.ds(off, shard)
        x = pieces[s][...]
        resid_ref[:, cols] = x
        normed_ref[:, cols] = (x.astype(F32) * inverse * gain[:, cols]).astype(BF)


def gated_terms(gate, up, grad_hidden):
    sigmoid = jax.nn.sigmoid(gate)
    silu = gate * sigmoid
    grad_gate = grad_hidden * up * sigmoid * (1.0 + gate * (1.0 - sigmoid))
    return silu * up, grad_gate, grad_hidden * silu


def feed_forward_body(tile, extra, ids, normed_hbm, cot_hbm, wg_hbm, wu_hbm, wd_hbm, *refs):
    refs = refs[extra:]
    grad_out, feed_out, normed, cot, wg, wu, wd, total, feed, sems = refs
    units = wg.shape[1]
    tiles = units // tile
    first = [
        pltpu.make_async_copy(normed_hbm, normed, sems.at[3 * tiles]),
        pltpu.make_async_copy(cot_hbm, cot, sems.at[3 * tiles + 1]),
    ]

    def weights(t):
        cols = pl.ds(pl.multiple_of(t * tile, tile), tile)
        return [
            pltpu.make_async_copy(wg_hbm.at[:, cols], wg.at[:, cols], sems.at[t]),
            pltpu.make_async_copy(wu_hbm.at[:, cols], wu.at[:, cols], sems.at[tiles + t]),
            pltpu.make_async_copy(wd_hbm.at[cols, :], wd.at[cols, :], sems.at[2 * tiles + t]),
        ]

    for copy in first:
        copy.start()
    for t in range(tiles):
        for copy in weights(t):
            copy.start()
    total[...] = jnp.zeros_like(total)
    feed[...] = jnp.zeros_like(feed)
    for copy in first:
        copy.wait()

    def step(t, carry):
        cols = pl.ds(pl.multiple_of(t * tile, tile), tile)
        gate_copy, up_copy, down_copy = weights(t)
        gate_copy.wait()
        gate = dot(normed[...], wg[:, cols])
        up_copy.wait()
        up = dot(normed[...], wu[:, cols])
        down_copy.wait()
        grad_hidden = dot_nt(cot[...], wd[cols, :])
        hidden, grad_gate, grad_up = gated_terms(gate, up, grad_hidden)
        total[...] += dot_nt(grad_gate.astype(BF), wg[:, cols]) + dot_nt(
            grad_up.astype(BF), wu[:, cols]
        )
        feed[...] += dot(hidden.astype(BF), wd[cols, :])
        return carry

    lax.fori_loop(0, tiles, step, 0)
    grad_out[...] = total[...].astype(BF)
    feed_out[...] = feed[...].astype(BF)


def feed_forward(ids, normed, cot, wg, wu, wd, after=()):
    rows, width = cot.shape
    units = wg.shape[1]
    tile = max(t for t in (512, 384, 256, 128) if units % t == 0)
    arrays = [normed, cot, wg, wu, wd]
    outs = [shape(rows, width)] * 2
    moved = size_of(arrays) + size_of(outs)
    return pl.pallas_call(
        functools.partial(feed_forward_body, tile, len(after)),
        out_shape=outs,
        in_specs=[SMEM] + [ANY] * (5 + len(after)),
        out_specs=[pl.BlockSpec(memory_space=pltpu.VMEM) for _ in outs],
        scratch_shapes=[pltpu.VMEM(a.shape, a.dtype) for a in arrays]
        + [
            pltpu.VMEM((rows, width), F32),
            pltpu.VMEM((rows, width), F32),
            pltpu.SemaphoreType.DMA((3 * (units // tile) + 2,)),
        ],
        compiler_params=pltpu.CompilerParams(
            vmem_limit_bytes=VMEM_LIMIT
        ),
        cost_estimate=cost(12 * rows * width * units, moved),
        name="feed_forward",
    )(ids, *arrays, *after)


def middle_body(count, group, blocks, ids, loads, own_ref, low_ref, sums_ref, *outs):
    grads, resid, inverse_ref, gain, cot = loads[:5]
    rows, width = grads.shape
    shard = width // count
    inverse = inverse_ref[...]
    row_total = 0.0
    for s in range(count):
        cols = pl.ds(pieces_of(s, ids[0], shard), shard)
        product = grads[:, cols].astype(F32) * (resid[:, cols].astype(F32) * inverse)
        sums_ref[:, cols] = jnp.sum(product, axis=0, keepdims=True)
        row_total += jnp.sum(product * gain[:, cols], axis=-1, keepdims=True)
    scale = row_total * inverse * (1.0 / width)
    wo = loads[5]
    mixed = jnp.zeros((rows, wo.shape[0]), F32)
    for s in range(count):
        cols = pl.ds(pieces_of(s, ids[0], shard), shard)
        unit = resid[:, cols].astype(F32) * inverse
        grad = (
            cot[:, cols].astype(F32)
            + inverse * (gain[:, cols] * grads[:, cols].astype(F32))
            - unit * scale
        )
        if s == 0:
            own_ref[...] = grad
        low = grad.astype(BF)
        low_ref[:, cols] = low
        mixed += dot_nt(low, wo[:, cols])
    attention_backward(group, blocks, ids, loads[6:], mixed.astype(BF), *outs)


def attention_backward(group, blocks, ids, loads, grads, low_ref, gain_ref, own_ref, *others):
    q, row_segment = loads[:2]
    kvs = loads[2 : 2 + blocks]
    key_segments = loads[2 + blocks : 2 + 2 * blocks]
    raw, query_gain, cosine, sine = loads[2 + 2 * blocks : 6 + 2 * blocks]
    kv_width = kvs[0].shape[1] // 2
    factor = HD ** (-0.5)
    gain_total = jnp.zeros((1, HD), F32)
    outs = [own_ref] + list(others)
    for kv in range(kv_width // HD):
        key_cols = slice(kv * HD, (kv + 1) * HD)
        value_cols = slice(kv_width + kv * HD, kv_width + (kv + 1) * HD)
        key_sums = [0.0] * blocks
        value_sums = [0.0] * blocks
        for h in range(kv * group, (kv + 1) * group):
            cols = slice(h * HD, (h + 1) * HD)
            probs = head_probs(ids, q, kvs, h, group, row_segment, key_segments)
            grad = grads[:, cols]
            grad_probs = [dot_nt(grad, block[:, value_cols]) for block in kvs]
            delta = sum(jnp.sum(p * g, axis=-1, keepdims=True) for p, g in zip(probs, grad_probs))
            scores = [(p * (g - delta)).astype(BF) for p, g in zip(probs, grad_probs)]
            grad_query = sum(dot(g, block[:, key_cols]) for g, block in zip(scores, kvs)) * factor
            for s in range(blocks):
                key_sums[s] += dot_tn(scores[s], q[:, cols])
                value_sums[s] += dot_tn(probs[s].astype(BF), grad)
            grad_raw, grad_gain = head_backward(
                grad_query, raw[:, cols], query_gain[...], cosine[...], sine[...]
            )
            low_ref[:, cols] = grad_raw.astype(BF)
            gain_total += grad_gain
        for s in range(blocks):
            outs[s][:, key_cols] = (key_sums[s] * factor).astype(outs[s].dtype)
            outs[s][:, value_cols] = value_sums[s].astype(outs[s].dtype)
    gain_ref[...] = gain_total


def key_backward_body(blocks, ids, loads, low_ref, gain_ref):
    sums = loads[:blocks]
    raw, key_gain, cosine, sine, query_low = loads[blocks : blocks + 5]
    q_width = query_low.shape[1]
    kv_width = raw.shape[1]
    low_ref[:, :q_width] = query_low[...]
    total = sums[0][...]
    for other in sums[1:]:
        total = total + other[...].astype(F32)
    gain_total = jnp.zeros((1, HD), F32)
    for h in range(kv_width // HD):
        cols = slice(h * HD, (h + 1) * HD)
        grad_raw, grad_gain = head_backward(
            total[:, cols], raw[:, cols], key_gain[...], cosine[...], sine[...]
        )
        low_ref[:, q_width + h * HD : q_width + (h + 1) * HD] = grad_raw.astype(BF)
        gain_total += grad_gain
    low_ref[:, q_width + kv_width :] = total[:, kv_width:].astype(BF)
    gain_ref[...] = gain_total


def first_grad_body(count, ids, loads, *outs):
    pieces = loads[:count]
    inverse_ref, gain, query_sums, key_sums, grads, wq, wk, wv = loads[count : count + 8]
    rows, shard = pieces[0].shape
    q_width, kv_width = wq.shape[1], wk.shape[1]
    inverse = inverse_ref[...]
    row_total = jnp.zeros((rows, 1), F32)
    for s in range(count):
        cols = pl.ds(pieces_of(s, ids[0], shard), shard)
        grad = (
            dot_nt(grads[:, :q_width], wq[cols, :])
            + dot_nt(grads[:, q_width : q_width + kv_width], wk[cols, :])
            + dot_nt(grads[:, q_width + kv_width :], wv[cols, :])
        )
        product = grad * (pieces[s][...].astype(F32) * inverse)
        outs[s][:rows, :] = grad.astype(BF)
        outs[s][rows:, :] = jnp.zeros((EXTRA, shard), BF)
        outs[s][rows : rows + 1, :] = jnp.sum(product, axis=0, keepdims=True).astype(BF)
        row_total += jnp.sum(product * gain[:, cols], axis=-1, keepdims=True)
    turned = jnp.broadcast_to(row_total, (rows, HD)).T[:1]
    small = jnp.concatenate([turned, query_sums[...], key_sums[...]], axis=1).astype(BF)
    for s in range(count):
        for r in range(small.shape[1] // shard):
            row = rows + 1 + r
            outs[s][row : row + 1, :] = small[:, r * shard : (r + 1) * shard]


def feed_weight_body(parts, extra, last, block, ids, *refs):
    rows_hbm, cots_hbm = refs[:parts], refs[parts : 2 * parts]
    wg_hbm, wu_hbm, wd_hbm = refs[2 * parts : 2 * parts + 3]
    refs = refs[2 * parts + 3 + extra :]
    dwg, dwu, dwd = refs[:3]
    lows = refs[3:6] if last else ()
    refs = refs[6:] if last else refs[3:]
    rows, cots, hid, gates, ups, wg, wu, wd, gate_out, up_out, down_out = refs[:11]
    refs = refs[11:]
    if last:
        gate_held, up_held, down_held, gate_cut, up_cut, down_cut = refs[:6]
        refs = refs[6:]
    row_sems, cot_sems, weight_sems, held_sems, out_sems = refs
    width = rows.shape[1]
    size = rows_hbm[0].shape[0]
    group = 2 if parts % 2 == 0 else 1
    chunk = group * size
    steps = wg_hbm.shape[1] // block // 2
    tile = width // 2

    def mine(b):
        return pl.ds(pl.multiple_of((ids[2] * steps + b) * block, block), block)

    def weights(b, slot):
        return [
            pltpu.make_async_copy(wg_hbm.at[:, mine(b)], wg.at[slot], weight_sems.at[slot, 0]),
            pltpu.make_async_copy(wu_hbm.at[:, mine(b)], wu.at[slot], weight_sems.at[slot, 1]),
            pltpu.make_async_copy(wd_hbm.at[mine(b), :], wd.at[slot], weight_sems.at[slot, 2]),
        ]

    def tile_at(t):
        return pl.ds(pl.multiple_of(t * tile, tile), tile)

    def held(b, t):
        at = tile_at(t)
        pairs = [
            (dwg.at[at, mine(b)], gate_held.at[at, :]),
            (dwu.at[at, mine(b)], up_held.at[at, :]),
            (dwd.at[mine(b), at], down_held.at[:, at]),
        ]
        return [pltpu.make_async_copy(a, c, held_sems.at[t, i]) for i, (a, c) in enumerate(pairs)]

    def results(b, t):
        at = tile_at(t)
        low = pl.ds(pl.multiple_of(b * block, block), block)
        pairs = [
            (gate_out.at[at, :], dwg.at[at, mine(b)]),
            (up_out.at[at, :], dwu.at[at, mine(b)]),
            (down_out.at[:, at], dwd.at[mine(b), at]),
        ]
        if last:
            pairs += [
                (gate_cut.at[at, :], lows[0].at[at, low]),
                (up_cut.at[at, :], lows[1].at[at, low]),
                (down_cut.at[:, at], lows[2].at[low, at]),
            ]
        return [pltpu.make_async_copy(a, c, out_sems.at[t, i]) for i, (a, c) in enumerate(pairs)]

    for copy in weights(0, 0):
        copy.start()
    for i in range(parts):
        place = pl.ds(i * size, size)
        pltpu.make_async_copy(rows_hbm[i], rows.at[place, :], row_sems.at[i // group]).start()
        pltpu.make_async_copy(cots_hbm[i], cots.at[place, :], cot_sems.at[i // group]).start()

    def one_block(b, carry):
        slot = lax.rem(b, 2)
        for copy in weights(b, slot):
            copy.wait()
        if last:
            for t in range(2):
                for copy in held(b, t):
                    copy.start()

        @pl.when(b + 1 < steps)
        def _():
            for copy in weights(b + 1, 1 - slot):
                copy.start()

        def recompute(c, carry):
            place = pl.ds(pl.multiple_of(c * chunk, chunk), chunk)

            @pl.when(b == 0)
            def _():
                pltpu.make_async_copy(rows.at[place, :], rows.at[place, :], row_sems.at[c]).wait()
                pltpu.make_async_copy(cots.at[place, :], cots.at[place, :], cot_sems.at[c]).wait()

            own = rows[place, :]
            gate = dot(own, wg[slot])
            up = dot(own, wu[slot])
            grad_hidden = dot_nt(cots[place, :], wd[slot])
            hidden, grad_gate, grad_up = gated_terms(gate, up, grad_hidden)
            hid[place, :] = hidden.astype(BF)
            gates[place, :] = grad_gate.astype(BF)
            ups[place, :] = grad_up.astype(BF)
            return carry

        lax.fori_loop(0, parts // group, recompute, 0)

        def products(t, carry):
            @pl.when(b > 0)
            def _():
                for copy in results(b, t):
                    copy.wait()

            cols = tile_at(t)
            down = dot_tn(hid[...], cots[:, cols])
            gate = dot_tn(rows[:, cols], gates[...])
            up = dot_tn(rows[:, cols], ups[...])
            if last:
                for copy in held(b, t):
                    copy.wait()
                down = (down + down_held[:, cols]).astype(BF)
                gate = (gate + gate_held[cols, :]).astype(BF)
                up = (up + up_held[cols, :]).astype(BF)
                down_cut[:, cols] = down
                gate_cut[cols, :] = gate
                up_cut[cols, :] = up
            down_out[:, cols] = down.astype(F32)
            gate_out[cols, :] = gate.astype(F32)
            up_out[cols, :] = up.astype(F32)
            for copy in results(b, t):
                copy.start()
            return carry

        lax.fori_loop(0, 2, products, 0)
        return carry

    lax.fori_loop(0, steps, one_block, 0)
    for t in range(2):
        for copy in results(0, t):
            copy.wait()


def feed_weights(ids, rows, cots, wg, wu, wd, block, held, last, after=()):
    parts = len(rows)
    size, width = rows[0].shape
    tokens = size * parts
    units = wg.shape[1]
    held = list(held or ())
    outs = [
        shape(width, units, dtype=F32),
        shape(width, units, dtype=F32),
        shape(units, width, dtype=F32),
    ]
    tiles = [
        shape(width, block, dtype=F32),
        shape(width, block, dtype=F32),
        shape(block, width, dtype=F32),
    ]
    scratch = [
        shape(tokens, width),
        shape(tokens, width),
        shape(tokens, block),
        shape(tokens, block),
        shape(tokens, block),
        shape(2, width, block),
        shape(2, width, block),
        shape(2, block, width),
        *tiles,
    ]
    if last:
        outs += [shape(width, units // 2), shape(width, units // 2), shape(units // 2, width)]
        scratch += [*tiles, shape(width, block), shape(width, block), shape(block, width)]
    if not held and last:
        held = [jnp.zeros(o.shape, F32) for o in outs[:3]]
    extra = len(held) + len(after)
    return pl.pallas_call(
        functools.partial(feed_weight_body, parts, extra, last, block),
        out_shape=outs,
        in_specs=[SMEM] + [ANY] * (2 * parts + 3 + extra),
        out_specs=[ANY] * len(outs),
        scratch_shapes=[pltpu.VMEM(a.shape, a.dtype) for a in scratch]
        + [
            pltpu.SemaphoreType.DMA((parts,)),
            pltpu.SemaphoreType.DMA((parts,)),
            pltpu.SemaphoreType.DMA((2, 3)),
            pltpu.SemaphoreType.DMA((2, 3)),
            pltpu.SemaphoreType.DMA((2, 6)),
        ],
        input_output_aliases={4 + 2 * parts + i: i for i in range(len(held))},
        compiler_params=pltpu.CompilerParams(vmem_limit_bytes=VMEM_LIMIT),
        cost_estimate=cost(6 * tokens * width * units, 4 * tokens * width),
        name="feed_weights",
    )(ids, *rows, *cots, wg, wu, wd, *held, *after)


def assemble_body(extra, ids, gate_low, up_low, down_low, *refs):
    dwg, dwu, dwd = refs[-3:]
    dwg[...] = gate_low[...].astype(F32)
    dwu[...] = up_low[...].astype(F32)
    dwd[...] = down_low[...].astype(F32)


def assemble(ids, lows, block, held, after=()):
    width, units = held[0].shape
    steps = units // block // 2
    tile = width // 2
    cols_in = pl.BlockSpec((tile, block), lambda b, i, ids: (i, b))
    rows_in = pl.BlockSpec((block, tile), lambda b, i, ids: (b, i))
    cols_out = pl.BlockSpec((tile, block), lambda b, i, ids: (i, (1 - ids[2]) * steps + b))
    rows_out = pl.BlockSpec((block, tile), lambda b, i, ids: ((1 - ids[2]) * steps + b, i))
    return pl.pallas_call(
        functools.partial(assemble_body, len(after)),
        out_shape=[shape(*a.shape, dtype=F32) for a in held],
        grid_spec=pltpu.PrefetchScalarGridSpec(
            num_scalar_prefetch=1,
            grid=(steps, 2),
            in_specs=[cols_in, cols_in, rows_in] + [ANY] * (3 + len(after)),
            out_specs=[cols_out, cols_out, rows_out],
        ),
        input_output_aliases={4: 0, 5: 1, 6: 2},
        compiler_params=pltpu.CompilerParams(vmem_limit_bytes=VMEM_LIMIT),
        cost_estimate=cost(0, 9 * width * units),
        name="assemble",
    )(ids, *lows, *held, *after)


def projection_body(parts, tile, extra, ids, *refs):
    rows_hbm, grads_hbm = refs[:parts], refs[parts : 2 * parts]
    refs = refs[2 * parts + extra :]
    outs_hbm = refs[:3]
    rows, grads, *outs, row_sems, grad_sem, out_sems = refs[3:]
    width = rows.shape[1]
    tiles = width // tile
    at = 0
    for i in range(parts):
        place = pl.ds(at, grads_hbm[i].shape[0])
        pltpu.make_async_copy(grads_hbm[i], grads.at[place, :], grad_sem).start()
        at += grads_hbm[i].shape[0]
    for t in range(tiles):
        cols = pl.ds(t * tile, tile)
        at = 0
        for i in range(parts):
            place = pl.ds(at, rows_hbm[i].shape[0])
            pltpu.make_async_copy(
                rows_hbm[i].at[:, cols], rows.at[place, cols], row_sems.at[t]
            ).start()
            at += rows_hbm[i].shape[0]
    pltpu.make_async_copy(grads, grads, grad_sem).wait()
    q_width, kv_width = outs[0].shape[1], outs[1].shape[1]

    def copies(t):
        cols = pl.ds(pl.multiple_of(t * tile, tile), tile)
        return [
            pltpu.make_async_copy(a.at[cols, :], b.at[cols, :], out_sems.at[t, i])
            for i, (a, b) in enumerate(zip(outs, outs_hbm))
        ]

    def products(t, carry):
        cols = pl.ds(pl.multiple_of(t * tile, tile), tile)
        pltpu.make_async_copy(rows.at[:, cols], rows.at[:, cols], row_sems.at[t]).wait()
        total = dot_tn(rows[:, cols], grads[...])
        outs[0][cols, :] = total[:, :q_width]
        outs[1][cols, :] = total[:, q_width : q_width + kv_width]
        outs[2][cols, :] = total[:, q_width + kv_width :]
        for copy in copies(t):
            copy.start()
        return carry

    lax.fori_loop(0, tiles, products, 0)

    def finish(t, carry):
        for copy in copies(t):
            copy.wait()
        return carry

    lax.fori_loop(0, tiles, finish, 0)


def projection_weights(ids, rows, grads, q_width, kv_width, after):
    parts = len(rows)
    width = rows[0].shape[1]
    tokens = sum(a.shape[0] for a in rows)
    tile = 512
    outs = [shape(width, w, dtype=F32) for w in (q_width, kv_width, kv_width)]
    scratch = [shape(tokens, width), shape(tokens, q_width + 2 * kv_width)] + outs
    return pl.pallas_call(
        functools.partial(projection_body, parts, tile, len(after)),
        out_shape=outs,
        in_specs=[SMEM] + [ANY] * (2 * parts + len(after)),
        out_specs=[ANY] * 3,
        scratch_shapes=[pltpu.VMEM(a.shape, a.dtype) for a in scratch]
        + [
            pltpu.SemaphoreType.DMA((width // tile,)),
            pltpu.SemaphoreType.DMA(()),
            pltpu.SemaphoreType.DMA((width // tile, 3)),
        ],
        compiler_params=pltpu.CompilerParams(
            vmem_limit_bytes=VMEM_LIMIT
        ),
        cost_estimate=cost(2 * tokens * width * (q_width + 2 * kv_width), 2 * tokens * width),
        name="projection_weights",
    )(ids, *rows, *grads, *after)


def matmul_tn(left, right):
    return lax.dot_general(left, right, (((0,), (0,)), ((), ())), preferred_element_type=F32)


def rope_tables(position_row):
    half = HD // 2
    freqs = jnp.exp(-(2.0 * jnp.arange(half, dtype=F32) / HD) * jnp.log(F32(THETA)))
    angles = position_row.astype(F32)[:, None] * freqs[None, :]
    cosine, sine = jnp.cos(angles), jnp.sin(angles)
    return jnp.concatenate([cosine, cosine], axis=1), jnp.concatenate([-sine, sine], axis=1)


def per_device(
    inputs,
    cotangent,
    segments,
    positions,
    attention_gain,
    query_weight,
    key_weight,
    value_weight,
    query_gain,
    key_gain,
    output_weight,
    feed_gain,
    gate_weight,
    up_weight,
    down_weight,
):
    count, shard = inputs.shape
    width = cotangent.shape[1]
    tensor = lax.axis_size("tensor")
    me = lax.axis_index("tensor")
    column = me * shard
    place = lax.axis_index("ctx")
    core = lax.axis_index("dp") % 2
    ids = jnp.stack([me, place, core, lax.axis_index("dp")]).astype(jnp.int32)
    q_width, kv_width = query_weight.shape[1], key_weight.shape[1]
    group = q_width // kv_width
    blocks = lax.axis_size("ctx")
    gain_one = attention_gain.astype(F32)[None]
    gain_two = feed_gain.astype(F32)[None]
    gain_q = query_gain.astype(F32)[None]
    gain_k = key_gain.astype(F32)[None]
    gain_one_part = lax.dynamic_slice_in_dim(gain_one, column, shard, 1)
    hidden_units = gate_weight.shape[1]
    block = 256 if (hidden_units // 2) % 256 == 0 else 128

    masks = far_masks()
    first_masks = len(masks) // 2 or 1
    x_pieces = gather_pieces(inputs, "tensor")
    cot_parts = [send_plane(cotangent, mask) for mask in masks[:first_masks + 1]]
    cosine, sine = rope_tables(positions[0])
    segment_row = segments[0]
    row_segment = lax.dynamic_slice_in_dim(segment_row, place * count, count)[:, None]
    key_segments = [
        lax.dynamic_slice_in_dim(segment_row, (place ^ s) * count, count)[None]
        for s in range(blocks)
    ]
    normed_one, kv_rows, key_raw, inverse_one = kernel_call(
        functools.partial(key_value_body, tensor),
        ids,
        [*x_pieces, gain_one, gain_k, cosine, sine, key_weight, value_weight],
        [
            shape(count, width),
            shape(count, 2 * kv_width),
            shape(count, kv_width, dtype=F32),
            shape(count, 1, dtype=F32),
        ],
        4 * count * width * kv_width,
        "key_value",
        after=[*cot_parts[1:], row_segment, *key_segments],
    )
    kv_pieces = gather_pieces(kv_rows, "ctx")
    all_normed_one = plane_all(normed_one)
    query_rows, query_raw = kernel_call(
        query_body,
        ids,
        [normed_one, query_weight, gain_q, cosine, sine],
        [shape(count, q_width), shape(count, q_width, dtype=F32)],
        2 * count * width * q_width,
        "query",
    )

    mixed_rows, *branch_pieces = kernel_call(
        functools.partial(attention_body, tensor, group, blocks),
        ids,
        [query_rows, row_segment, *kv_pieces, *key_segments, output_weight],
        [shape(count, q_width)] + [shape(count, shard)] * tensor,
        4 * count * count * blocks * q_width + 2 * count * width * q_width,
        "attention",
    )
    branch = second_half(first_half(branch_pieces, "tensor"), "tensor")
    resid_part = (inputs.astype(F32) + branch).astype(BF)
    resid_pieces = gather_pieces(resid_part, "tensor")
    cot_partners = partners(cot_parts[: first_masks + 1])

    normed_two, resid, inverse_two = kernel_call(
        functools.partial(second_norm_body, tensor),
        ids,
        [*resid_pieces, gain_two],
        [shape(count, width), shape(count, width), shape(count, 1, dtype=F32)],
        8 * count * width,
        "second_norm",
        after=cot_partners,
    )
    two_parts = [send_plane(normed_two, mask) for mask in masks[: first_masks + 1]]
    grad_two_part, feed_part = feed_forward(
        ids, normed_two, cotangent, gate_weight, up_weight, down_weight
    )
    feed_done = feed_part
    grad_two_part = sum_tensor(grad_two_part)
    two_parts = pass_on(two_parts, masks, True, feed_done)
    cot_parts = pass_on(cot_parts, masks, False, feed_done)
    groups = [slice(0, first_masks), slice(first_masks, None)] if len(masks) > 1 else [slice(0, None)]
    last = len(groups) - 1
    two_partners = partners(two_parts[:1]) + partners(two_parts[1 : first_masks + 1], feed_done)

    def weights_of(g, held, after):
        return feed_weights(
            ids,
            two_parts[groups[g]] + two_partners[groups[g]],
            cot_parts[groups[g]] + cot_partners[groups[g]],
            gate_weight,
            up_weight,
            down_weight,
            block,
            held,
            g == last,
            after,
        )

    held, done = None, [feed_done, *two_partners, all_normed_one]
    for g in range(last):
        held = weights_of(g, held, done)
        done = held[:1]
    two_partners += partners(two_parts[first_masks + 1 :], *done)
    cot_partners += partners(cot_parts[first_masks + 1 :], *done)
    grad_two = lax.all_gather(grad_two_part, "tensor", axis=1, tiled=True)
    *held, gate_low, up_low, down_low = weights_of(last, held, [grad_two_part])
    lows = [gate_low, up_low, down_low]
    feed = sum_tensor(order_after(feed_part, gate_low))
    lows = [swap(low, "dp", 1) for low in lows] if has_pair() else lows

    (
        grad_resid_part,
        grad_resid_low,
        feed_sums,
        grad_query_low,
        grad_query_gain,
        grad_kv,
        *grad_kv_sent,
    ) = kernel_call(
        functools.partial(middle_body, tensor, group, blocks),
        ids,
        [
            grad_two,
            resid,
            inverse_two,
            gain_two,
            cotangent,
            output_weight,
            query_rows,
            row_segment,
            *kv_pieces,
            *key_segments,
            query_raw,
            gain_q,
            cosine,
            sine,
        ],
        [
            shape(count, shard, dtype=F32),
            shape(count, width),
            shape(1, width, dtype=F32),
            shape(count, q_width),
            shape(1, HD, dtype=F32),
            shape(count, 2 * kv_width, dtype=F32),
        ]
        + [shape(count, 2 * kv_width)] * (blocks - 1),
        2 * count * width * q_width,
        "middle",
        after=[gate_low],
    )
    kv_sums = [grad_kv] + [
        lax.ppermute(sent, "ctx", [(i, i ^ (s + 1)) for i in range(blocks)])
        for s, sent in enumerate(grad_kv_sent)
    ]
    output_part = matmul_tn(mixed_rows, grad_resid_low).astype(BF)
    if has_pair():
        half = q_width // 2
        keep = lax.dynamic_slice_in_dim(output_part, core * half, half, 0)
        send = lax.dynamic_slice_in_dim(output_part, (1 - core) * half, half, 0)
        output_part = (keep.astype(F32) + swap(send, "dp", 1).astype(F32)).astype(BF)
    half = output_part.shape[0] // 2
    output_parts = [output_part[:half], output_part[half:]]
    bits = [mask for mask in masks if mask and mask & (mask - 1) == 0]

    def summed(parts, bit_of, earlier=(), later=()):
        received = [
            send_plane(order_after(part, *earlier), bit) for part, bit in zip(parts, bit_of)
        ]
        return [
            (part.astype(F32) + order_after(other, *later).astype(F32)).astype(BF)
            for part, other in zip(parts, received)
        ]

    grad_low, grad_key_gain = kernel_call(
        functools.partial(key_backward_body, len(kv_sums)),
        ids,
        [*kv_sums, key_raw, gain_k, cosine, sine, grad_query_low],
        [shape(count, q_width + 2 * kv_width), shape(1, HD, dtype=F32)],
        40 * count * kv_width,
        "key_backward",
        after=output_parts,
    )
    all_grad_low = plane_all(grad_low)
    first_parts = output_parts

    grad_one_pieces = kernel_call(
        functools.partial(first_grad_body, tensor),
        ids,
        [
            *x_pieces,
            inverse_one,
            gain_one,
            grad_query_gain,
            grad_key_gain,
            grad_low,
            query_weight,
            key_weight,
            value_weight,
        ],
        [shape(count + EXTRA, shard)] * tensor,
        2 * count * width * (q_width + 2 * kv_width),
        "first_grad",
    )
    grad_gate_w, grad_up_w, grad_down_w = assemble(ids, lows, block, held, grad_one_pieces[:1])
    outputs = (resid_part.astype(F32) + order_after(feed, grad_gate_w).astype(F32)).astype(BF)

    grad_one = first_half(grad_one_pieces, "tensor", grad_gate_w)
    grad_query_w, grad_key_w, grad_value_w = projection_weights(
        ids, [all_normed_one], [all_grad_low], q_width, kv_width, [grad_gate_w, *grad_one.values()]
    )

    grad_one = second_half(grad_one, "tensor", [grad_query_w])
    grad_one_part = grad_one[:count]
    small = grad_one[count + 1 : count + 1 + (count + 2 * HD) // shard].reshape(-1)
    row_total_one = small[:count, None]
    feed_part_sums = lax.dynamic_slice_in_dim(feed_sums[0], column, shard)
    small = jnp.concatenate([grad_one[count], feed_part_sums, small[count:]])
    unit_one_part = inputs.astype(F32) * inverse_one
    grad_inputs = (
        grad_resid_part
        + inverse_one * (gain_one_part * grad_one_part)
        - unit_one_part * (inverse_one / width) * row_total_one
    )

    output_parts = summed(first_parts, (bits[0], bits[-1]), (), [grad_gate_w])
    for i in range(1, len(bits)):
        output_parts = summed(output_parts, (bits[i], bits[-1 - i]), [grad_gate_w], [grad_query_w])
    if has_pair():
        small = small + swap(small, "dp", 1)
    for bit in bits:
        small = small + send_plane(small, bit)
    grad_attention_gain = small[:shard]
    grad_feed_gain = small[shard : 2 * shard]
    grad_query_gain = small[2 * shard : 2 * shard + HD]
    grad_key_gain = small[2 * shard + HD :]
    if has_pair():
        others = [swap(part, "dp", 1) for part in output_parts]
        grad_output_w = jnp.where(
            core == 0,
            jnp.concatenate(output_parts + others, axis=0),
            jnp.concatenate(others + output_parts, axis=0),
        )
    else:
        grad_output_w = jnp.concatenate(output_parts, axis=0)
    grad_output_w = grad_output_w.astype(F32)

    return (
        outputs,
        grad_inputs,
        grad_attention_gain,
        grad_query_w,
        grad_key_w,
        grad_value_w,
        grad_query_gain,
        grad_key_gain,
        grad_output_w,
        grad_feed_gain,
        grad_gate_w,
        grad_up_w,
        grad_down_w,
    )


def solution(mesh):
    in_specs = (
        P(("dp", "ctx"), "tensor"),
        P(("dp", "ctx"), None),
        P("dp", None),
        P("dp", "ctx"),
        P(),
        P(None, "tensor"),
        P(None, "tensor"),
        P(None, "tensor"),
        P(),
        P(),
        P("tensor", None),
        P(),
        P(None, "tensor"),
        P(None, "tensor"),
        P("tensor", None),
    )
    out_specs = (
        P(("dp", "ctx"), "tensor"),
        P(("dp", "ctx"), "tensor"),
        P("tensor"),
        P(None, "tensor"),
        P(None, "tensor"),
        P(None, "tensor"),
        P(),
        P(),
        P("tensor", None),
        P("tensor"),
        P(None, "tensor"),
        P(None, "tensor"),
        P("tensor", None),
    )
    return jax.shard_map(
        per_device, mesh=mesh, in_specs=in_specs, out_specs=out_specs, check_vma=False
    )
```
